32 devices in a mesh: tile: 8 (over z, y), band: 4 (over x, core).
Axes of the slice: x: 2, y: 2, z: 4, core: 2. Of those that a mesh axis runs over, the one named last changes fastest.
Arguments:
- calib: bfloat16 [16, 8, 64, 8192], P('tile', None, None, 'band'), may hold values from -0.09375 to 0.09375
- support: int32 [16, 8], P('tile'), may hold values from 0 to 15, as said below
- band_window: int32 [16, 8, 2], P('tile'), may hold values from 0 to 128, as said below
- measured: float32 [1024], P('tile'), may hold values from -60 to 60
Outputs:
- solution: float32 [16, 8192], P('tile', 'band')
- residual: float32 [1024], P('tile')
The draws below stay inside these ranges and needn't reach their ends.
Inputs may be any that keep to these rules, and one draw needn't show every extreme that they name: `support`: entries 0 to 3 of each tile name blocks within 4 of the tile's own number along the cyclic order; the other entries name blocks whose index of tile (block // 2) lies 3 to 8 - 3 steps ahead of the tile's own, cyclically, and the tiles of one index of tile name at most 3 such blocks of any one other index. `band_window`: each window holds at least a quarter of the 128 bands; the first band is at most half of 128.
All inputs are finite; a program needn't handle non-finite values.
Results may differ from the reference program's by a relative error of at most 0.012.
The reference program's roundings to bfloat16 on the way count: a program that leaves them out, or rounds other values in their place, can miss the bound.
Values may be sent and summed in bfloat16 or wider, within the bound.
A program may use at most 64 MiB of HBM per device.

```python
import jax
import jax.numpy as jnp
from jax import lax

PIX = 64
BANDS = 128
K = 8
TILE_DEV = 2
ITERS = 2
TILES = 16
BLOCKS = 16
SENSOR = 1024


def draw_support(key, part):
    key_near, key_pick, key_perm = jax.random.split(key, 3)
    devices = TILES // TILE_DEV
    half = K // 2
    far_count = K - half
    spread = devices - 5
    anchor = jnp.arange(TILES, dtype=jnp.int32)[:, None]
    offset = jax.random.randint(key_near, (TILES, half), -2 * TILE_DEV, 2 * TILE_DEV + 1)
    offset = offset.at[0, 0].set(-1)
    offset = offset.at[1, 0].set(-1)
    near = (anchor + offset) % BLOCKS
    orders = jax.vmap(lambda sub: jax.random.permutation(sub, spread))(jax.random.split(key_perm, devices)).astype(jnp.int32)
    device = anchor // TILE_DEV
    position = anchor % TILE_DEV * far_count + jnp.arange(far_count, dtype=jnp.int32)[None, :]
    ahead = 3 + orders[device, position % spread]
    owner = (device + ahead) % devices
    far = owner * TILE_DEV + jax.random.randint(key_pick, (TILES, far_count), 0, TILE_DEV)
    return jnp.concatenate([near, far], axis=1).astype(jnp.int32)


def draw_band_window(key, part):
    key_start, key_len = jax.random.split(key)
    start = jax.random.randint(key_start, (TILES, K), 0, BANDS // 2)
    length = jax.random.randint(key_len, (TILES, K), BANDS // 4, BANDS // 2 + 1)
    window = jnp.stack([start, start + length], axis=2).astype(jnp.int32)
    window = window.at[0, 0, 0].set(BANDS // 2)
    window = window.at[0, 0, 1].set(BANDS)
    window = window.at[1, 0, 0].set(0)
    return window


def draw_measured(key, part):
    key_base, key_rough = jax.random.split(key)
    place = jnp.arange(SENSOR, dtype=jnp.float32) / SENSOR
    rough = jnp.exp(jnp.log(3.0) * jax.random.uniform(key_rough, (SENSOR // PIX, 1), dtype=jnp.float32))
    rough = jnp.broadcast_to(rough, (SENSOR // PIX, PIX)).reshape(SENSOR)
    base = jnp.clip(jax.random.normal(key_base, (SENSOR,), dtype=jnp.float32), -6.0, 6.0)
    rise = jnp.exp(jnp.log(3.0) * place)
    return (base * rise * rough).astype(jnp.float32)


def block_levels(own_key, shape, shards, smallest, high):
    loudness = 1.0
    for axis_at, shards_of in shards:
        draws = jax.random.uniform(jax.random.fold_in(jax.random.fold_in(own_key, 6), axis_at), (shards_of,), jnp.float32, smallest / len(shards), high / len(shards))
        loudness = loudness * jnp.repeat(jnp.exp(draws), shape[axis_at] // shards_of).reshape((-1,) + (1,) * (len(shape) - 1 - axis_at))
    return loudness


def scatter_about(stream_key, dims, scale, limit, cuts=(), held_as=jnp.bfloat16):
    drawn = jax.random.normal(stream_key, dims, jnp.float32) * scale
    if len(cuts) > 0:
        drawn = block_levels(stream_key, dims, cuts, -0.22, 0.18) * drawn
    return jnp.clip(drawn, min=-limit, max=limit).astype(held_as)


def setup_inputs(seed: int = 0) -> dict:
    seeds = jax.random.split(jax.random.key(seed), 5)
    return {
        "calib": scatter_about(seeds[0], (TILES, K, PIX, BANDS * PIX), (PIX * BANDS // 2) ** -0.5, 0.09375, ((0, 8), (3, 4))),
        "support": draw_support(jax.random.fold_in(seeds[4], 71), 0),
        "band_window": draw_band_window(jax.random.fold_in(seeds[4], 71), 0),
        "measured": draw_measured(jax.random.fold_in(seeds[4], 71), 0),
    }


ridge_weight = 0.25


def reference(calib, support, band_window, measured):
    width = BANDS * PIX
    bands = jnp.arange(width, dtype=jnp.int32) // PIX
    inside = (bands[None, None, :] >= band_window[:, :, 0:1]) & (bands[None, None, :] < band_window[:, :, 1:2])

    def forward(direction):
        blocks_b = lax.optimization_barrier(direction.astype(jnp.bfloat16)).astype(jnp.float32)

        def one_tile(args):
            rows, ids, mask = args
            picked = jnp.where(mask, blocks_b[ids], jnp.zeros((), jnp.float32))
            return jnp.einsum("kij,kj->i", rows.astype(jnp.float32), picked, precision=lax.Precision.HIGHEST)

        return lax.map(one_tile, (calib, support, inside)).reshape(-1)

    def adjoint(sensor):
        rows_b = lax.optimization_barrier(sensor.astype(jnp.bfloat16)).astype(jnp.float32).reshape(TILES, PIX)

        def one_tile(args):
            rows, vec, mask = args
            terms = jnp.einsum("kij,i->kj", rows.astype(jnp.float32), vec, precision=lax.Precision.HIGHEST)
            return jnp.where(mask, terms, jnp.zeros((), jnp.float32))

        terms = lax.map(one_tile, (calib, rows_b, inside))
        return jax.ops.segment_sum(terms.reshape(TILES * K, width), support.reshape(-1), num_segments=BLOCKS)

    residual = measured
    gradient = adjoint(measured)
    direction = gradient
    solution = jnp.zeros_like(gradient)
    gamma = jnp.sum(gradient * gradient)
    for step in range(ITERS):
        image = forward(direction)
        delta = jnp.sum(image * image) + ridge_weight * jnp.sum(direction * direction)
        alpha = gamma / delta
        solution = solution + alpha * direction
        residual = residual - alpha * image
        if step + 1 < ITERS:
            gradient = adjoint(residual) - ridge_weight * solution
            gamma_next = jnp.sum(gradient * gradient)
            direction = gradient + (gamma_next / gamma) * direction
            gamma = gamma_next
    return solution, residual
```

```python
import functools

import jax
import jax.numpy as jnp
from jax import lax
from jax.experimental import pallas as pl
from jax.experimental.pallas import tpu as pltpu
from jax.sharding import PartitionSpec as P

BANDS_PER_GROUP_PIX = 64
RIDGE = 0.25
LANES = 128
VMEM_BYTES = 24 << 20
MESH = pl.DeviceIdType.MESH


def far_first(n):
    return sorted(range(n), key=lambda h: (-bin(h).count("1"), -h))


def pieces_of(n_tile, n_block, width):
    col_groups = min(n_tile, width // LANES)
    row_groups = n_tile // col_groups
    return col_groups, row_groups, n_block // row_groups, width // col_groups


def kernel(
    n_tile,
    n_band,
    calib,
    support_in,
    window_in,
    measured_in,
    solved_out,
    residual_out,
    support,
    window,
    measured,
    held,
    turned,
    stage,
    landed,
    packed,
    passed,
    grad_buf,
    norm_buf,
    own_buf,
    all_buf,
    small_sem,
    load_sem,
    rs_send,
    rs_recv,
    ag_send,
    ag_pass,
    ag_recv,
    all_send,
    all_recv,
):
    tile_rows, k, pix, width = calib.shape
    entries = tile_rows * k
    rows = entries * pix
    n_block = n_tile * tile_rows
    col_groups, row_groups, piece_rows, piece_cols = pieces_of(n_tile, n_block, width)
    me = lax.axis_index("tile")
    band = lax.axis_index("band")
    odd = band % 2
    f32, bf16 = jnp.float32, jnp.bfloat16

    small = [
        pltpu.make_async_copy(source, target, small_sem.at[i])
        for i, (source, target) in enumerate(
            ((support_in, support), (window_in, window), (measured_in, measured))
        )
    ]
    for copy in small:
        copy.start()
    loads = []
    for e in range(entries):
        copy = pltpu.make_async_copy(
            calib.at[e // k, e % k], held.at[pl.ds(e * pix, pix), :], load_sem.at[e]
        )
        copy.start()
        loads.append(copy)

    def paired(index, n):
        turns = [(1 << b) * (1 - 2 * (index // (1 << b) % 2)) for b in range(n.bit_length() - 1)]
        return [
            sum([turn for b, turn in enumerate(turns) if h >> b & 1], index) for h in range(n)
        ]

    peers, others = paired(me, n_tile), paired(band, n_band)
    tile_order = far_first(n_tile)
    everyone = sorted(
        [(a, b) for a in range(n_tile) for b in range(n_band) if a or b],
        key=lambda s: -bin(s[0] * n_band + s[1]).count("1"),
    )
    barrier = pltpu.get_barrier_semaphore()
    for a, b in everyone:
        pl.semaphore_signal(
            barrier,
            inc=1,
            device_id={"tile": peers[a], "band": others[b]},
            device_id_type=MESH,
        )

    for copy in small:
        copy.wait()
    lane_entry = lax.broadcasted_iota(jnp.int32, (1, rows), 1) // pix
    sup_row = jnp.zeros((1, rows), jnp.int32)
    for e in range(entries):
        sup_row = jnp.where(lane_entry == e, support[e // k, e % k], sup_row)
    names = jnp.broadcast_to(sup_row, (n_block, rows)) == lax.broadcasted_iota(
        jnp.int32, (n_block, rows), 0
    )

    lane = lax.broadcasted_iota(jnp.int32, (1, LANES), 1)
    low = lane < pix
    first_half = lane < LANES // 2

    def spread(w):
        pieces = []
        for t in range(tile_rows):
            col = t * pix // LANES * LANES
            tilev = w[:, col : col + LANES]
            rolled = pltpu.roll(tilev, pix, 1)
            both = jnp.where(low, tilev, rolled) if t * pix % LANES == 0 else jnp.where(low, rolled, tilev)
            pieces += [both] * (k * pix // LANES)
        return jnp.concatenate(pieces, axis=1)

    def left_side(w):
        wide = jnp.broadcast_to(spread(w), (n_block, rows))
        return jnp.where(names, wide, jnp.zeros((), f32)).astype(bf16)

    def scatter_copy(it, slab, h):
        return pltpu.make_async_remote_copy(
            src_ref=stage.at[it, peers[h]],
            dst_ref=landed.at[it, slab, h],
            send_sem=rs_send.at[it, h],
            recv_sem=rs_recv.at[it, slab, h],
            device_id={"tile": peers[h], "band": band + 1 - odd},
            device_id_type=MESH,
        )

    def gather_copy(it, slab, h):
        return pltpu.make_async_remote_copy(
            src_ref=packed.at[it, me] if slab else passed.at[it],
            dst_ref=packed.at[it, me],
            send_sem=(ag_send if slab else ag_pass).at[it, h],
            recv_sem=ag_recv.at[it, h],
            device_id={"tile": peers[h], "band": band if slab else band - 1},
            device_id_type=MESH,
        )

    def all_copy(it, a, b):
        return pltpu.make_async_remote_copy(
            src_ref=all_buf.at[it, 0, 0],
            dst_ref=all_buf.at[it, b, a],
            send_sem=all_send.at[it, a, b],
            recv_sem=all_recv.at[it, a, b],
            device_id={"tile": peers[a], "band": others[b]},
            device_id_type=MESH,
        )

    def scatter_send(it, product):
        for p in range(n_tile):
            r, c = p // col_groups * piece_rows, p % col_groups * piece_cols
            stage[it, p] = product[r : r + piece_rows, c : c + piece_cols].astype(bf16)
        for h in tile_order[:-1]:
            scatter_copy(it, odd, h).start()

        @pl.when(odd == 0)
        def _():
            scatter_copy(it, 0, 0).start()

    def lanes_sum(x):
        x = jnp.sum(x, axis=0, keepdims=True)
        total = x[:, 0:LANES]
        for c in range(1, piece_cols // LANES):
            total = total + x[:, c * LANES : (c + 1) * LANES]
        return total

    def reduce_gather(it, finish):
        norm_buf[it] = jnp.zeros((2, LANES), f32)

        @pl.when(odd == 1)
        def _():
            for slab in range(2):
                total = jnp.zeros((piece_rows, piece_cols), f32)
                if slab:
                    total = stage[it, me].astype(f32)
                for h in reversed(tile_order):
                    if h or not slab:
                        scatter_copy(it, slab, h).wait_recv()
                        total = total + landed[it, slab, h].astype(f32)
                total, sums = finish(slab, total)
                if slab:
                    packed[it, me] = total.astype(bf16)
                else:
                    passed[it] = total.astype(bf16)
                for h in tile_order:
                    if h or not slab:
                        gather_copy(it, slab, h).start()
                grad_buf[it, slab] = total
                norm_buf[it] = norm_buf[it] + sums

    def gathered(it):
        return jnp.concatenate(
            [
                jnp.concatenate(
                    [packed[it, r * col_groups + c] for c in range(col_groups)], axis=1
                )
                for r in range(row_groups)
            ],
            axis=0,
        )

    def forward(it):
        @pl.when(odd == 0)
        def _():
            gather_copy(it, 1, 0).wait_recv()

        for h in reversed(tile_order[:-1]):
            gather_copy(it, 1, h).wait_recv()
        direction = gathered(it)
        out = jnp.dot(direction, turned[...], preferred_element_type=f32)
        out = jnp.sum(jnp.where(names, out, jnp.zeros((), f32)), axis=0, keepdims=True)
        cols = []
        per = k * pix // LANES
        for t in range(tile_rows):
            acc = out[:, t * per * LANES : t * per * LANES + LANES]
            for c in range(1, per):
                at = (t * per + c) * LANES
                acc = acc + out[:, at : at + LANES]
            cols.append(acc + pltpu.roll(acc, pix, 1))
        image = jnp.concatenate(
            [jnp.where(low, cols[t], cols[t + 1]) for t in range(0, tile_rows, 2)], axis=1
        )
        halves = [
            x + pltpu.roll(x, LANES // 2, 1) for x in (norm_buf[it, 0:1, :], norm_buf[it, 1:2, :])
        ]
        all_buf[it, 0, 0, 0:1, :] = image
        all_buf[it, 0, 0, 1:2, :] = jnp.where(first_half, halves[0], halves[1])
        for a, b in everyone:
            all_copy(it, a, b).start()
        own = (lax.broadcasted_iota(jnp.int32, (8, n_block), 1) - me * tile_rows) == (
            lax.broadcasted_iota(jnp.int32, (8, n_block), 0)
        )
        own = jnp.where(own, 1.0, 0.0).astype(bf16)
        own_buf[it] = jnp.dot(own, direction, preferred_element_type=f32)
        for a, b in reversed(everyone):
            all_copy(it, a, b).wait_recv()
        total = all_buf[it, 0]
        for b in range(1, n_band):
            total = total + all_buf[it, b]
        sums = jnp.sum(total, axis=0)[1:2, :]
        zero = jnp.zeros_like(sums)
        return (
            total,
            total[0, 0:1, :],
            jnp.sum(jnp.where(first_half, sums, zero), axis=1, keepdims=True),
            jnp.sum(jnp.where(first_half, zero, sums), axis=1, keepdims=True),
        )

    def image_square(total):
        square = jnp.sum(total * total, axis=0)[0:1, :]
        return jnp.sum(square, axis=1, keepdims=True)

    def sent(it):
        for h in tile_order[:-1]:
            scatter_copy(it, odd, h).wait_send()

        @pl.when(odd == 0)
        def _():
            scatter_copy(it, 0, 0).wait_send()

        @pl.when(odd == 1)
        def _():
            for h in tile_order:
                gather_copy(it, 0, h).wait_send()
            for h in tile_order[:-1]:
                gather_copy(it, 1, h).wait_send()

    def all_sent(it):
        for a, b in everyone:
            all_copy(it, a, b).wait_send()

    start = measured[...]
    left = left_side(start)
    bands = band * (width // BANDS_PER_GROUP_PIX) + (
        lax.broadcasted_iota(jnp.int32, (1, width), 1) // BANDS_PER_GROUP_PIX
    )
    for e in range(entries):
        t, j = e // k, e % k
        loads[e].wait()
        at = pl.ds(e * pix, pix)
        inside = jnp.where(
            (bands >= window[t, 0, j]) & (bands < window[t, 1, j]), 1.0, 0.0
        ).astype(bf16)
        held[at, :] = held[at, :] * inside
    product = jnp.dot(left, held[...], preferred_element_type=f32)
    pl.semaphore_wait(barrier, n_tile * n_band - 1)
    scatter_send(0, product)
    for c in range(0, width, 256):
        turned[c : c + 256, :] = held[:, c : c + 256].T

    def first(slab, total):
        norm = lanes_sum(total * total)
        return total, jnp.concatenate([norm, norm], axis=0)

    reduce_gather(0, first)
    images, image, gamma, _ = forward(0)
    alpha = gamma / (image_square(images) + RIDGE * gamma)
    residual = start - alpha * image

    scatter_send(1, jnp.dot(left_side(residual), held[...], preferred_element_type=f32))

    def second(slab, total):
        direction = grad_buf[0, slab]
        gradient = total - RIDGE * (alpha * direction)
        return gradient, jnp.concatenate(
            [lanes_sum(gradient * gradient), lanes_sum(gradient * direction)], axis=0
        )

    sent(0)
    all_sent(0)
    reduce_gather(1, second)
    partials, partial, gamma_next, cross = forward(1)
    beta = gamma_next / gamma
    image = partial + beta * image
    images = partials + beta * images
    square = gamma_next + 2.0 * beta * cross + beta * beta * gamma
    step = gamma_next / (image_square(images) + RIDGE * square)
    solved_out[...] = (alpha + step * beta) * own_buf[0, 0:tile_rows, :] + step * own_buf[1, 0:tile_rows, :]
    residual_out[...] = residual - step * image
    sent(1)
    all_sent(1)


def finish_kernel(solved, residual, solution_out, residual_out):
    solution_out[...] = solved[...]
    residual_out[...] = residual[...]


def body(calib, support, band_window, measured):
    n_tile, n_band = lax.axis_size("tile"), lax.axis_size("band")
    tile_rows, k, pix, width = calib.shape
    entries = tile_rows * k
    sensor = tile_rows * pix
    n_block = n_tile * tile_rows
    _, _, piece_rows, piece_cols = pieces_of(n_tile, n_block, width)
    f32, bf16 = jnp.float32, jnp.bfloat16
    vmem = pl.BlockSpec(memory_space=pltpu.VMEM)
    dma = pltpu.SemaphoreType.DMA
    piece = (piece_rows, piece_cols)
    hbm = pl.BlockSpec(memory_space=pl.ANY)
    in_hbm = lambda x: pltpu.with_memory_space_constraint(x, pltpu.HBM)
    in_vmem = lambda x: pltpu.with_memory_space_constraint(x, pltpu.VMEM)
    turned_window = jnp.transpose(band_window, (0, 2, 1))
    held_back = pl.pallas_call(
        functools.partial(kernel, n_tile, n_band),
        out_shape=(pltpu.VMEM((tile_rows, width), f32), pltpu.VMEM((1, sensor), f32)),
        in_specs=[hbm] * 4,
        out_specs=(vmem,) * 2,
        scratch_shapes=[
            pltpu.SMEM((tile_rows, k), jnp.int32),
            pltpu.SMEM((tile_rows, 2, k), jnp.int32),
            pltpu.VMEM((1, sensor), f32),
            pltpu.VMEM((entries * pix, width), bf16),
            pltpu.VMEM((width, entries * pix), bf16),
            pltpu.VMEM((2, n_tile) + piece, bf16),
            pltpu.VMEM((2, 2, n_tile) + piece, bf16),
            pltpu.VMEM((2, n_tile) + piece, bf16),
            pltpu.VMEM((2,) + piece, bf16),
            pltpu.VMEM((2, 2) + piece, f32),
            pltpu.VMEM((2, 2, LANES), f32),
            pltpu.VMEM((2, 8, width), f32),
            pltpu.VMEM((2, n_band, n_tile, 2, sensor), f32),
            dma((3,)),
            dma((entries,)),
            dma((2, n_tile)),
            dma((2, 2, n_tile)),
            dma((2, n_tile)),
            dma((2, n_tile)),
            dma((2, n_tile)),
            dma((2, n_tile, n_band)),
            dma((2, n_tile, n_band)),
        ],
        compiler_params=pltpu.CompilerParams(
            collective_id=0, has_side_effects=True, vmem_limit_bytes=VMEM_BYTES
        ),
    )(in_hbm(calib), in_hbm(support), in_hbm(turned_window), in_hbm(measured.reshape(1, sensor)))
    solved, residual = pl.pallas_call(
        finish_kernel,
        out_shape=(
            jax.ShapeDtypeStruct((tile_rows, width), f32),
            jax.ShapeDtypeStruct((1, sensor), f32),
        ),
        in_specs=[vmem] * 2,
        out_specs=(vmem, vmem),
        compiler_params=pltpu.CompilerParams(vmem_limit_bytes=VMEM_BYTES),
    )(*[in_vmem(x) for x in held_back])
    return solved, residual.reshape(sensor)


def solution(mesh):
    placed = (P("tile", None, None, "band"), P("tile", None), P("tile", None, None), P("tile"))
    return jax.shard_map(
        body, mesh=mesh, in_specs=placed, out_specs=(P("tile", "band"), P("tile")), check_vma=False
    )
```

```python
import functools

import jax
import jax.numpy as jnp
from jax import lax
from jax.experimental import pallas as pl
from jax.experimental.pallas import tpu as pltpu
from jax.sharding import PartitionSpec as P

BANDS_PER_GROUP_PIX = 64
RIDGE = 0.25
LANES = 128
PACKED_ROWS = 16
ENTRIES_AT_ONCE = 4
VMEM_BYTES = 24 << 20
MESH = pl.DeviceIdType.MESH


def centre_of(n_tile):
    summing = n_tile // 2 if n_tile % 4 == 0 else n_tile
    return (n_tile - summing) // 2, summing


def far_first(n_tile):
    first, _ = centre_of(n_tile)

    def hops(h):
        there = first ^ h
        return abs(there // 2 - first // 2) + (there ^ first) % 2

    return sorted(range(n_tile), key=lambda h: (-hops(h), -h))


def pieces_of(n_tile, n_block, width):
    summing = centre_of(n_tile)[1]
    col_groups = min(summing, width // LANES)
    row_groups = summing // col_groups
    return col_groups, row_groups, n_block // row_groups, width // col_groups


def kernel(
    n_tile,
    n_band,
    calib,
    support_in,
    window_in,
    measured_in,
    solved_out,
    residual_out,
    support,
    window,
    measured,
    held,
    turned,
    stage,
    landed,
    packed,
    passed,
    grad_buf,
    norm_buf,
    own_buf,
    mask_buf,
    all_mine,
    all_in,
    small_sem,
    load_sem,
    rs_send,
    rs_recv,
    ag_send,
    ag_pass,
    ag_recv,
    all_send,
    all_recv,
):
    tile_rows, k, pix, width = calib.shape
    entries = tile_rows * k
    rows = entries * pix
    n_block = n_tile * tile_rows
    col_groups, row_groups, piece_rows, piece_cols = pieces_of(n_tile, n_block, width)
    me = lax.axis_index("tile")
    band = lax.axis_index("band")
    odd = band % 2
    first, summing = centre_of(n_tile)
    mine = me - first
    sums_here = (odd == 1) & (mine >= 0) & (mine < summing)
    f32, bf16 = jnp.float32, jnp.bfloat16

    small = [
        pltpu.make_async_copy(source, target, small_sem.at[i])
        for i, (source, target) in enumerate(
            ((support_in, support), (window_in, window), (measured_in, measured))
        )
    ]
    for copy in small:
        copy.start()
    loads = []
    for e in range(entries):
        copy = pltpu.make_async_copy(
            calib.at[e // k, e % k], held.at[pl.ds(e * pix, pix), :], load_sem.at[e]
        )
        copy.start()
        loads.append(copy)

    def paired(index, n):
        turns = [(1 << b) * (1 - 2 * (index // (1 << b) % 2)) for b in range(n.bit_length() - 1)]
        return [
            sum([turn for b, turn in enumerate(turns) if h >> b & 1], index) for h in range(n)
        ]

    peers, others = paired(me, n_tile), paired(band, n_band)
    tile_order = far_first(n_tile)
    everyone = sorted(
        [(a, b) for a in range(n_tile) for b in range(n_band) if a or b],
        key=lambda s: -bin(s[0] * n_band + s[1]).count("1"),
    )
    barrier = pltpu.get_barrier_semaphore()
    for a, b in everyone:
        pl.semaphore_signal(
            barrier,
            inc=1,
            device_id={"tile": peers[a], "band": others[b]},
            device_id_type=MESH,
        )

    for copy in small:
        copy.wait()
    lane_entry = lax.broadcasted_iota(jnp.int32, (1, rows), 1) // pix
    sup_row = jnp.zeros((1, rows), jnp.int32)
    for e in range(entries):
        sup_row = jnp.where(lane_entry == e, support[e // k, e % k], sup_row)
    names = jnp.broadcast_to(sup_row, (n_block, rows)) == lax.broadcasted_iota(
        jnp.int32, (n_block, rows), 0
    )

    lane = lax.broadcasted_iota(jnp.int32, (1, LANES), 1)
    low = lane < pix
    first_half = lane < LANES // 2

    def spread(w):
        pieces = []
        for t in range(tile_rows):
            col = t * pix // LANES * LANES
            tilev = w[:, col : col + LANES]
            rolled = pltpu.roll(tilev, pix, 1)
            both = jnp.where(low, tilev, rolled) if t * pix % LANES == 0 else jnp.where(low, rolled, tilev)
            pieces += [both] * (k * pix // LANES)
        return jnp.concatenate(pieces, axis=1)

    def left_side(w):
        wide = jnp.broadcast_to(spread(w), (n_block, rows))
        return jnp.where(names, wide, jnp.zeros((), f32)).astype(bf16)

    side = me // (n_tile // 2)
    ahead = [(1 - side) * (summing - 1 - j) + side * j for j in range(summing)]

    def scatter_copy(it, j):
        return pltpu.make_async_remote_copy(
            src_ref=stage.at[it, ahead[j]],
            dst_ref=landed.at[it, odd, me],
            send_sem=rs_send.at[it, j],
            recv_sem=rs_recv.at[it, odd, me],
            device_id={"tile": first + ahead[j], "band": band + 1 - odd},
            device_id_type=MESH,
        )

    def landing(it, slab, tile):
        return pltpu.make_async_remote_copy(
            src_ref=stage.at[it, 0],
            dst_ref=landed.at[it, slab, tile],
            send_sem=rs_send.at[it, 0],
            recv_sem=rs_recv.at[it, slab, tile],
            device_id={"tile": tile, "band": band - 1},
            device_id_type=MESH,
        )

    def gather_copy(it, slab, h):
        return pltpu.make_async_remote_copy(
            src_ref=packed.at[it, mine] if slab else passed.at[it],
            dst_ref=packed.at[it, mine],
            send_sem=(ag_send if slab else ag_pass).at[it, h],
            recv_sem=ag_recv.at[it, mine],
            device_id={"tile": peers[h], "band": band if slab else band - 1},
            device_id_type=MESH,
        )

    def arriving(it, piece):
        return pltpu.make_async_remote_copy(
            src_ref=packed.at[it, piece],
            dst_ref=packed.at[it, piece],
            send_sem=ag_send.at[it, 0],
            recv_sem=ag_recv.at[it, piece],
            device_id={"tile": first + piece, "band": band + 1 - odd},
            device_id_type=MESH,
        )

    def all_copy(it, a, b):
        return pltpu.make_async_remote_copy(
            src_ref=all_mine.at[it],
            dst_ref=all_in.at[it, a * n_band + b - 1],
            send_sem=all_send.at[it],
            recv_sem=all_recv.at[it],
            device_id={"tile": peers[a], "band": others[b]},
            device_id_type=MESH,
        )

    def all_whole(it):
        return pltpu.make_async_remote_copy(
            src_ref=all_in.at[it],
            dst_ref=all_in.at[it],
            send_sem=all_send.at[it],
            recv_sem=all_recv.at[it],
            device_id={"tile": peers[1], "band": band},
            device_id_type=MESH,
        )

    def scatter_send(it, product):
        for p in range(summing):
            r, c = p // col_groups * piece_rows, p % col_groups * piece_cols
            stage[it, p] = product[r : r + piece_rows, c : c + piece_cols].astype(bf16)
        for j in range(summing):

            @pl.when((odd == 0) | (ahead[j] != mine))
            def _():
                scatter_copy(it, j).start()

    def lanes_sum(x):
        x = jnp.sum(x, axis=0, keepdims=True)
        total = x[:, 0:LANES]
        for c in range(1, piece_cols // LANES):
            total = total + x[:, c * LANES : (c + 1) * LANES]
        return total

    def reduce_gather(it, finish):
        norm_buf[it] = jnp.zeros((2, LANES), f32)

        @pl.when(sums_here)
        def _():
            for slab in range(2):
                total = stage[it, mine].astype(f32) if slab else jnp.zeros((piece_rows, piece_cols), f32)
                for h in reversed(tile_order):
                    if h or not slab:
                        landing(it, slab, peers[h]).wait_recv()
                        total = total + landed[it, slab, peers[h]].astype(f32)
                total, sums = finish(slab, total)
                if slab:
                    packed[it, mine] = total.astype(bf16)
                else:
                    passed[it] = total.astype(bf16)
                for h in tile_order:
                    if h or not slab:
                        gather_copy(it, slab, h).start()
                grad_buf[it, slab] = total
                norm_buf[it] = norm_buf[it] + sums

    def gathered(it):
        return jnp.concatenate(
            [
                jnp.concatenate(
                    [packed[it, r * col_groups + c] for c in range(col_groups)], axis=1
                )
                for r in range(row_groups)
            ],
            axis=0,
        )

    def forward(it):
        out = jnp.zeros((n_block, rows), f32)
        for j in reversed(range(summing)):

            @pl.when((odd == 0) | (ahead[j] != mine))
            def _():
                arriving(it, ahead[j]).wait_recv()

            if row_groups == 1:
                out = out + jnp.dot(
                    packed[it, ahead[j]], turned[ahead[j]], preferred_element_type=f32
                )
        if row_groups > 1:
            for c in range(col_groups):
                column = [packed[it, r * col_groups + c] for r in range(row_groups)]
                out = out + jnp.dot(
                    jnp.concatenate(column, axis=0), turned[c], preferred_element_type=f32
                )
        out = jnp.sum(jnp.where(names, out, jnp.zeros((), f32)), axis=0, keepdims=True)
        cols = []
        per = k * pix // LANES
        for t in range(tile_rows):
            acc = out[:, t * per * LANES : t * per * LANES + LANES]
            for c in range(1, per):
                at = (t * per + c) * LANES
                acc = acc + out[:, at : at + LANES]
            cols.append(acc + pltpu.roll(acc, pix, 1))
        image = jnp.concatenate(
            [jnp.where(low, cols[t], cols[t + 1]) for t in range(0, tile_rows, 2)], axis=1
        )
        halves = [
            x + pltpu.roll(x, LANES // 2, 1) for x in (norm_buf[it, 0:1, :], norm_buf[it, 1:2, :])
        ]
        all_mine[it, 0:1, :] = image
        all_mine[it, 1:2, :] = jnp.where(first_half, halves[0], halves[1])
        for a, b in everyone:
            all_copy(it, a, b).start()
        own = (lax.broadcasted_iota(jnp.int32, (8, n_block), 1) - me * tile_rows) == (
            lax.broadcasted_iota(jnp.int32, (8, n_block), 0)
        )
        own = jnp.where(own, 1.0, 0.0).astype(bf16)
        own_buf[it] = jnp.dot(own, gathered(it), preferred_element_type=f32)
        sent(it)
        all_whole(it).wait_recv()
        totals = []
        for a in range(n_tile):
            total = all_in[it, a * n_band - 1] if a else all_mine[it]
            for b in range(1, n_band):
                total = total + all_in[it, a * n_band + b - 1]
            totals.append(total)
        sums = totals[0]
        for total in totals[1:]:
            sums = sums + total
        sums = sums[1:2, :]
        zero = jnp.zeros_like(sums)
        return (
            jnp.stack(totals),
            totals[0][0:1, :],
            jnp.sum(jnp.where(first_half, sums, zero), axis=1, keepdims=True),
            jnp.sum(jnp.where(first_half, zero, sums), axis=1, keepdims=True),
        )

    def image_square(total):
        square = jnp.sum(total * total, axis=0)[0:1, :]
        return jnp.sum(square, axis=1, keepdims=True)

    def sent(it):
        for j in range(summing):

            @pl.when((odd == 0) | (ahead[j] != mine))
            def _():
                scatter_copy(it, j).wait_send()

        @pl.when(sums_here)
        def _():
            for h in tile_order:
                gather_copy(it, 0, h).wait_send()
                if h:
                    gather_copy(it, 1, h).wait_send()

    start = measured[...]
    left = left_side(start)
    bands = band * (width // BANDS_PER_GROUP_PIX) + (
        lax.broadcasted_iota(jnp.int32, (PACKED_ROWS, width), 1) // BANDS_PER_GROUP_PIX
    )
    for e in range(entries):
        t, j = e // k, e % k
        inside = (bands >= window[t, 0, j]) & (bands < window[t, 1, j])
        mask_buf[e] = jnp.where(inside, 1.0, 0.0).astype(bf16)
    product = jnp.zeros((n_block, width), f32)
    for e in range(entries):
        loads[e].wait()
        inside = mask_buf[e]
        for at in range(e * pix, (e + 1) * pix, PACKED_ROWS):
            held[at : at + PACKED_ROWS, :] = held[at : at + PACKED_ROWS, :] * inside
        if (e + 1) % ENTRIES_AT_ONCE == 0:
            upto = (e + 1) * pix
            part = slice(upto - ENTRIES_AT_ONCE * pix, upto)
            product = product + jnp.dot(left[:, part], held[part, :], preferred_element_type=f32)
    pl.semaphore_wait(barrier, n_tile * n_band - 1)
    scatter_send(0, product)
    for c in range(col_groups):
        turned[c] = held[:, c * piece_cols : (c + 1) * piece_cols].T

    def start_sums(slab, total):
        norm = lanes_sum(total * total)
        return total, jnp.concatenate([norm, norm], axis=0)

    reduce_gather(0, start_sums)
    images, image, gamma, _ = forward(0)
    alpha = gamma / (image_square(images) + RIDGE * gamma)
    residual = start - alpha * image

    scatter_send(1, jnp.dot(left_side(residual), held[...], preferred_element_type=f32))

    def second(slab, total):
        direction = grad_buf[0, slab]
        gradient = total - RIDGE * (alpha * direction)
        return gradient, jnp.concatenate(
            [lanes_sum(gradient * gradient), lanes_sum(gradient * direction)], axis=0
        )

    all_whole(0).wait_send()
    reduce_gather(1, second)
    partials, partial, gamma_next, cross = forward(1)
    beta = gamma_next / gamma
    image = partial + beta * image
    images = partials + beta * images
    square = gamma_next + 2.0 * beta * cross + beta * beta * gamma
    step = gamma_next / (image_square(images) + RIDGE * square)
    solved_out[...] = (alpha + step * beta) * own_buf[0, 0:tile_rows, :] + step * own_buf[1, 0:tile_rows, :]
    residual_out[...] = residual - step * image
    all_whole(1).wait_send()


def finish_kernel(solved, residual, solution_out, residual_out):
    solution_out[...] = solved[...]
    residual_out[...] = residual[...]


def body(calib, support, band_window, measured):
    n_tile, n_band = lax.axis_size("tile"), lax.axis_size("band")
    tile_rows, k, pix, width = calib.shape
    entries = tile_rows * k
    sensor = tile_rows * pix
    n_block = n_tile * tile_rows
    _, _, piece_rows, piece_cols = pieces_of(n_tile, n_block, width)
    summing = centre_of(n_tile)[1]
    f32, bf16 = jnp.float32, jnp.bfloat16
    vmem = pl.BlockSpec(memory_space=pltpu.VMEM)
    dma = pltpu.SemaphoreType.DMA
    piece = (piece_rows, piece_cols)
    hbm = pl.BlockSpec(memory_space=pl.ANY)
    in_hbm = lambda x: pltpu.with_memory_space_constraint(x, pltpu.HBM)
    in_vmem = lambda x: pltpu.with_memory_space_constraint(x, pltpu.VMEM)
    turned_window = jnp.transpose(band_window, (0, 2, 1))
    held_back = pl.pallas_call(
        functools.partial(kernel, n_tile, n_band),
        out_shape=(pltpu.VMEM((tile_rows, width), f32), pltpu.VMEM((1, sensor), f32)),
        in_specs=[hbm] * 4,
        out_specs=(vmem,) * 2,
        scratch_shapes=[
            pltpu.SMEM((tile_rows, k), jnp.int32),
            pltpu.SMEM((tile_rows, 2, k), jnp.int32),
            pltpu.VMEM((1, sensor), f32),
            pltpu.VMEM((entries * pix, width), bf16),
            pltpu.VMEM((width // piece_cols, piece_cols, entries * pix), bf16),
            pltpu.VMEM((2, summing) + piece, bf16),
            pltpu.VMEM((2, 2, n_tile) + piece, bf16),
            pltpu.VMEM((2, summing) + piece, bf16),
            pltpu.VMEM((2,) + piece, bf16),
            pltpu.VMEM((2, 2) + piece, f32),
            pltpu.VMEM((2, 2, LANES), f32),
            pltpu.VMEM((2, 8, width), f32),
            pltpu.VMEM((entries, PACKED_ROWS, width), bf16),
            pltpu.VMEM((2, 2, sensor), f32),
            pltpu.VMEM((2, n_band * n_tile - 1, 2, sensor), f32),
            dma((3,)),
            dma((entries,)),
            dma((2, summing)),
            dma((2, 2, n_tile)),
            dma((2, n_tile)),
            dma((2, n_tile)),
            dma((2, summing)),
            dma((2,)),
            dma((2,)),
        ],
        compiler_params=pltpu.CompilerParams(
            collective_id=0, has_side_effects=True, vmem_limit_bytes=VMEM_BYTES
        ),
    )(in_hbm(calib), in_hbm(support), in_hbm(turned_window), in_hbm(measured.reshape(1, sensor)))
    solved, residual = pl.pallas_call(
        finish_kernel,
        out_shape=(
            jax.ShapeDtypeStruct((tile_rows, width), f32),
            jax.ShapeDtypeStruct((1, sensor), f32),
        ),
        in_specs=[vmem] * 2,
        out_specs=(vmem, vmem),
        compiler_params=pltpu.CompilerParams(vmem_limit_bytes=VMEM_BYTES),
    )(*[in_vmem(x) for x in held_back])
    return solved, residual.reshape(sensor)


def solution(mesh):
    placed = (P("tile", None, None, "band"), P("tile", None), P("tile", None, None), P("tile"))
    return jax.shard_map(
        body, mesh=mesh, in_specs=placed, out_specs=(P("tile", "band"), P("tile")), check_vma=False
    )
```

```python
import functools

import jax
import jax.numpy as jnp
from jax import lax
from jax.experimental import pallas as pl
from jax.experimental.pallas import tpu as pltpu
from jax.sharding import PartitionSpec as P

BANDS_PER_GROUP_PIX = 64
RIDGE = 0.25
LANES = 128
PACKED_ROWS = 16
ENTRIES_AT_ONCE = 4
VMEM_BYTES = 48 << 20
MESH = pl.DeviceIdType.MESH


def centre_of(n_tile):
    summing = n_tile // 2 if n_tile % 4 == 0 else n_tile
    return (n_tile - summing) // 2, summing


def far_first(n_tile):
    first, _ = centre_of(n_tile)

    def hops(h):
        there = first ^ h
        return abs(there // 2 - first // 2) + (there ^ first) % 2

    return sorted(range(n_tile), key=lambda h: (-hops(h), -h))


def pieces_of(n_tile, n_block, width):
    summing = centre_of(n_tile)[1]
    col_groups = min(summing, width // LANES)
    row_groups = summing // col_groups
    return col_groups, row_groups, n_block // row_groups, width // col_groups


def kernel(
    n_tile,
    n_band,
    calib,
    support_in,
    window_in,
    measured_in,
    solved_out,
    residual_out,
    support,
    window,
    measured,
    held,
    turned,
    stage,
    landed,
    packed,
    passed,
    grad_buf,
    base_buf,
    norm_buf,
    own_buf,
    mask_buf,
    band_mine,
    band_in,
    all_mine,
    all_in,
    small_sem,
    load_sem,
    rs_send,
    rs_recv,
    ag_send,
    ag_pass,
    ag_recv,
    band_send,
    band_recv,
    all_send,
    all_recv,
):
    tile_rows, k, pix, width = calib.shape
    entries = tile_rows * k
    rows = entries * pix
    n_block = n_tile * tile_rows
    col_groups, row_groups, piece_rows, piece_cols = pieces_of(n_tile, n_block, width)
    me = lax.axis_index("tile")
    band = lax.axis_index("band")
    odd = band % 2
    first, summing = centre_of(n_tile)
    mine = me - first
    sums_here = (odd == 1) & (mine >= 0) & (mine < summing)
    f32, bf16 = jnp.float32, jnp.bfloat16

    small = [
        pltpu.make_async_copy(source, target, small_sem.at[i])
        for i, (source, target) in enumerate(
            ((support_in, support), (window_in, window), (measured_in, measured))
        )
    ]
    for copy in small:
        copy.start()
    loads = []
    for e in range(entries):
        copy = pltpu.make_async_copy(
            calib.at[e // k, e % k], held.at[pl.ds(e * pix, pix), :], load_sem.at[e]
        )
        copy.start()
        loads.append(copy)

    def paired(index, n):
        turns = [(1 << b) * (1 - 2 * (index // (1 << b) % 2)) for b in range(n.bit_length() - 1)]
        return [
            sum([turn for b, turn in enumerate(turns) if h >> b & 1], index) for h in range(n)
        ]

    peers, others = paired(me, n_tile), paired(band, n_band)
    tile_order = far_first(n_tile)
    everyone = sorted(
        [(a, b) for a in range(n_tile) for b in range(n_band) if a or b],
        key=lambda s: -bin(s[0] * n_band + s[1]).count("1"),
    )
    barrier = pltpu.get_barrier_semaphore()
    for a, b in everyone:
        pl.semaphore_signal(
            barrier,
            inc=1,
            device_id={"tile": peers[a], "band": others[b]},
            device_id_type=MESH,
        )

    for copy in small:
        copy.wait()
    lane_entry = lax.broadcasted_iota(jnp.int32, (1, rows), 1) // pix
    sup_row = jnp.zeros((1, rows), jnp.int32)
    for e in range(entries):
        sup_row = jnp.where(lane_entry == e, support[e // k, e % k], sup_row)
    names = jnp.broadcast_to(sup_row, (n_block, rows)) == lax.broadcasted_iota(
        jnp.int32, (n_block, rows), 0
    )

    lane = lax.broadcasted_iota(jnp.int32, (1, LANES), 1)
    low = lane < pix

    def spread(w):
        pieces = []
        for t in range(tile_rows):
            col = t * pix // LANES * LANES
            tilev = w[:, col : col + LANES]
            rolled = pltpu.roll(tilev, pix, 1)
            both = jnp.where(low, tilev, rolled) if t * pix % LANES == 0 else jnp.where(low, rolled, tilev)
            pieces += [both] * (k * pix // LANES)
        return jnp.concatenate(pieces, axis=1)

    def rounded(x):
        return x.astype(bf16).astype(f32)

    def left_side(w):
        wide = jnp.broadcast_to(spread(w), (n_block, rows))
        return jnp.where(names, wide, jnp.zeros((), f32)).astype(bf16)

    def both_parts(w):
        high = rounded(w)
        return jnp.concatenate([left_side(high), left_side(w - high)], axis=0)

    def three_parts(x):
        high = rounded(x)
        middle = rounded(x - high)
        row = lax.broadcasted_iota(jnp.int32, (piece_rows, LANES), 0)
        rest = jnp.where(row == 2, x - high - middle, jnp.zeros((), f32))
        return jnp.where(row == 0, high, jnp.where(row == 1, middle, rest)).astype(bf16)

    def row_of(parts):
        return jnp.sum(parts.astype(f32), axis=0, keepdims=True)

    def lane_total(x):
        return jnp.sum(x, axis=1, keepdims=True)

    side = me // (n_tile // 2)
    ahead = [(1 - side) * (summing - 1 - j) + side * j for j in range(summing)]

    lanes = piece_cols // LANES
    parts_of = [lanes, lanes + 1, lanes]

    def scatter_copy(it, j):
        some = pl.ds(0, parts_of[it])
        return pltpu.make_async_remote_copy(
            src_ref=stage.at[it, ahead[j], some],
            dst_ref=landed.at[it, odd, me, some],
            send_sem=rs_send.at[it, j],
            recv_sem=rs_recv.at[it, odd, me],
            device_id={"tile": first + ahead[j], "band": band + 1 - odd},
            device_id_type=MESH,
        )

    def landing(it, slab, tile):
        some = pl.ds(0, parts_of[it])
        return pltpu.make_async_remote_copy(
            src_ref=stage.at[it, 0, some],
            dst_ref=landed.at[it, slab, tile, some],
            send_sem=rs_send.at[it, 0],
            recv_sem=rs_recv.at[it, slab, tile],
            device_id={"tile": tile, "band": band - 1},
            device_id_type=MESH,
        )

    def gather_copy(it, slab, h):
        return pltpu.make_async_remote_copy(
            src_ref=packed.at[it, mine] if slab else passed.at[it],
            dst_ref=packed.at[it, mine],
            send_sem=(ag_send if slab else ag_pass).at[it, h],
            recv_sem=ag_recv.at[it, mine],
            device_id={"tile": peers[h], "band": band if slab else band - 1},
            device_id_type=MESH,
        )

    def arriving(it, piece):
        return pltpu.make_async_remote_copy(
            src_ref=packed.at[it, piece],
            dst_ref=packed.at[it, piece],
            send_sem=ag_send.at[it, 0],
            recv_sem=ag_recv.at[it, piece],
            device_id={"tile": first + piece, "band": band + 1 - odd},
            device_id_type=MESH,
        )

    def band_copy(b):
        return pltpu.make_async_remote_copy(
            src_ref=band_mine,
            dst_ref=band_in.at[b - 1],
            send_sem=band_send,
            recv_sem=band_recv,
            device_id={"tile": me, "band": others[b]},
            device_id_type=MESH,
        )

    def all_copy(a, b):
        return pltpu.make_async_remote_copy(
            src_ref=all_mine,
            dst_ref=all_in.at[a * n_band + b - 1],
            send_sem=all_send,
            recv_sem=all_recv,
            device_id={"tile": peers[a], "band": others[b]},
            device_id_type=MESH,
        )

    band_whole = pltpu.make_async_remote_copy(
        src_ref=band_in,
        dst_ref=band_in,
        send_sem=band_send,
        recv_sem=band_recv,
        device_id={"tile": me, "band": others[1]},
        device_id_type=MESH,
    )
    all_whole = pltpu.make_async_remote_copy(
        src_ref=all_in,
        dst_ref=all_in,
        send_sem=all_send,
        recv_sem=all_recv,
        device_id={"tile": me, "band": others[1]},
        device_id_type=MESH,
    )

    def scatter_send(it, product, tail=None):
        for p in range(summing):
            r, c = p // col_groups * piece_rows, p % col_groups * piece_cols
            for l in range(lanes):
                at = c + l * LANES
                stage[it, p, l] = product[r : r + piece_rows, at : at + LANES].astype(bf16)
            if tail is not None:
                stage[it, p, lanes] = tail
        for j in range(summing):

            @pl.when((odd == 0) | (ahead[j] != mine))
            def _():
                scatter_copy(it, j).start()

    def lanes_sum(x):
        total = x[0]
        for l in range(1, lanes):
            total = total + x[l]
        return jnp.sum(total, axis=0, keepdims=True)

    def landed_sum(it, slab):
        some = pl.ds(0, parts_of[it])
        total = (
            stage[it, mine, some].astype(f32)
            if slab
            else jnp.zeros((parts_of[it], piece_rows, LANES), f32)
        )
        for h in reversed(tile_order):
            if h or not slab:
                landing(it, slab, peers[h]).wait_recv()
                total = total + landed[it, slab, peers[h], some].astype(f32)
        return total

    def gather_send(it, slab, vector, tail):
        for l in range(lanes + 1):
            part = three_parts(tail) if l == lanes else vector[l].astype(bf16)
            if slab:
                packed[it, mine, l] = part
            else:
                passed[it, l] = part
        for h in tile_order:
            if h or not slab:
                gather_copy(it, slab, h).start()

    def joined(it, piece):
        return jnp.concatenate([packed[it, piece, l] for l in range(lanes)], axis=1)

    def column(it, c):
        return jnp.concatenate(
            [joined(it, r * col_groups + c) for r in range(row_groups)], axis=0
        )

    def forward(it):
        out = jnp.zeros((n_block, rows), f32)
        for j in reversed(range(summing)):

            @pl.when((odd == 0) | (ahead[j] != mine))
            def _():
                arriving(it, ahead[j]).wait_recv()

            if row_groups == 1:
                out = out + jnp.dot(
                    joined(it, ahead[j]), turned[ahead[j]], preferred_element_type=f32
                )
        if row_groups > 1:
            for c in range(col_groups):
                out = out + jnp.dot(column(it, c), turned[c], preferred_element_type=f32)
        out = jnp.sum(jnp.where(names, out, jnp.zeros((), f32)), axis=0, keepdims=True)
        cols = []
        per = k * pix // LANES
        for t in range(tile_rows):
            acc = out[:, t * per * LANES : t * per * LANES + LANES]
            for c in range(1, per):
                at = (t * per + c) * LANES
                acc = acc + out[:, at : at + LANES]
            cols.append(acc + pltpu.roll(acc, pix, 1))
        return jnp.concatenate(
            [jnp.where(low, cols[t], cols[t + 1]) for t in range(0, tile_rows, 2)], axis=1
        )

    def keep_own(it):
        own = (lax.broadcasted_iota(jnp.int32, (8, n_block), 1) - me * tile_rows) == (
            lax.broadcasted_iota(jnp.int32, (8, n_block), 0)
        )
        own = jnp.where(own, 1.0, 0.0).astype(bf16)
        for c in range(col_groups):
            own_buf[it, :, c * piece_cols : (c + 1) * piece_cols] = jnp.dot(
                own, column(it, c), preferred_element_type=f32
            )

    def scatter_sent(it):
        for j in range(summing):

            @pl.when((odd == 0) | (ahead[j] != mine))
            def _():
                scatter_copy(it, j).wait_send()

    def gather_sent(it):
        @pl.when(sums_here)
        def _():
            for h in tile_order:
                gather_copy(it, 0, h).wait_send()
                if h:
                    gather_copy(it, 1, h).wait_send()

    start = measured[...]
    left = both_parts(start)
    bands = band * (width // BANDS_PER_GROUP_PIX) + (
        lax.broadcasted_iota(jnp.int32, (PACKED_ROWS, width), 1) // BANDS_PER_GROUP_PIX
    )
    for e in range(entries):
        t, j = e // k, e % k
        inside = (bands >= window[t, 0, j]) & (bands < window[t, 1, j])
        mask_buf[e] = jnp.where(inside, 1.0, 0.0).astype(bf16)
    product = jnp.zeros((2 * n_block, width), f32)
    for e in range(entries):
        loads[e].wait()
        inside = mask_buf[e]
        for at in range(e * pix, (e + 1) * pix, PACKED_ROWS):
            held[at : at + PACKED_ROWS, :] = held[at : at + PACKED_ROWS, :] * inside
        if (e + 1) % ENTRIES_AT_ONCE == 0:
            upto = (e + 1) * pix
            part = slice(upto - ENTRIES_AT_ONCE * pix, upto)
            product = product + jnp.dot(left[:, part], held[part, :], preferred_element_type=f32)
    pl.semaphore_wait(barrier, n_tile * n_band - 1)
    scatter_send(0, product[:n_block])
    scatter_send(2, product[n_block:])
    for c in range(col_groups):
        turned[c] = held[:, c * piece_cols : (c + 1) * piece_cols].T
    norm_buf[...] = jnp.zeros((3, LANES), f32)

    @pl.when(sums_here)
    def _():
        for slab in range(2):
            gradient = landed_sum(0, slab)
            gather_send(0, slab, gradient, lanes_sum(gradient * gradient))
            grad_buf[slab] = gradient
        for slab in range(2):
            base_buf[slab] = grad_buf[slab] + landed_sum(2, slab)

    band_mine[0:1, :] = forward(0)
    norm = row_of(packed[0, 0, lanes])
    for p in range(1, summing):
        norm = norm + row_of(packed[0, p, lanes])
    band_mine[1:2, :] = norm
    for b in reversed(range(1, n_band)):
        band_copy(b).start()
    keep_own(0)
    for it in (0, 2):
        scatter_sent(it)
    gather_sent(0)
    band_whole.wait_recv()
    total = band_mine[...]
    for b in range(1, n_band):
        total = total + band_in[b - 1]
    image, gamma = total[0:1, :], lane_total(total[1:2, :])

    product = jnp.dot(both_parts(image), held[...], preferred_element_type=f32)
    scatter_send(1, product[:n_block] + product[n_block:], three_parts(image * image))
    band_whole.wait_send()

    def alpha_of(image_square):
        return gamma / (image_square + RIDGE * gamma)

    @pl.when(sums_here)
    def _():
        for slab in range(2):
            turned_image = landed_sum(1, slab)
            square = jnp.sum(turned_image[lanes], axis=0, keepdims=True)
            turned_image = turned_image[:lanes]
            alpha = alpha_of(lane_total(square))
            direction = grad_buf[slab]
            gradient = base_buf[slab] - alpha * (turned_image + RIDGE * direction)
            gather_send(1, slab, gradient, square)
            norm_buf[...] = norm_buf[...] + jnp.concatenate(
                [lanes_sum(gradient * x) for x in (gradient, direction, turned_image)], axis=0
            )

    quarter = LANES // 4
    folded = norm_buf[...]
    folded = folded + pltpu.roll(folded, LANES // 2, 1)
    folded = folded + pltpu.roll(folded, quarter, 1)
    third, zero = lane // quarter, jnp.zeros((1, LANES), f32)
    folded = jnp.where(
        third == 0,
        folded[0:1],
        jnp.where(third == 1, folded[1:2], jnp.where(third == 2, folded[2:3], zero)),
    )
    all_mine[1:2, :] = folded
    all_mine[0:1, :] = forward(1)
    for a, b in everyone:
        all_copy(a, b).start()
    keep_own(1)
    scatter_sent(1)
    gather_sent(1)
    image_square = lane_total(row_of(packed[1, 0, lanes]))
    alpha = alpha_of(image_square)
    residual = start - alpha * image
    all_whole.wait_recv()
    partial = square = None
    for a in range(n_tile):
        total = all_in[a * n_band - 1] if a else all_mine[...]
        for b in range(1, n_band):
            total = total + all_in[a * n_band + b - 1]
        if a:
            sums, square = sums + total, square + total * total
        else:
            partial, sums, square = total[0:1, :], total, total * total
    sums = sums[1:2, :]
    gamma_next, cross, image_cross = [
        lane_total(jnp.where(third == q, sums, zero)) for q in range(3)
    ]
    beta = gamma_next / gamma
    square = lane_total(square[0:1, :]) + 2.0 * beta * image_cross + beta * beta * image_square
    direction_square = gamma_next + 2.0 * beta * cross + beta * beta * gamma
    step = gamma_next / (square + RIDGE * direction_square)
    solved_out[...] = (alpha + step * beta) * own_buf[0, 0:tile_rows, :] + step * own_buf[1, 0:tile_rows, :]
    residual_out[...] = residual - step * (partial + beta * image)
    all_whole.wait_send()


def finish_kernel(solved, residual, solution_out, residual_out):
    solution_out[...] = solved[...]
    residual_out[...] = residual[...]


def body(calib, support, band_window, measured):
    n_tile, n_band = lax.axis_size("tile"), lax.axis_size("band")
    tile_rows, k, pix, width = calib.shape
    entries = tile_rows * k
    sensor = tile_rows * pix
    n_block = n_tile * tile_rows
    _, _, piece_rows, piece_cols = pieces_of(n_tile, n_block, width)
    summing = centre_of(n_tile)[1]
    f32, bf16 = jnp.float32, jnp.bfloat16
    vmem = pl.BlockSpec(memory_space=pltpu.VMEM)
    dma = pltpu.SemaphoreType.DMA
    lanes = piece_cols // LANES
    piece = (lanes + 1, piece_rows, LANES)
    bare = (lanes, piece_rows, LANES)
    hbm = pl.BlockSpec(memory_space=pl.ANY)
    in_hbm = lambda x: pltpu.with_memory_space_constraint(x, pltpu.HBM)
    in_vmem = lambda x: pltpu.with_memory_space_constraint(x, pltpu.VMEM)
    turned_window = jnp.transpose(band_window, (0, 2, 1))
    held_back = pl.pallas_call(
        functools.partial(kernel, n_tile, n_band),
        out_shape=(pltpu.VMEM((tile_rows, width), f32), pltpu.VMEM((1, sensor), f32)),
        in_specs=[hbm] * 4,
        out_specs=(vmem,) * 2,
        scratch_shapes=[
            pltpu.SMEM((tile_rows, k), jnp.int32),
            pltpu.SMEM((tile_rows, 2, k), jnp.int32),
            pltpu.VMEM((1, sensor), f32),
            pltpu.VMEM((entries * pix, width), bf16),
            pltpu.VMEM((width // piece_cols, piece_cols, entries * pix), bf16),
            pltpu.VMEM((3, summing) + piece, bf16),
            pltpu.VMEM((3, 2, n_tile) + piece, bf16),
            pltpu.VMEM((2, summing) + piece, bf16),
            pltpu.VMEM((2,) + piece, bf16),
            pltpu.VMEM((2,) + bare, f32),
            pltpu.VMEM((2,) + bare, f32),
            pltpu.VMEM((3, LANES), f32),
            pltpu.VMEM((2, 8, width), f32),
            pltpu.VMEM((entries, PACKED_ROWS, width), bf16),
            pltpu.VMEM((2, sensor), f32),
            pltpu.VMEM((n_band - 1, 2, sensor), f32),
            pltpu.VMEM((2, sensor), f32),
            pltpu.VMEM((n_band * n_tile - 1, 2, sensor), f32),
            dma((3,)),
            dma((entries,)),
            dma((3, summing)),
            dma((3, 2, n_tile)),
            dma((2, n_tile)),
            dma((2, n_tile)),
            dma((2, summing)),
            dma,
            dma,
            dma,
            dma,
        ],
        compiler_params=pltpu.CompilerParams(
            collective_id=0, has_side_effects=True, vmem_limit_bytes=VMEM_BYTES
        ),
    )(in_hbm(calib), in_hbm(support), in_hbm(turned_window), in_hbm(measured.reshape(1, sensor)))
    solved, residual = pl.pallas_call(
        finish_kernel,
        out_shape=(
            jax.ShapeDtypeStruct((tile_rows, width), f32),
            jax.ShapeDtypeStruct((1, sensor), f32),
        ),
        in_specs=[vmem] * 2,
        out_specs=(vmem, vmem),
        compiler_params=pltpu.CompilerParams(vmem_limit_bytes=VMEM_BYTES),
    )(*[in_vmem(x) for x in held_back])
    return solved, residual.reshape(sensor)


def solution(mesh):
    placed = (P("tile", None, None, "band"), P("tile", None), P("tile", None, None), P("tile"))
    return jax.shard_map(
        body, mesh=mesh, in_specs=placed, out_specs=(P("tile", "band"), P("tile")), check_vma=False
    )
```

```python
import functools

import jax
import jax.numpy as jnp
from jax import lax
from jax.experimental import pallas as pl
from jax.experimental.pallas import tpu as pltpu
from jax.sharding import PartitionSpec as P

BANDS_PER_GROUP_PIX = 64
RIDGE = 0.25
LANES = 128
PACKED_ROWS = 16
VMEM_BYTES = 48 << 20
MESH = pl.DeviceIdType.MESH


def centre_of(n_tile):
    summing = n_tile // 2 if n_tile % 4 == 0 else n_tile
    return (n_tile - summing) // 2, summing


def far_first(n_tile):
    first, _ = centre_of(n_tile)

    def hops(h):
        there = first ^ h
        return abs(there // 2 - first // 2) + (there ^ first) % 2

    return sorted(range(n_tile), key=lambda h: (-hops(h), -h))


def pieces_of(n_tile, n_block, width):
    summing = centre_of(n_tile)[1]
    col_groups = min(summing, width // LANES)
    row_groups = summing // col_groups
    return col_groups, row_groups, n_block // row_groups, width // col_groups


def kernel(
    n_tile,
    n_band,
    calib,
    support_in,
    window_in,
    measured_in,
    solved_out,
    residual_out,
    support,
    window,
    measured,
    held,
    turned,
    stage,
    landed,
    packed,
    passed,
    grad_buf,
    base_buf,
    norm_buf,
    own_buf,
    mask_buf,
    band_mine,
    band_in,
    all_mine,
    all_in,
    small_sem,
    load_sem,
    rs_send,
    rs_recv,
    ag_send,
    ag_pass,
    ag_recv,
    band_send,
    band_recv,
    all_send,
    all_recv,
):
    tile_rows, k, pix, width = calib.shape
    entries = tile_rows * k
    rows = entries * pix
    n_block = n_tile * tile_rows
    col_groups, row_groups, piece_rows, piece_cols = pieces_of(n_tile, n_block, width)
    me = lax.axis_index("tile")
    band = lax.axis_index("band")
    odd = band % 2
    first, summing = centre_of(n_tile)
    mine = me - first
    sums_here = (odd == 1) & (mine >= 0) & (mine < summing)
    f32, bf16 = jnp.float32, jnp.bfloat16

    small = [
        pltpu.make_async_copy(source, target, small_sem.at[i])
        for i, (source, target) in enumerate(
            ((support_in, support), (window_in, window), (measured_in, measured))
        )
    ]
    for copy in small:
        copy.start()
    loads = []
    for e in range(entries):
        copy = pltpu.make_async_copy(
            calib.at[e // k, e % k], held.at[pl.ds(e * pix, pix), :], load_sem.at[e]
        )
        copy.start()
        loads.append(copy)

    def paired(index, n):
        turns = [(1 << b) * (1 - 2 * (index // (1 << b) % 2)) for b in range(n.bit_length() - 1)]
        return [
            sum([turn for b, turn in enumerate(turns) if h >> b & 1], index) for h in range(n)
        ]

    peers, others = paired(me, n_tile), paired(band, n_band)
    tile_order = far_first(n_tile)
    everyone = sorted(
        [(a, b) for a in range(n_tile) for b in range(n_band) if a or b],
        key=lambda s: -bin(s[0] * n_band + s[1]).count("1"),
    )
    barrier = pltpu.get_barrier_semaphore()
    for a, b in everyone:
        pl.semaphore_signal(
            barrier,
            inc=1,
            device_id={"tile": peers[a], "band": others[b]},
            device_id_type=MESH,
        )

    for copy in small:
        copy.wait()
    lane_entry = lax.broadcasted_iota(jnp.int32, (1, rows), 1) // pix
    sup_row = jnp.zeros((1, rows), jnp.int32)
    for e in range(entries):
        sup_row = jnp.where(lane_entry == e, support[e // k, e % k], sup_row)
    names = jnp.broadcast_to(sup_row, (n_block, rows)) == lax.broadcasted_iota(
        jnp.int32, (n_block, rows), 0
    )

    lane = lax.broadcasted_iota(jnp.int32, (1, LANES), 1)
    low = lane < pix

    def spread(w):
        pieces = []
        for t in range(tile_rows):
            col = t * pix // LANES * LANES
            tilev = w[:, col : col + LANES]
            rolled = pltpu.roll(tilev, pix, 1)
            both = jnp.where(low, tilev, rolled) if t * pix % LANES == 0 else jnp.where(low, rolled, tilev)
            pieces += [both] * (k * pix // LANES)
        return jnp.concatenate(pieces, axis=1)

    def rounded(x):
        return x.astype(bf16).astype(f32)

    def left_side(w):
        wide = jnp.broadcast_to(spread(w), (n_block, rows))
        return jnp.where(names, wide, jnp.zeros((), f32)).astype(bf16)

    def both_parts(w):
        high = rounded(w)
        return jnp.concatenate([left_side(high), left_side(w - high)], axis=0)

    def three_parts(values):
        row = lax.broadcasted_iota(jnp.int32, (piece_rows, LANES), 0)
        parts = jnp.zeros((piece_rows, LANES), f32)
        for i, x in enumerate(values):
            high = rounded(x)
            middle = rounded(x - high)
            for l, part in enumerate((high, middle, x - high - middle)):
                parts = jnp.where(row == 3 * i + l, part, parts)
        return parts.astype(bf16)

    def lane_total(x):
        return jnp.sum(x, axis=1, keepdims=True)

    side = me // (n_tile // 2)
    ahead = [(1 - side) * (summing - 1 - j) + side * j for j in range(summing)]

    lanes = piece_cols // LANES
    parts_of = [lanes, lanes + 1, lanes]

    def scatter_copy(it, j):
        some = pl.ds(0, parts_of[it])
        return pltpu.make_async_remote_copy(
            src_ref=stage.at[it, ahead[j], some],
            dst_ref=landed.at[it, odd, me, some],
            send_sem=rs_send.at[it, j],
            recv_sem=rs_recv.at[it, odd, me],
            device_id={"tile": first + ahead[j], "band": band + 1 - odd},
            device_id_type=MESH,
        )

    def landing(it, slab, tile):
        some = pl.ds(0, parts_of[it])
        return pltpu.make_async_remote_copy(
            src_ref=stage.at[it, 0, some],
            dst_ref=landed.at[it, slab, tile, some],
            send_sem=rs_send.at[it, 0],
            recv_sem=rs_recv.at[it, slab, tile],
            device_id={"tile": tile, "band": band - 1},
            device_id_type=MESH,
        )

    def gather_copy(it, slab, h):
        return pltpu.make_async_remote_copy(
            src_ref=packed.at[it, mine] if slab else passed.at[it],
            dst_ref=packed.at[it, mine],
            send_sem=(ag_send if slab else ag_pass).at[it, h],
            recv_sem=ag_recv.at[it, mine],
            device_id={"tile": peers[h], "band": band if slab else band - 1},
            device_id_type=MESH,
        )

    def arriving(it, piece):
        return pltpu.make_async_remote_copy(
            src_ref=packed.at[it, piece],
            dst_ref=packed.at[it, piece],
            send_sem=ag_send.at[it, 0],
            recv_sem=ag_recv.at[it, piece],
            device_id={"tile": first + piece, "band": band + 1 - odd},
            device_id_type=MESH,
        )

    def band_copy(b):
        return pltpu.make_async_remote_copy(
            src_ref=band_mine,
            dst_ref=band_in.at[b - 1],
            send_sem=band_send,
            recv_sem=band_recv,
            device_id={"tile": me, "band": others[b]},
            device_id_type=MESH,
        )

    def all_copy(a, b):
        return pltpu.make_async_remote_copy(
            src_ref=all_mine,
            dst_ref=all_in.at[a * n_band + b - 1],
            send_sem=all_send,
            recv_sem=all_recv,
            device_id={"tile": peers[a], "band": others[b]},
            device_id_type=MESH,
        )

    band_whole = pltpu.make_async_remote_copy(
        src_ref=band_in,
        dst_ref=band_in,
        send_sem=band_send,
        recv_sem=band_recv,
        device_id={"tile": me, "band": others[1]},
        device_id_type=MESH,
    )
    all_whole = pltpu.make_async_remote_copy(
        src_ref=all_in,
        dst_ref=all_in,
        send_sem=all_send,
        recv_sem=all_recv,
        device_id={"tile": me, "band": others[1]},
        device_id_type=MESH,
    )

    def scatter_start(it, j):
        @pl.when((odd == 0) | (ahead[j] != mine))
        def _():
            scatter_copy(it, j).start()

    def put(it, p, product):
        for l in range(lanes):
            stage[it, p, l] = product[:, l * LANES : (l + 1) * LANES].astype(bf16)

    def scatter_send(it, left, finish):
        if row_groups > 1:
            product = jnp.dot(left, held[...], preferred_element_type=f32)
            for p in range(summing):
                r, c = p // col_groups * piece_rows, p % col_groups * piece_cols
                at = product[:, c : c + piece_cols]
                finish(p, at[r : r + piece_rows], at[n_block + r : n_block + r + piece_rows])
        for j in range(summing):
            if row_groups == 1:
                at = pl.ds(pl.multiple_of(ahead[j] * piece_cols, LANES), piece_cols)
                product = jnp.dot(left, held[:, at], preferred_element_type=f32)
                finish(ahead[j], product[:n_block], product[n_block:])
            scatter_start(it, j)

    def lanes_sum(x):
        total = x[0]
        for l in range(1, lanes):
            total = total + x[l]
        return jnp.sum(total, axis=0, keepdims=True)

    def landed_sum(it, slab):
        some = pl.ds(0, parts_of[it])
        total = (
            stage[it, mine, some].astype(f32)
            if slab
            else jnp.zeros((parts_of[it], piece_rows, LANES), f32)
        )
        for h in reversed(tile_order):
            if h or not slab:
                landing(it, slab, peers[h]).wait_recv()
                total = total + landed[it, slab, peers[h], some].astype(f32)
        return total

    gather_order = sorted(
        [(h, slab) for slab in range(2) for h in range(n_tile) if h or not slab],
        key=lambda s: (tile_order.index(s[0]) + (2 * len(tile_order) // 3) * s[1], s[1]),
    )

    def gather_send(it, vectors):
        for l in range(lanes):
            passed[it, l] = vectors[0][l].astype(bf16)
            packed[it, mine, l] = vectors[1][l].astype(bf16)
        for h, slab in gather_order:
            gather_copy(it, slab, h).start()

    def joined(it, piece):
        return jnp.concatenate([packed[it, piece, l] for l in range(lanes)], axis=1)

    def column(it, c):
        return jnp.concatenate(
            [joined(it, r * col_groups + c) for r in range(row_groups)], axis=0
        )

    def forward(it):
        out = jnp.zeros((n_block, rows), f32)
        for j in reversed(range(summing)):

            @pl.when((odd == 0) | (ahead[j] != mine))
            def _():
                arriving(it, ahead[j]).wait_recv()

            if row_groups == 1:
                out = out + jnp.dot(
                    joined(it, ahead[j]), turned[ahead[j]], preferred_element_type=f32
                )
        if row_groups > 1:
            for c in range(col_groups):
                out = out + jnp.dot(column(it, c), turned[c], preferred_element_type=f32)
        out = jnp.where(names, out, jnp.zeros((), f32))
        cols = []
        per = k * pix // LANES
        for t in range(tile_rows):
            acc = out[:, t * per * LANES : t * per * LANES + LANES]
            for c in range(1, per):
                at = (t * per + c) * LANES
                acc = acc + out[:, at : at + LANES]
            acc = jnp.sum(acc, axis=0, keepdims=True)
            cols.append(acc + pltpu.roll(acc, pix, 1))
        return jnp.concatenate(
            [jnp.where(low, cols[t], cols[t + 1]) for t in range(0, tile_rows, 2)], axis=1
        )

    def keep_own(it):
        own = (lax.broadcasted_iota(jnp.int32, (8, n_block), 1) - me * tile_rows) == (
            lax.broadcasted_iota(jnp.int32, (8, n_block), 0)
        )
        own = jnp.where(own, 1.0, 0.0).astype(bf16)
        for c in range(col_groups):
            own_buf[it, :, c * piece_cols : (c + 1) * piece_cols] = jnp.dot(
                own, column(it, c), preferred_element_type=f32
            )

    def scatter_sent(it):
        for j in range(summing):

            @pl.when((odd == 0) | (ahead[j] != mine))
            def _():
                scatter_copy(it, j).wait_send()

    def gather_sent(it):
        @pl.when(sums_here)
        def _():
            for h in tile_order:
                gather_copy(it, 0, h).wait_send()
                if h:
                    gather_copy(it, 1, h).wait_send()

    start = measured[...]
    left = both_parts(start)
    bands = band * (width // BANDS_PER_GROUP_PIX) + (
        lax.broadcasted_iota(jnp.int32, (PACKED_ROWS, width), 1) // BANDS_PER_GROUP_PIX
    )
    for e in range(entries):
        t, j = e // k, e % k
        inside = (bands >= window[t, 0, j]) & (bands < window[t, 1, j])
        mask_buf[e] = jnp.where(inside, 1.0, 0.0).astype(bf16)
    for e in range(entries):
        loads[e].wait()
        inside = mask_buf[e]
        for at in range(e * pix, (e + 1) * pix, PACKED_ROWS):
            held[at : at + PACKED_ROWS, :] = held[at : at + PACKED_ROWS, :] * inside
    pl.semaphore_wait(barrier, n_tile * n_band - 1)

    def put_both(p, high, rest):
        put(0, p, high)
        put(2, p, rest)

    scatter_send(0, left, put_both)
    for j in range(summing):
        scatter_start(2, j)
    for c in range(col_groups):
        turned[c] = held[:, c * piece_cols : (c + 1) * piece_cols].T
    norm_buf[...] = jnp.zeros((8, LANES), f32)

    @pl.when(sums_here)
    def _():
        own = landed_sum(0, 1)
        gradients = [landed_sum(0, 0), own]
        gather_send(0, gradients)
        norm_buf[3:4, :] = sum(lanes_sum(gradient * gradient) for gradient in gradients)
        for slab in range(2):
            grad_buf[slab] = gradients[slab]
            base_buf[slab] = gradients[slab] + landed_sum(2, slab)

    band_mine[1:2, :] = norm_buf[3:4, :]
    band_mine[0:1, :] = forward(0)
    for b in reversed(range(1, n_band)):
        band_copy(b).start()
    keep_own(0)
    for it in (0, 2):
        scatter_sent(it)
    gather_sent(0)
    band_whole.wait_recv()
    total = band_mine[...]
    for b in range(1, n_band):
        total = total + band_in[b - 1]
    image = total[0:1, :]

    tail = three_parts((image * image, total[1:2, :]))
    for p in range(summing):
        stage[1, p, lanes] = tail
    scatter_send(1, both_parts(image), lambda p, high, rest: put(1, p, high + rest))
    norm_buf[4:5, :] = image * image * (1.0 / n_band)
    band_whole.wait_send()

    @pl.when(sums_here)
    def _():
        own = landed_sum(1, 1)
        sums = lane_total(own[lanes])
        image_square, gamma = [sum(sums[3 * i + l : 3 * i + l + 1] for l in range(3)) for i in range(2)]
        alpha = gamma / (image_square + RIDGE * gamma)
        kept = [
            base_buf[slab] - (RIDGE * alpha) * grad_buf[slab] for slab in range(2)
        ]
        turned_images = [landed_sum(1, 0)[:lanes], own[:lanes]]
        gradients = [kept[slab] - alpha * turned_images[slab] for slab in range(2)]
        gather_send(1, gradients)
        norm_buf[0:1, :] = sum(lanes_sum(x * x) for x in gradients)
        norm_buf[1:2, :] = sum(lanes_sum(x * grad_buf[slab]) for slab, x in enumerate(gradients))
        norm_buf[2:3, :] = sum(lanes_sum(x * y) for x, y in zip(gradients, turned_images))

    group = LANES // 8
    folded = norm_buf[...]
    for by in (4, 2, 1):
        folded = folded + pltpu.roll(folded, by * group, 1)
    one_of = lax.broadcasted_iota(jnp.int32, (8, LANES), 1) // group == lax.broadcasted_iota(
        jnp.int32, (8, LANES), 0
    )
    folded = jnp.sum(jnp.where(one_of, folded, jnp.zeros((), f32)), axis=0, keepdims=True)
    all_mine[1:2, :] = folded
    all_mine[0:1, :] = forward(1)
    for a, b in everyone:
        all_copy(a, b).start()
    keep_own(1)
    scatter_sent(1)
    gather_sent(1)
    all_whole.wait_recv()
    partial = square = None
    for a in range(n_tile):
        total = all_in[a * n_band - 1] if a else all_mine[...]
        for b in range(1, n_band):
            total = total + all_in[a * n_band + b - 1]
        if a:
            sums, square = sums + total, square + total * total
        else:
            partial, sums, square = total[0:1, :], total, total * total
    sums = jnp.broadcast_to(sums[1:2, :], (8, LANES))
    sums = lane_total(jnp.where(one_of, sums, jnp.zeros((), f32)))
    gamma_next, cross, image_cross, gamma, image_square = [sums[q : q + 1] for q in range(5)]
    alpha = gamma / (image_square + RIDGE * gamma)
    beta = gamma_next / gamma
    square = lane_total(square[0:1, :]) + 2.0 * beta * image_cross + beta * beta * image_square
    direction_square = gamma_next + 2.0 * beta * cross + beta * beta * gamma
    step = gamma_next / (square + RIDGE * direction_square)
    solved_out[...] = (alpha + step * beta) * own_buf[0, 0:tile_rows, :] + step * own_buf[1, 0:tile_rows, :]
    residual_out[...] = start - (alpha + step * beta) * image - step * partial
    all_whole.wait_send()


def finish_kernel(solved, residual, solution_out, residual_out):
    solution_out[...] = solved[...]
    residual_out[...] = residual[...]


def body(calib, support, band_window, measured):
    n_tile, n_band = lax.axis_size("tile"), lax.axis_size("band")
    tile_rows, k, pix, width = calib.shape
    entries = tile_rows * k
    sensor = tile_rows * pix
    n_block = n_tile * tile_rows
    _, _, piece_rows, piece_cols = pieces_of(n_tile, n_block, width)
    summing = centre_of(n_tile)[1]
    f32, bf16 = jnp.float32, jnp.bfloat16
    vmem = pl.BlockSpec(memory_space=pltpu.VMEM)
    dma = pltpu.SemaphoreType.DMA
    lanes = piece_cols // LANES
    piece = (lanes + 1, piece_rows, LANES)
    bare = (lanes, piece_rows, LANES)
    hbm = pl.BlockSpec(memory_space=pl.ANY)
    in_hbm = lambda x: pltpu.with_memory_space_constraint(x, pltpu.HBM)
    in_vmem = lambda x: pltpu.with_memory_space_constraint(x, pltpu.VMEM)
    turned_window = jnp.transpose(band_window, (0, 2, 1))
    held_back = pl.pallas_call(
        functools.partial(kernel, n_tile, n_band),
        out_shape=(pltpu.VMEM((tile_rows, width), f32), pltpu.VMEM((1, sensor), f32)),
        in_specs=[hbm] * 4,
        out_specs=(vmem,) * 2,
        scratch_shapes=[
            pltpu.SMEM((tile_rows, k), jnp.int32),
            pltpu.SMEM((tile_rows, 2, k), jnp.int32),
            pltpu.VMEM((1, sensor), f32),
            pltpu.VMEM((entries * pix, width), bf16),
            pltpu.VMEM((width // piece_cols, piece_cols, entries * pix), bf16),
            pltpu.VMEM((3, summing) + piece, bf16),
            pltpu.VMEM((3, 2, n_tile) + piece, bf16),
            pltpu.VMEM((2, summing) + bare, bf16),
            pltpu.VMEM((2,) + bare, bf16),
            pltpu.VMEM((2,) + bare, f32),
            pltpu.VMEM((2,) + bare, f32),
            pltpu.VMEM((8, LANES), f32),
            pltpu.VMEM((2, 8, width), f32),
            pltpu.VMEM((entries, PACKED_ROWS, width), bf16),
            pltpu.VMEM((2, sensor), f32),
            pltpu.VMEM((n_band - 1, 2, sensor), f32),
            pltpu.VMEM((2, sensor), f32),
            pltpu.VMEM((n_band * n_tile - 1, 2, sensor), f32),
            dma((3,)),
            dma((entries,)),
            dma((3, summing)),
            dma((3, 2, n_tile)),
            dma((2, n_tile)),
            dma((2, n_tile)),
            dma((2, summing)),
            dma,
            dma,
            dma,
            dma,
        ],
        compiler_params=pltpu.CompilerParams(
            collective_id=0, has_side_effects=True, vmem_limit_bytes=VMEM_BYTES
        ),
    )(in_hbm(calib), in_hbm(support), in_hbm(turned_window), in_hbm(measured.reshape(1, sensor)))
    solved, residual = pl.pallas_call(
        finish_kernel,
        out_shape=(
            jax.ShapeDtypeStruct((tile_rows, width), f32),
            jax.ShapeDtypeStruct((1, sensor), f32),
        ),
        in_specs=[vmem] * 2,
        out_specs=(vmem, vmem),
        compiler_params=pltpu.CompilerParams(vmem_limit_bytes=VMEM_BYTES),
    )(*[in_vmem(x) for x in held_back])
    return solved, residual.reshape(sensor)


def solution(mesh):
    placed = (P("tile", None, None, "band"), P("tile", None), P("tile", None, None), P("tile"))
    return jax.shard_map(
        body, mesh=mesh, in_specs=placed, out_specs=(P("tile", "band"), P("tile")), check_vma=False
    )
```

```python
import functools

import jax
import jax.numpy as jnp
from jax import lax
from jax.experimental import pallas as pl
from jax.experimental.pallas import tpu as pltpu
from jax.sharding import PartitionSpec as P

BANDS_PER_GROUP_PIX = 64
RIDGE = 0.25
LANES = 128
PACKED_ROWS = 16
VMEM_BYTES = 48 << 20
MESH = pl.DeviceIdType.MESH


def centre_of(n_tile):
    summing = n_tile // 2 if n_tile % 4 == 0 else n_tile
    return (n_tile - summing) // 2, summing


def far_first(n_tile):
    first, _ = centre_of(n_tile)

    def hops(h):
        there = first ^ h
        return abs(there // 2 - first // 2) + (there ^ first) % 2

    return sorted(range(n_tile), key=lambda h: (-hops(h), -h))


def pieces_of(n_tile, n_block, width):
    summing = centre_of(n_tile)[1]
    col_groups = min(summing, width // LANES)
    row_groups = summing // col_groups
    return col_groups, row_groups, n_block // row_groups, width // col_groups


def kernel(
    n_tile,
    n_band,
    calib,
    support_in,
    window_in,
    measured_in,
    solved_out,
    residual_out,
    support,
    window,
    measured,
    held,
    turned,
    stage,
    landed,
    packed,
    passed,
    grad_buf,
    base_buf,
    norm_buf,
    own_buf,
    mask_buf,
    band_mine,
    band_in,
    all_mine,
    all_in,
    small_sem,
    load_sem,
    rs_send,
    rs_recv,
    ag_send,
    ag_pass,
    ag_recv,
    band_send,
    band_recv,
    all_send,
    all_recv,
):
    tile_rows, k, pix, width = calib.shape
    entries = tile_rows * k
    rows = entries * pix
    n_block = n_tile * tile_rows
    col_groups, row_groups, piece_rows, piece_cols = pieces_of(n_tile, n_block, width)
    me = lax.axis_index("tile")
    band = lax.axis_index("band")
    odd = band % 2
    first, summing = centre_of(n_tile)
    mine = me - first
    sums_here = (odd == 1) & (mine >= 0) & (mine < summing)
    f32, bf16 = jnp.float32, jnp.bfloat16

    small = [
        pltpu.make_async_copy(source, target, small_sem.at[i])
        for i, (source, target) in enumerate(
            ((support_in, support), (window_in, window), (measured_in, measured))
        )
    ]
    for copy in small:
        copy.start()
    loads = []
    for e in range(entries):
        copy = pltpu.make_async_copy(
            calib.at[e // k, e % k], held.at[pl.ds(e * pix, pix), :], load_sem.at[e]
        )
        copy.start()
        loads.append(copy)

    def paired(index, n):
        turns = [(1 << b) * (1 - 2 * (index // (1 << b) % 2)) for b in range(n.bit_length() - 1)]
        return [
            sum([turn for b, turn in enumerate(turns) if h >> b & 1], index) for h in range(n)
        ]

    peers, others = paired(me, n_tile), paired(band, n_band)
    tile_order = far_first(n_tile)
    everyone = sorted(
        [(a, b) for a in range(n_tile) for b in range(n_band) if a or b],
        key=lambda s: -bin(s[0] * n_band + s[1]).count("1"),
    )
    barrier = pltpu.get_barrier_semaphore()

    def greet(tile, band):
        pl.semaphore_signal(
            barrier, inc=1, device_id={"tile": tile, "band": band}, device_id_type=MESH
        )

    @pl.when(sums_here)
    def _():
        for h in tile_order:
            greet(peers[h], band - 1)
            if h:
                greet(peers[h], band)

    @pl.when(jnp.logical_not(sums_here))
    def _():
        for p in range(summing):
            greet(first + p, band + 1 - odd)

    for b in range(1, n_band):
        greet(me, others[b])

    for copy in small:
        copy.wait()
    lane_entry = lax.broadcasted_iota(jnp.int32, (1, rows), 1) // pix
    sup_row = jnp.zeros((1, rows), jnp.int32)
    for e in range(entries):
        sup_row = jnp.where(lane_entry == e, support[e // k, e % k], sup_row)
    names = jnp.broadcast_to(sup_row, (n_block, rows)) == lax.broadcasted_iota(
        jnp.int32, (n_block, rows), 0
    )

    lane = lax.broadcasted_iota(jnp.int32, (1, LANES), 1)
    low = lane < pix

    def spread(w):
        pieces = []
        for t in range(tile_rows):
            col = t * pix // LANES * LANES
            tilev = w[:, col : col + LANES]
            rolled = pltpu.roll(tilev, pix, 1)
            both = jnp.where(low, tilev, rolled) if t * pix % LANES == 0 else jnp.where(low, rolled, tilev)
            pieces += [both] * (k * pix // LANES)
        return jnp.concatenate(pieces, axis=1)

    def rounded(x):
        return x.astype(bf16).astype(f32)

    def left_side(w):
        wide = jnp.broadcast_to(spread(w), (n_block, rows))
        return jnp.where(names, wide, jnp.zeros((), f32)).astype(bf16)

    def both_parts(w):
        high = rounded(w)
        return jnp.concatenate([left_side(high), left_side(w - high)], axis=0)

    def three_parts(values):
        row = lax.broadcasted_iota(jnp.int32, (piece_rows, LANES), 0)
        parts = jnp.zeros((piece_rows, LANES), f32)
        for i, x in enumerate(values):
            high = rounded(x)
            middle = rounded(x - high)
            for l, part in enumerate((high, middle, x - high - middle)):
                parts = jnp.where(row == 3 * i + l, part, parts)
        return parts.astype(bf16)

    def lane_total(x):
        return jnp.sum(x, axis=1, keepdims=True)

    side = me // (n_tile // 2)
    ahead = [(1 - side) * (summing - 1 - j) + side * j for j in range(summing)]

    lanes = piece_cols // LANES
    parts_of = [lanes, lanes + 1, lanes]

    def scatter_copy(it, j):
        some = pl.ds(0, parts_of[it])
        return pltpu.make_async_remote_copy(
            src_ref=stage.at[it, ahead[j], some],
            dst_ref=landed.at[it, odd, me, some],
            send_sem=rs_send.at[it, j],
            recv_sem=rs_recv.at[it, odd, me],
            device_id={"tile": first + ahead[j], "band": band + 1 - odd},
            device_id_type=MESH,
        )

    def landing(it, slab, tile):
        some = pl.ds(0, parts_of[it])
        return pltpu.make_async_remote_copy(
            src_ref=stage.at[it, 0, some],
            dst_ref=landed.at[it, slab, tile, some],
            send_sem=rs_send.at[it, 0],
            recv_sem=rs_recv.at[it, slab, tile],
            device_id={"tile": tile, "band": band - 1},
            device_id_type=MESH,
        )

    def gather_copy(it, slab, h):
        return pltpu.make_async_remote_copy(
            src_ref=packed.at[it, mine] if slab else passed.at[it],
            dst_ref=packed.at[it, mine],
            send_sem=(ag_send if slab else ag_pass).at[it, h],
            recv_sem=ag_recv.at[it, mine],
            device_id={"tile": peers[h], "band": band if slab else band - 1},
            device_id_type=MESH,
        )

    def arriving(it, piece):
        return pltpu.make_async_remote_copy(
            src_ref=packed.at[it, piece],
            dst_ref=packed.at[it, piece],
            send_sem=ag_send.at[it, 0],
            recv_sem=ag_recv.at[it, piece],
            device_id={"tile": first + piece, "band": band + 1 - odd},
            device_id_type=MESH,
        )

    def band_copy(b):
        return pltpu.make_async_remote_copy(
            src_ref=band_mine,
            dst_ref=band_in.at[b - 1],
            send_sem=band_send,
            recv_sem=band_recv,
            device_id={"tile": me, "band": others[b]},
            device_id_type=MESH,
        )

    def all_copy(a, b):
        return pltpu.make_async_remote_copy(
            src_ref=all_mine,
            dst_ref=all_in.at[a * n_band + b - 1],
            send_sem=all_send,
            recv_sem=all_recv,
            device_id={"tile": peers[a], "band": others[b]},
            device_id_type=MESH,
        )

    band_whole = pltpu.make_async_remote_copy(
        src_ref=band_in,
        dst_ref=band_in,
        send_sem=band_send,
        recv_sem=band_recv,
        device_id={"tile": me, "band": others[1]},
        device_id_type=MESH,
    )
    all_whole = pltpu.make_async_remote_copy(
        src_ref=all_in,
        dst_ref=all_in,
        send_sem=all_send,
        recv_sem=all_recv,
        device_id={"tile": me, "band": others[1]},
        device_id_type=MESH,
    )

    def scatter_start(it, j):
        @pl.when((odd == 0) | (ahead[j] != mine))
        def _():
            scatter_copy(it, j).start()

    def put(it, p, product):
        for l in range(lanes):
            stage[it, p, l] = product[:, l * LANES : (l + 1) * LANES].astype(bf16)

    def scatter_send(it, left, finish):
        if row_groups > 1:
            product = jnp.dot(left, held[...], preferred_element_type=f32)
            for p in range(summing):
                r, c = p // col_groups * piece_rows, p % col_groups * piece_cols
                at = product[:, c : c + piece_cols]
                finish(p, at[r : r + piece_rows], at[n_block + r : n_block + r + piece_rows])
        for j in range(summing):
            if row_groups == 1:
                at = pl.ds(pl.multiple_of(ahead[j] * piece_cols, LANES), piece_cols)
                product = jnp.dot(left, held[:, at], preferred_element_type=f32)
                finish(ahead[j], product[:n_block], product[n_block:])
            scatter_start(it, j)

    def lanes_sum(x):
        total = x[0]
        for l in range(1, lanes):
            total = total + x[l]
        return jnp.sum(total, axis=0, keepdims=True)

    def landed_sum(it, slab):
        some = pl.ds(0, parts_of[it])
        total = (
            stage[it, mine, some].astype(f32)
            if slab
            else jnp.zeros((parts_of[it], piece_rows, LANES), f32)
        )
        for h in reversed(tile_order):
            if h or not slab:
                landing(it, slab, peers[h]).wait_recv()
                total = total + landed[it, slab, peers[h], some].astype(f32)
        return total

    gather_order = sorted(
        [(h, slab) for slab in range(2) for h in range(n_tile) if h or not slab],
        key=lambda s: (tile_order.index(s[0]) + (2 * len(tile_order) // 3) * s[1], s[1]),
    )

    def gather_send(it, vectors):
        for l in range(lanes):
            passed[it, l] = vectors[0][l].astype(bf16)
            packed[it, mine, l] = vectors[1][l].astype(bf16)
        for h, slab in gather_order:
            gather_copy(it, slab, h).start()

    def joined(it, piece):
        return jnp.concatenate([packed[it, piece, l] for l in range(lanes)], axis=1)

    def column(it, c):
        return jnp.concatenate(
            [joined(it, r * col_groups + c) for r in range(row_groups)], axis=0
        )

    def forward(it):
        out = jnp.zeros((n_block, rows), f32)
        for j in reversed(range(summing)):

            @pl.when((odd == 0) | (ahead[j] != mine))
            def _():
                arriving(it, ahead[j]).wait_recv()

            if row_groups == 1:
                out = out + jnp.dot(
                    joined(it, ahead[j]), turned[ahead[j]], preferred_element_type=f32
                )
        if row_groups > 1:
            for c in range(col_groups):
                out = out + jnp.dot(column(it, c), turned[c], preferred_element_type=f32)
        out = jnp.where(names, out, jnp.zeros((), f32))
        cols = []
        per = k * pix // LANES
        for t in range(tile_rows):
            acc = out[:, t * per * LANES : t * per * LANES + LANES]
            for c in range(1, per):
                at = (t * per + c) * LANES
                acc = acc + out[:, at : at + LANES]
            acc = jnp.sum(acc, axis=0, keepdims=True)
            cols.append(acc + pltpu.roll(acc, pix, 1))
        return jnp.concatenate(
            [jnp.where(low, cols[t], cols[t + 1]) for t in range(0, tile_rows, 2)], axis=1
        )

    def keep_own(it):
        own = (lax.broadcasted_iota(jnp.int32, (8, n_block), 1) - me * tile_rows) == (
            lax.broadcasted_iota(jnp.int32, (8, n_block), 0)
        )
        own = jnp.where(own, 1.0, 0.0).astype(bf16)
        for c in range(col_groups):
            own_buf[it, :, c * piece_cols : (c + 1) * piece_cols] = jnp.dot(
                own, column(it, c), preferred_element_type=f32
            )

    def scatter_sent(it):
        for j in range(summing):

            @pl.when((odd == 0) | (ahead[j] != mine))
            def _():
                scatter_copy(it, j).wait_send()

    def gather_sent(it):
        @pl.when(sums_here)
        def _():
            for h in tile_order:
                gather_copy(it, 0, h).wait_send()
                if h:
                    gather_copy(it, 1, h).wait_send()

    start = measured[...]
    left = both_parts(start)
    bands = band * (width // BANDS_PER_GROUP_PIX) + (
        lax.broadcasted_iota(jnp.int32, (PACKED_ROWS, width), 1) // BANDS_PER_GROUP_PIX
    )
    for e in range(entries):
        t, j = e // k, e % k
        inside = (bands >= window[t, 0, j]) & (bands < window[t, 1, j])
        mask_buf[e] = jnp.where(inside, 1.0, 0.0).astype(bf16)
    for e in range(entries):
        loads[e].wait()
        inside = mask_buf[e]
        for at in range(e * pix, (e + 1) * pix, PACKED_ROWS):
            held[at : at + PACKED_ROWS, :] = held[at : at + PACKED_ROWS, :] * inside
    pl.semaphore_wait(barrier, jnp.where(sums_here, 2 * n_tile - 1, summing) + n_band - 1)

    def put_both(p, high, rest):
        put(0, p, high)
        put(2, p, rest)

    scatter_send(0, left, put_both)
    for c in range(col_groups):
        turned[c] = held[:, c * piece_cols : (c + 1) * piece_cols].T
    norm_buf[...] = jnp.zeros((8, LANES), f32)

    @pl.when(sums_here)
    def _():
        own = landed_sum(0, 1)
        gradients = [landed_sum(0, 0), own]
        gather_send(0, gradients)
        norm_buf[3:4, :] = sum(lanes_sum(gradient * gradient) for gradient in gradients)
        for slab in range(2):
            grad_buf[slab] = gradients[slab]

    band_mine[1:2, :] = norm_buf[3:4, :]
    band_mine[0:1, :] = forward(0)
    for b in reversed(range(1, n_band)):
        band_copy(b).start()
    for j in range(summing):
        scatter_start(2, j)
    keep_own(0)
    scatter_sent(0)
    gather_sent(0)
    band_whole.wait_recv()
    total = band_mine[...]
    for b in range(1, n_band):
        total = total + band_in[b - 1]
    image = total[0:1, :]

    tail = three_parts((image * image, total[1:2, :]))
    for p in range(summing):
        stage[1, p, lanes] = tail
    scatter_send(1, both_parts(image), lambda p, high, rest: put(1, p, high + rest))
    norm_buf[4:5, :] = image * image * (1.0 / n_band)
    band_whole.wait_send()
    scatter_sent(2)

    @pl.when(sums_here)
    def _():
        for slab in range(2):
            base_buf[slab] = grad_buf[slab] + landed_sum(2, slab)
        own = landed_sum(1, 1)
        sums = lane_total(own[lanes])
        image_square, gamma = [sum(sums[3 * i + l : 3 * i + l + 1] for l in range(3)) for i in range(2)]
        alpha = gamma / (image_square + RIDGE * gamma)
        kept = [
            base_buf[slab] - (RIDGE * alpha) * grad_buf[slab] for slab in range(2)
        ]
        turned_images = [landed_sum(1, 0)[:lanes], own[:lanes]]
        gradients = [kept[slab] - alpha * turned_images[slab] for slab in range(2)]
        gather_send(1, gradients)
        norm_buf[0:1, :] = sum(lanes_sum(x * x) for x in gradients)
        norm_buf[1:2, :] = sum(lanes_sum(x * grad_buf[slab]) for slab, x in enumerate(gradients))
        norm_buf[2:3, :] = sum(lanes_sum(x * y) for x, y in zip(gradients, turned_images))

    group = LANES // 8
    folded = norm_buf[...]
    for by in (4, 2, 1):
        folded = folded + pltpu.roll(folded, by * group, 1)
    one_of = lax.broadcasted_iota(jnp.int32, (8, LANES), 1) // group == lax.broadcasted_iota(
        jnp.int32, (8, LANES), 0
    )
    folded = jnp.sum(jnp.where(one_of, folded, jnp.zeros((), f32)), axis=0, keepdims=True)
    all_mine[1:2, :] = folded
    all_mine[0:1, :] = forward(1)
    for a, b in everyone:
        all_copy(a, b).start()
    keep_own(1)
    scatter_sent(1)
    gather_sent(1)
    all_whole.wait_recv()
    partial = square = None
    for a in range(n_tile):
        total = all_in[a * n_band - 1] if a else all_mine[...]
        for b in range(1, n_band):
            total = total + all_in[a * n_band + b - 1]
        if a:
            sums, square = sums + total, square + total * total
        else:
            partial, sums, square = total[0:1, :], total, total * total
    sums = jnp.broadcast_to(sums[1:2, :], (8, LANES))
    sums = lane_total(jnp.where(one_of, sums, jnp.zeros((), f32)))
    gamma_next, cross, image_cross, gamma, image_square = [sums[q : q + 1] for q in range(5)]
    alpha = gamma / (image_square + RIDGE * gamma)
    beta = gamma_next / gamma
    square = lane_total(square[0:1, :]) + 2.0 * beta * image_cross + beta * beta * image_square
    direction_square = gamma_next + 2.0 * beta * cross + beta * beta * gamma
    step = gamma_next / (square + RIDGE * direction_square)
    solved_out[...] = (alpha + step * beta) * own_buf[0, 0:tile_rows, :] + step * own_buf[1, 0:tile_rows, :]
    residual_out[...] = start - (alpha + step * beta) * image - step * partial
    all_whole.wait_send()


def finish_kernel(solved, residual, solution_out, residual_out):
    solution_out[...] = solved[...]
    residual_out[...] = residual[...]


def body(calib, support, band_window, measured):
    n_tile, n_band = lax.axis_size("tile"), lax.axis_size("band")
    tile_rows, k, pix, width = calib.shape
    entries = tile_rows * k
    sensor = tile_rows * pix
    n_block = n_tile * tile_rows
    _, _, piece_rows, piece_cols = pieces_of(n_tile, n_block, width)
    summing = centre_of(n_tile)[1]
    f32, bf16 = jnp.float32, jnp.bfloat16
    vmem = pl.BlockSpec(memory_space=pltpu.VMEM)
    dma = pltpu.SemaphoreType.DMA
    lanes = piece_cols // LANES
    piece = (lanes + 1, piece_rows, LANES)
    bare = (lanes, piece_rows, LANES)
    hbm = pl.BlockSpec(memory_space=pl.ANY)
    in_hbm = lambda x: pltpu.with_memory_space_constraint(x, pltpu.HBM)
    in_vmem = lambda x: pltpu.with_memory_space_constraint(x, pltpu.VMEM)
    turned_window = jnp.transpose(band_window, (0, 2, 1))
    held_back = pl.pallas_call(
        functools.partial(kernel, n_tile, n_band),
        out_shape=(pltpu.VMEM((tile_rows, width), f32), pltpu.VMEM((1, sensor), f32)),
        in_specs=[hbm] * 4,
        out_specs=(vmem,) * 2,
        scratch_shapes=[
            pltpu.SMEM((tile_rows, k), jnp.int32),
            pltpu.SMEM((tile_rows, 2, k), jnp.int32),
            pltpu.VMEM((1, sensor), f32),
            pltpu.VMEM((entries * pix, width), bf16),
            pltpu.VMEM((width // piece_cols, piece_cols, entries * pix), bf16),
            pltpu.VMEM((3, summing) + piece, bf16),
            pltpu.VMEM((3, 2, n_tile) + piece, bf16),
            pltpu.VMEM((2, summing) + bare, bf16),
            pltpu.VMEM((2,) + bare, bf16),
            pltpu.VMEM((2,) + bare, f32),
            pltpu.VMEM((2,) + bare, f32),
            pltpu.VMEM((8, LANES), f32),
            pltpu.VMEM((2, 8, width), f32),
            pltpu.VMEM((entries, PACKED_ROWS, width), bf16),
            pltpu.VMEM((2, sensor), f32),
            pltpu.VMEM((n_band - 1, 2, sensor), f32),
            pltpu.VMEM((2, sensor), f32),
            pltpu.VMEM((n_band * n_tile - 1, 2, sensor), f32),
            dma((3,)),
            dma((entries,)),
            dma((3, summing)),
            dma((3, 2, n_tile)),
            dma((2, n_tile)),
            dma((2, n_tile)),
            dma((2, summing)),
            dma,
            dma,
            dma,
            dma,
        ],
        compiler_params=pltpu.CompilerParams(
            collective_id=0, has_side_effects=True, vmem_limit_bytes=VMEM_BYTES
        ),
    )(in_hbm(calib), in_hbm(support), in_hbm(turned_window), in_hbm(measured.reshape(1, sensor)))
    solved, residual = pl.pallas_call(
        finish_kernel,
        out_shape=(
            jax.ShapeDtypeStruct((tile_rows, width), f32),
            jax.ShapeDtypeStruct((1, sensor), f32),
        ),
        in_specs=[vmem] * 2,
        out_specs=(vmem, vmem),
        compiler_params=pltpu.CompilerParams(vmem_limit_bytes=VMEM_BYTES),
    )(*[in_vmem(x) for x in held_back])
    return solved, residual.reshape(sensor)


def solution(mesh):
    placed = (P("tile", None, None, "band"), P("tile", None), P("tile", None, None), P("tile"))
    return jax.shard_map(
        body, mesh=mesh, in_specs=placed, out_specs=(P("tile", "band"), P("tile")), check_vma=False
    )
```

```python
import functools

import jax
import jax.numpy as jnp
from jax import lax
from jax.experimental import pallas as pl
from jax.experimental.pallas import tpu as pltpu
from jax.sharding import PartitionSpec as P

BANDS_PER_GROUP_PIX = 64
RIDGE = 0.25
LANES = 128
PACKED_ROWS = 16
VMEM_BYTES = 48 << 20
MESH = pl.DeviceIdType.MESH


def centre_of(n_tile):
    summing = n_tile // 2 if n_tile % 4 == 0 else n_tile
    return (n_tile - summing) // 2, summing


def far_first(n_tile):
    first, _ = centre_of(n_tile)

    def hops(h):
        there = first ^ h
        return abs(there // 2 - first // 2) + (there ^ first) % 2

    return sorted(range(n_tile), key=lambda h: (-hops(h), -h))


def pieces_of(n_tile, n_block, width):
    summing = centre_of(n_tile)[1]
    col_groups = min(summing, width // LANES)
    row_groups = summing // col_groups
    return col_groups, row_groups, n_block // row_groups, width // col_groups


def kernel(
    n_tile,
    n_band,
    calib,
    support_in,
    window_in,
    measured_in,
    solved_out,
    residual_out,
    support,
    window,
    measured,
    held,
    turned,
    stage,
    landed,
    packed,
    passed,
    grad_buf,
    base_buf,
    norm_buf,
    own_buf,
    mask_buf,
    band_mine,
    band_in,
    all_mine,
    all_in,
    small_sem,
    load_sem,
    rs_send,
    rs_recv,
    ag_send,
    ag_pass,
    ag_recv,
    band_send,
    band_recv,
    all_send,
    all_recv,
):
    tile_rows, k, pix, width = calib.shape
    entries = tile_rows * k
    rows = entries * pix
    n_block = n_tile * tile_rows
    col_groups, row_groups, piece_rows, piece_cols = pieces_of(n_tile, n_block, width)
    me = lax.axis_index("tile")
    band = lax.axis_index("band")
    odd = band % 2
    first, summing = centre_of(n_tile)
    mine = me - first
    sums_here = (odd == 1) & (mine >= 0) & (mine < summing)
    f32, bf16 = jnp.float32, jnp.bfloat16

    small = [
        pltpu.make_async_copy(source, target, small_sem.at[i])
        for i, (source, target) in enumerate(
            ((support_in, support), (window_in, window), (measured_in, measured))
        )
    ]
    for copy in small:
        copy.start()
    side = me // (n_tile // 2)
    ahead = [(1 - side) * (summing - 1 - j) + side * j for j in range(summing)]
    pieces = ahead if row_groups == 1 else list(range(col_groups))
    loads = []
    for c in pieces:
        cols = pl.ds(pl.multiple_of(c * piece_cols, LANES), piece_cols)
        copy = pltpu.make_async_copy(calib.at[:, :, :, cols], held.at[c], load_sem.at[c])
        copy.start()
        loads.append(copy)

    def paired(index, n):
        turns = [(1 << b) * (1 - 2 * (index // (1 << b) % 2)) for b in range(n.bit_length() - 1)]
        return [
            sum([turn for b, turn in enumerate(turns) if h >> b & 1], index) for h in range(n)
        ]

    peers, others = paired(me, n_tile), paired(band, n_band)
    tile_order = far_first(n_tile)
    everyone = sorted(
        [(a, b) for a in range(n_tile) for b in range(n_band) if a or b],
        key=lambda s: -bin(s[0] * n_band + s[1]).count("1"),
    )
    barrier = pltpu.get_barrier_semaphore()

    def greet(tile, band):
        pl.semaphore_signal(
            barrier, inc=1, device_id={"tile": tile, "band": band}, device_id_type=MESH
        )

    @pl.when(sums_here)
    def _():
        for h in tile_order:
            greet(peers[h], band - 1)
            if h:
                greet(peers[h], band)

    @pl.when(jnp.logical_not(sums_here))
    def _():
        for p in range(summing):
            greet(first + p, band + 1 - odd)

    for b in range(1, n_band):
        greet(me, others[b])

    for copy in small:
        copy.wait()
    lane_entry = lax.broadcasted_iota(jnp.int32, (1, rows), 1) // pix
    sup_row = jnp.zeros((1, rows), jnp.int32)
    for e in range(entries):
        sup_row = jnp.where(lane_entry == e, support[e // k, e % k], sup_row)
    names = jnp.broadcast_to(sup_row, (n_block, rows)) == lax.broadcasted_iota(
        jnp.int32, (n_block, rows), 0
    )

    lane = lax.broadcasted_iota(jnp.int32, (1, LANES), 1)
    low = lane < pix

    def spread(w):
        pieces = []
        for t in range(tile_rows):
            col = t * pix // LANES * LANES
            tilev = w[:, col : col + LANES]
            rolled = pltpu.roll(tilev, pix, 1)
            both = jnp.where(low, tilev, rolled) if t * pix % LANES == 0 else jnp.where(low, rolled, tilev)
            pieces += [both] * (k * pix // LANES)
        return jnp.concatenate(pieces, axis=1)

    def rounded(x):
        return x.astype(bf16).astype(f32)

    def left_side(w):
        wide = jnp.broadcast_to(spread(w), (n_block, rows))
        return jnp.where(names, wide, jnp.zeros((), f32)).astype(bf16)

    def both_parts(w):
        high = rounded(w)
        return jnp.concatenate([left_side(high), left_side(w - high)], axis=0)

    def three_parts(values):
        row = lax.broadcasted_iota(jnp.int32, (piece_rows, LANES), 0)
        parts = jnp.zeros((piece_rows, LANES), f32)
        for i, x in enumerate(values):
            high = rounded(x)
            middle = rounded(x - high)
            for l, part in enumerate((high, middle, x - high - middle)):
                parts = jnp.where(row == 3 * i + l, part, parts)
        return parts.astype(bf16)

    def lane_total(x):
        return jnp.sum(x, axis=1, keepdims=True)

    lanes = piece_cols // LANES
    parts_of = [lanes, lanes + 1, lanes]

    def scatter_copy(it, j):
        some = pl.ds(0, parts_of[it])
        return pltpu.make_async_remote_copy(
            src_ref=stage.at[it, ahead[j], some],
            dst_ref=landed.at[it, odd, me, some],
            send_sem=rs_send.at[it, j],
            recv_sem=rs_recv.at[it, odd, me],
            device_id={"tile": first + ahead[j], "band": band + 1 - odd},
            device_id_type=MESH,
        )

    def landing(it, slab, tile):
        some = pl.ds(0, parts_of[it])
        return pltpu.make_async_remote_copy(
            src_ref=stage.at[it, 0, some],
            dst_ref=landed.at[it, slab, tile, some],
            send_sem=rs_send.at[it, 0],
            recv_sem=rs_recv.at[it, slab, tile],
            device_id={"tile": tile, "band": band - 1},
            device_id_type=MESH,
        )

    def gather_copy(it, slab, h):
        return pltpu.make_async_remote_copy(
            src_ref=packed.at[it, mine] if slab else passed.at[it],
            dst_ref=packed.at[it, mine],
            send_sem=(ag_send if slab else ag_pass).at[it, h],
            recv_sem=ag_recv.at[it, mine],
            device_id={"tile": peers[h], "band": band if slab else band - 1},
            device_id_type=MESH,
        )

    def arriving(it, piece):
        return pltpu.make_async_remote_copy(
            src_ref=packed.at[it, piece],
            dst_ref=packed.at[it, piece],
            send_sem=ag_send.at[it, 0],
            recv_sem=ag_recv.at[it, piece],
            device_id={"tile": first + piece, "band": band + 1 - odd},
            device_id_type=MESH,
        )

    def band_copy(b):
        return pltpu.make_async_remote_copy(
            src_ref=band_mine,
            dst_ref=band_in.at[b - 1],
            send_sem=band_send,
            recv_sem=band_recv,
            device_id={"tile": me, "band": others[b]},
            device_id_type=MESH,
        )

    def all_copy(a, b):
        return pltpu.make_async_remote_copy(
            src_ref=all_mine,
            dst_ref=all_in.at[a * n_band + b - 1],
            send_sem=all_send,
            recv_sem=all_recv,
            device_id={"tile": peers[a], "band": others[b]},
            device_id_type=MESH,
        )

    band_whole = pltpu.make_async_remote_copy(
        src_ref=band_in,
        dst_ref=band_in,
        send_sem=band_send,
        recv_sem=band_recv,
        device_id={"tile": me, "band": others[1]},
        device_id_type=MESH,
    )
    all_whole = pltpu.make_async_remote_copy(
        src_ref=all_in,
        dst_ref=all_in,
        send_sem=all_send,
        recv_sem=all_recv,
        device_id={"tile": me, "band": others[1]},
        device_id_type=MESH,
    )

    def scatter_start(it, j):
        @pl.when((odd == 0) | (ahead[j] != mine))
        def _():
            scatter_copy(it, j).start()

    def put(it, p, product):
        for l in range(lanes):
            stage[it, p, l] = product[:, l * LANES : (l + 1) * LANES].astype(bf16)

    def matrix(c):
        return held[c].reshape(rows, piece_cols)

    def scatter_send(it, left, ready, finish, later):
        for i, c in enumerate(pieces):
            ready(i, c)
            product = jnp.dot(left, matrix(c), preferred_element_type=f32)
            for r in range(row_groups):
                at = slice(r * piece_rows, (r + 1) * piece_rows)
                rest = slice(n_block + r * piece_rows, n_block + (r + 1) * piece_rows)
                finish(r * col_groups + c, product[at], product[rest])
            if row_groups == 1:
                scatter_start(it, i)
            later(c, product)
        if row_groups > 1:
            for j in range(summing):
                scatter_start(it, j)

    def lanes_sum(x):
        total = x[0]
        for l in range(1, lanes):
            total = total + x[l]
        return jnp.sum(total, axis=0, keepdims=True)

    def landed_sum(it, slab):
        some = pl.ds(0, parts_of[it])
        total = (
            stage[it, mine, some].astype(f32)
            if slab
            else jnp.zeros((parts_of[it], piece_rows, LANES), f32)
        )
        for h in reversed(tile_order):
            if h or not slab:
                landing(it, slab, peers[h]).wait_recv()
                total = total + landed[it, slab, peers[h], some].astype(f32)
        return total

    gather_order = sorted(
        [(h, slab) for slab in range(2) for h in range(n_tile) if h or not slab],
        key=lambda s: (tile_order.index(s[0]) + (2 * len(tile_order) // 3) * s[1], s[1]),
    )

    def gather_send(it, vectors):
        for l in range(lanes):
            passed[it, l] = vectors[0][l].astype(bf16)
            packed[it, mine, l] = vectors[1][l].astype(bf16)
        for h, slab in gather_order:
            gather_copy(it, slab, h).start()

    def joined(it, piece):
        return jnp.concatenate([packed[it, piece, l] for l in range(lanes)], axis=1)

    def column(it, c):
        return jnp.concatenate(
            [joined(it, r * col_groups + c) for r in range(row_groups)], axis=0
        )

    def forward(it):
        out = jnp.zeros((n_block, rows), f32)
        for j in reversed(range(summing)):

            @pl.when((odd == 0) | (ahead[j] != mine))
            def _():
                arriving(it, ahead[j]).wait_recv()

            if row_groups == 1:
                out = out + jnp.dot(
                    joined(it, ahead[j]), turned[ahead[j]], preferred_element_type=f32
                )
        if row_groups > 1:
            for c in range(col_groups):
                out = out + jnp.dot(column(it, c), turned[c], preferred_element_type=f32)
        out = jnp.where(names, out, jnp.zeros((), f32))
        cols = []
        per = k * pix // LANES
        for t in range(tile_rows):
            acc = out[:, t * per * LANES : t * per * LANES + LANES]
            for c in range(1, per):
                at = (t * per + c) * LANES
                acc = acc + out[:, at : at + LANES]
            acc = jnp.sum(acc, axis=0, keepdims=True)
            cols.append(acc + pltpu.roll(acc, pix, 1))
        return jnp.concatenate(
            [jnp.where(low, cols[t], cols[t + 1]) for t in range(0, tile_rows, 2)], axis=1
        )

    def keep_own(it):
        own = (lax.broadcasted_iota(jnp.int32, (8, n_block), 1) - me * tile_rows) == (
            lax.broadcasted_iota(jnp.int32, (8, n_block), 0)
        )
        own = jnp.where(own, 1.0, 0.0).astype(bf16)
        for c in range(col_groups):
            own_buf[it, :, c * piece_cols : (c + 1) * piece_cols] = jnp.dot(
                own, column(it, c), preferred_element_type=f32
            )

    def scatter_sent(it):
        for j in range(summing):

            @pl.when((odd == 0) | (ahead[j] != mine))
            def _():
                scatter_copy(it, j).wait_send()

    def gather_sent(it):
        @pl.when(sums_here)
        def _():
            for h in tile_order:
                gather_copy(it, 0, h).wait_send()
                if h:
                    gather_copy(it, 1, h).wait_send()

    start = measured[...]
    left = both_parts(start)
    columns = lax.broadcasted_iota(jnp.int32, (PACKED_ROWS, width), 1)
    bands = band * (width // BANDS_PER_GROUP_PIX) + columns // BANDS_PER_GROUP_PIX
    for e in range(entries):
        t, j = e // k, e % k
        inside = (bands >= window[t, 0, j]) & (bands < window[t, 1, j])
        inside = jnp.where(inside, 1.0, 0.0).astype(bf16)
        for c in range(col_groups):
            mask_buf[c, e] = inside[:, c * piece_cols : (c + 1) * piece_cols]

    def load(i, c):
        loads[i].wait()
        for e in range(entries):
            inside = mask_buf[c, e]
            for at in range(0, pix, PACKED_ROWS):
                at = pl.ds(at, PACKED_ROWS)
                held[c, e // k, e % k, at, :] = held[c, e // k, e % k, at, :] * inside
        if i == 0:
            pl.semaphore_wait(barrier, jnp.where(sums_here, 2 * n_tile - 1, summing) + n_band - 1)

    def put_rest(c, product):
        for r in range(row_groups):
            rest = slice(n_block + r * piece_rows, n_block + (r + 1) * piece_rows)
            put(2, r * col_groups + c, product[rest])

    scatter_send(0, left, load, lambda p, high, rest: put(0, p, high), put_rest)
    for c in range(col_groups):
        turned[c] = matrix(c).T
    norm_buf[...] = jnp.zeros((8, LANES), f32)

    @pl.when(sums_here)
    def _():
        own = landed_sum(0, 1)
        gradients = [landed_sum(0, 0), own]
        gather_send(0, gradients)
        norm_buf[3:4, :] = sum(lanes_sum(gradient * gradient) for gradient in gradients)
        for slab in range(2):
            grad_buf[slab] = gradients[slab]

    band_mine[1:2, :] = norm_buf[3:4, :]
    band_mine[0:1, :] = forward(0)
    for b in reversed(range(1, n_band)):
        band_copy(b).start()
    for j in range(summing):
        scatter_start(2, j)
    keep_own(0)
    scatter_sent(0)
    gather_sent(0)
    band_whole.wait_recv()
    total = band_mine[...]
    for b in range(1, n_band):
        total = total + band_in[b - 1]
    image = total[0:1, :]

    tail = three_parts((image * image, total[1:2, :]))
    for p in range(summing):
        stage[1, p, lanes] = tail
    scatter_send(
        1,
        both_parts(image),
        lambda i, c: None,
        lambda p, high, rest: put(1, p, high + rest),
        lambda c, product: None,
    )
    norm_buf[4:5, :] = image * image * (1.0 / n_band)
    band_whole.wait_send()
    scatter_sent(2)

    @pl.when(sums_here)
    def _():
        for slab in range(2):
            base_buf[slab] = grad_buf[slab] + landed_sum(2, slab)
        own = landed_sum(1, 1)
        sums = lane_total(own[lanes])
        image_square, gamma = [sum(sums[3 * i + l : 3 * i + l + 1] for l in range(3)) for i in range(2)]
        alpha = gamma / (image_square + RIDGE * gamma)
        kept = [
            base_buf[slab] - (RIDGE * alpha) * grad_buf[slab] for slab in range(2)
        ]
        turned_images = [landed_sum(1, 0)[:lanes], own[:lanes]]
        gradients = [kept[slab] - alpha * turned_images[slab] for slab in range(2)]
        gather_send(1, gradients)
        norm_buf[0:1, :] = sum(lanes_sum(x * x) for x in gradients)
        norm_buf[1:2, :] = sum(lanes_sum(x * grad_buf[slab]) for slab, x in enumerate(gradients))
        norm_buf[2:3, :] = sum(lanes_sum(x * y) for x, y in zip(gradients, turned_images))

    group = LANES // 8
    folded = norm_buf[...]
    for by in (4, 2, 1):
        folded = folded + pltpu.roll(folded, by * group, 1)
    one_of = lax.broadcasted_iota(jnp.int32, (8, LANES), 1) // group == lax.broadcasted_iota(
        jnp.int32, (8, LANES), 0
    )
    folded = jnp.sum(jnp.where(one_of, folded, jnp.zeros((), f32)), axis=0, keepdims=True)
    all_mine[1:2, :] = folded
    all_mine[0:1, :] = forward(1)
    for a, b in everyone:
        all_copy(a, b).start()
    keep_own(1)
    scatter_sent(1)
    gather_sent(1)
    all_whole.wait_recv()
    partial = square = None
    for a in range(n_tile):
        total = all_in[a * n_band - 1] if a else all_mine[...]
        for b in range(1, n_band):
            total = total + all_in[a * n_band + b - 1]
        if a:
            sums, square = sums + total, square + total * total
        else:
            partial, sums, square = total[0:1, :], total, total * total
    sums = jnp.broadcast_to(sums[1:2, :], (8, LANES))
    sums = lane_total(jnp.where(one_of, sums, jnp.zeros((), f32)))
    gamma_next, cross, image_cross, gamma, image_square = [sums[q : q + 1] for q in range(5)]
    alpha = gamma / (image_square + RIDGE * gamma)
    beta = gamma_next / gamma
    square = lane_total(square[0:1, :]) + 2.0 * beta * image_cross + beta * beta * image_square
    direction_square = gamma_next + 2.0 * beta * cross + beta * beta * gamma
    step = gamma_next / (square + RIDGE * direction_square)
    solved_out[...] = (alpha + step * beta) * own_buf[0, 0:tile_rows, :] + step * own_buf[1, 0:tile_rows, :]
    residual_out[...] = start - (alpha + step * beta) * image - step * partial
    all_whole.wait_send()


def finish_kernel(solved, residual, solution_out, residual_out):
    solution_out[...] = solved[...]
    residual_out[...] = residual[...]


def body(calib, support, band_window, measured):
    n_tile, n_band = lax.axis_size("tile"), lax.axis_size("band")
    tile_rows, k, pix, width = calib.shape
    entries = tile_rows * k
    sensor = tile_rows * pix
    n_block = n_tile * tile_rows
    _, _, piece_rows, piece_cols = pieces_of(n_tile, n_block, width)
    summing = centre_of(n_tile)[1]
    f32, bf16 = jnp.float32, jnp.bfloat16
    vmem = pl.BlockSpec(memory_space=pltpu.VMEM)
    dma = pltpu.SemaphoreType.DMA
    lanes = piece_cols // LANES
    piece = (lanes + 1, piece_rows, LANES)
    bare = (lanes, piece_rows, LANES)
    hbm = pl.BlockSpec(memory_space=pl.ANY)
    in_hbm = lambda x: pltpu.with_memory_space_constraint(x, pltpu.HBM)
    in_vmem = lambda x: pltpu.with_memory_space_constraint(x, pltpu.VMEM)
    turned_window = jnp.transpose(band_window, (0, 2, 1))
    held_back = pl.pallas_call(
        functools.partial(kernel, n_tile, n_band),
        out_shape=(pltpu.VMEM((tile_rows, width), f32), pltpu.VMEM((1, sensor), f32)),
        in_specs=[hbm] * 4,
        out_specs=(vmem,) * 2,
        scratch_shapes=[
            pltpu.SMEM((tile_rows, k), jnp.int32),
            pltpu.SMEM((tile_rows, 2, k), jnp.int32),
            pltpu.VMEM((1, sensor), f32),
            pltpu.VMEM((width // piece_cols, tile_rows, k, pix, piece_cols), bf16),
            pltpu.VMEM((width // piece_cols, piece_cols, entries * pix), bf16),
            pltpu.VMEM((3, summing) + piece, bf16),
            pltpu.VMEM((3, 2, n_tile) + piece, bf16),
            pltpu.VMEM((2, summing) + bare, bf16),
            pltpu.VMEM((2,) + bare, bf16),
            pltpu.VMEM((2,) + bare, f32),
            pltpu.VMEM((2,) + bare, f32),
            pltpu.VMEM((8, LANES), f32),
            pltpu.VMEM((2, 8, width), f32),
            pltpu.VMEM((width // piece_cols, entries, PACKED_ROWS, piece_cols), bf16),
            pltpu.VMEM((2, sensor), f32),
            pltpu.VMEM((n_band - 1, 2, sensor), f32),
            pltpu.VMEM((2, sensor), f32),
            pltpu.VMEM((n_band * n_tile - 1, 2, sensor), f32),
            dma((3,)),
            dma((width // piece_cols,)),
            dma((3, summing)),
            dma((3, 2, n_tile)),
            dma((2, n_tile)),
            dma((2, n_tile)),
            dma((2, summing)),
            dma,
            dma,
            dma,
            dma,
        ],
        compiler_params=pltpu.CompilerParams(
            collective_id=0, has_side_effects=True, vmem_limit_bytes=VMEM_BYTES
        ),
    )(in_hbm(calib), in_hbm(support), in_hbm(turned_window), in_hbm(measured.reshape(1, sensor)))
    solved, residual = pl.pallas_call(
        finish_kernel,
        out_shape=(
            jax.ShapeDtypeStruct((tile_rows, width), f32),
            jax.ShapeDtypeStruct((1, sensor), f32),
        ),
        in_specs=[vmem] * 2,
        out_specs=(vmem, vmem),
        compiler_params=pltpu.CompilerParams(vmem_limit_bytes=VMEM_BYTES),
    )(*[in_vmem(x) for x in held_back])
    return solved, residual.reshape(sensor)


def solution(mesh):
    placed = (P("tile", None, None, "band"), P("tile", None), P("tile", None, None), P("tile"))
    return jax.shard_map(
        body, mesh=mesh, in_specs=placed, out_specs=(P("tile", "band"), P("tile")), check_vma=False
    )
```

```python
import functools

import jax
import jax.numpy as jnp
from jax import lax
from jax.experimental import pallas as pl
from jax.experimental.pallas import tpu as pltpu
from jax.sharding import PartitionSpec as P

BANDS_PER_GROUP_PIX = 64
RIDGE = 0.25
LANES = 128
PACKED_ROWS = 16
VMEM_BYTES = 48 << 20
MESH = pl.DeviceIdType.MESH


def centre_of(n_tile):
    summing = n_tile // 2 if n_tile % 4 == 0 else n_tile
    return (n_tile - summing) // 2, summing


def far_first(n_tile):
    first, _ = centre_of(n_tile)

    def hops(h):
        there = first ^ h
        return abs(there // 2 - first // 2) + (there ^ first) % 2

    return sorted(range(n_tile), key=lambda h: (-hops(h), -abs((first ^ h) // 2 - first // 2), -h))


def pieces_of(n_tile, n_block, width):
    summing = centre_of(n_tile)[1]
    col_groups = min(summing, width // LANES)
    row_groups = summing // col_groups
    return col_groups, row_groups, n_block // row_groups, width // col_groups


def kernel(
    n_tile,
    n_band,
    calib,
    support_in,
    window_in,
    measured_in,
    solved_out,
    residual_out,
    support,
    window,
    measured,
    held,
    turned,
    stage,
    landed,
    packed,
    passed,
    grad_buf,
    base_buf,
    norm_buf,
    own_buf,
    mask_buf,
    band_mine,
    band_in,
    all_mine,
    all_in,
    small_sem,
    load_sem,
    rs_send,
    rs_recv,
    ag_send,
    ag_pass,
    ag_recv,
    band_send,
    band_recv,
    all_send,
    all_recv,
):
    tile_rows, k, pix, width = calib.shape
    entries = tile_rows * k
    rows = entries * pix
    n_block = n_tile * tile_rows
    col_groups, row_groups, piece_rows, piece_cols = pieces_of(n_tile, n_block, width)
    me = lax.axis_index("tile")
    band = lax.axis_index("band")
    odd = band % 2
    first, summing = centre_of(n_tile)
    mine = me - first
    sums_here = (odd == 1) & (mine >= 0) & (mine < summing)
    f32, bf16 = jnp.float32, jnp.bfloat16

    small = [
        pltpu.make_async_copy(source, target, small_sem.at[i])
        for i, (source, target) in enumerate(
            ((support_in, support), (window_in, window), (measured_in, measured))
        )
    ]
    for copy in small:
        copy.start()
    side = me // (n_tile // 2)
    across = me % 2
    ahead = []
    for j in range(summing):
        along = (1 - side) * (summing // 2 - 1 - j // 2) + side * (j // 2)
        ahead.append(2 * along + (across if j % 2 else 1 - across))
    pieces = ahead if row_groups == 1 else list(range(col_groups))
    loads = []
    for c in pieces:
        cols = pl.ds(pl.multiple_of(c * piece_cols, LANES), piece_cols)
        copy = pltpu.make_async_copy(calib.at[:, :, :, cols], held.at[c], load_sem.at[c])
        copy.start()
        loads.append(copy)

    def paired(index, n):
        turns = [(1 << b) * (1 - 2 * (index // (1 << b) % 2)) for b in range(n.bit_length() - 1)]
        return [
            sum([turn for b, turn in enumerate(turns) if h >> b & 1], index) for h in range(n)
        ]

    peers, others = paired(me, n_tile), paired(band, n_band)
    tile_order = far_first(n_tile)
    everyone = sorted(
        [(a, b) for a in range(n_tile) for b in range(n_band) if a or b],
        key=lambda s: (-(s[0] // 2 + s[0] % 2 + s[1] // 2), s[1] % 2),
    )
    barrier = pltpu.get_barrier_semaphore()

    def greet(tile, band):
        pl.semaphore_signal(
            barrier, inc=1, device_id={"tile": tile, "band": band}, device_id_type=MESH
        )

    @pl.when(sums_here)
    def _():
        for h in tile_order:
            greet(peers[h], band - 1)
            if h:
                greet(peers[h], band)

    @pl.when(jnp.logical_not(sums_here))
    def _():
        for p in range(summing):
            greet(first + p, band + 1 - odd)

    for b in range(1, n_band):
        greet(me, others[b])

    for copy in small:
        copy.wait()
    lane_entry = lax.broadcasted_iota(jnp.int32, (1, rows), 1) // pix
    sup_row = jnp.zeros((1, rows), jnp.int32)
    for e in range(entries):
        sup_row = jnp.where(lane_entry == e, support[e // k, e % k], sup_row)
    names = jnp.broadcast_to(sup_row, (n_block, rows)) == lax.broadcasted_iota(
        jnp.int32, (n_block, rows), 0
    )

    lane = lax.broadcasted_iota(jnp.int32, (1, LANES), 1)
    low = lane < pix

    def spread(w):
        pieces = []
        for t in range(tile_rows):
            col = t * pix // LANES * LANES
            tilev = w[:, col : col + LANES]
            rolled = pltpu.roll(tilev, pix, 1)
            both = jnp.where(low, tilev, rolled) if t * pix % LANES == 0 else jnp.where(low, rolled, tilev)
            pieces += [both] * (k * pix // LANES)
        return jnp.concatenate(pieces, axis=1)

    def rounded(x):
        return x.astype(bf16).astype(f32)

    def left_side(w):
        wide = jnp.broadcast_to(spread(w), (n_block, rows))
        return jnp.where(names, wide, jnp.zeros((), f32)).astype(bf16)

    def both_parts(w):
        high = rounded(w)
        return jnp.concatenate([left_side(high), left_side(w - high)], axis=0)

    def three_parts(values):
        row = lax.broadcasted_iota(jnp.int32, (piece_rows, LANES), 0)
        parts = jnp.zeros((piece_rows, LANES), f32)
        for i, x in enumerate(values):
            high = rounded(x)
            middle = rounded(x - high)
            for l, part in enumerate((high, middle, x - high - middle)):
                parts = jnp.where(row == 3 * i + l, part, parts)
        return parts.astype(bf16)

    def lane_total(x):
        return jnp.sum(x, axis=1, keepdims=True)

    lanes = piece_cols // LANES
    parts_of = [lanes, lanes + 1, lanes]

    def scatter_copy(it, j):
        some = pl.ds(0, parts_of[it])
        return pltpu.make_async_remote_copy(
            src_ref=stage.at[it, ahead[j], some],
            dst_ref=landed.at[it, odd, me, some],
            send_sem=rs_send.at[it, j],
            recv_sem=rs_recv.at[it, odd, me],
            device_id={"tile": first + ahead[j], "band": band + 1 - odd},
            device_id_type=MESH,
        )

    def landing(it, slab, tile):
        some = pl.ds(0, parts_of[it])
        return pltpu.make_async_remote_copy(
            src_ref=stage.at[it, 0, some],
            dst_ref=landed.at[it, slab, tile, some],
            send_sem=rs_send.at[it, 0],
            recv_sem=rs_recv.at[it, slab, tile],
            device_id={"tile": tile, "band": band - 1},
            device_id_type=MESH,
        )

    def gather_copy(it, slab, h):
        return pltpu.make_async_remote_copy(
            src_ref=packed.at[it, mine] if slab else passed.at[it],
            dst_ref=packed.at[it, mine],
            send_sem=(ag_send if slab else ag_pass).at[it, h],
            recv_sem=ag_recv.at[it, mine],
            device_id={"tile": peers[h], "band": band if slab else band - 1},
            device_id_type=MESH,
        )

    def arriving(it, piece):
        return pltpu.make_async_remote_copy(
            src_ref=packed.at[it, piece],
            dst_ref=packed.at[it, piece],
            send_sem=ag_send.at[it, 0],
            recv_sem=ag_recv.at[it, piece],
            device_id={"tile": first + piece, "band": band + 1 - odd},
            device_id_type=MESH,
        )

    def band_copy(b):
        return pltpu.make_async_remote_copy(
            src_ref=band_mine,
            dst_ref=band_in.at[b - 1],
            send_sem=band_send,
            recv_sem=band_recv,
            device_id={"tile": me, "band": others[b]},
            device_id_type=MESH,
        )

    def all_copy(a, b):
        return pltpu.make_async_remote_copy(
            src_ref=all_mine,
            dst_ref=all_in.at[a * n_band + b - 1],
            send_sem=all_send,
            recv_sem=all_recv,
            device_id={"tile": peers[a], "band": others[b]},
            device_id_type=MESH,
        )

    band_whole = pltpu.make_async_remote_copy(
        src_ref=band_in,
        dst_ref=band_in,
        send_sem=band_send,
        recv_sem=band_recv,
        device_id={"tile": me, "band": others[1]},
        device_id_type=MESH,
    )
    all_whole = pltpu.make_async_remote_copy(
        src_ref=all_in,
        dst_ref=all_in,
        send_sem=all_send,
        recv_sem=all_recv,
        device_id={"tile": me, "band": others[1]},
        device_id_type=MESH,
    )

    def scatter_start(it, j):
        @pl.when((odd == 0) | (ahead[j] != mine))
        def _():
            scatter_copy(it, j).start()

    def put(it, p, product):
        for l in range(lanes):
            stage[it, p, l] = product[:, l * LANES : (l + 1) * LANES].astype(bf16)

    def matrix(c):
        return held[c].reshape(rows, piece_cols)

    def scatter_send(it, left, ready, finish, later):
        for i, c in enumerate(pieces):
            ready(i, c)
            product = jnp.dot(left, matrix(c), preferred_element_type=f32)
            for r in range(row_groups):
                at = slice(r * piece_rows, (r + 1) * piece_rows)
                rest = slice(n_block + r * piece_rows, n_block + (r + 1) * piece_rows)
                finish(r * col_groups + c, product[at], product[rest])
            if row_groups == 1:
                scatter_start(it, i)
            later(c, product)
        if row_groups > 1:
            for j in range(summing):
                scatter_start(it, j)

    def lanes_sum(x):
        total = x[0]
        for l in range(1, lanes):
            total = total + x[l]
        return jnp.sum(total, axis=0, keepdims=True)

    def landed_sum(it, slab):
        some = pl.ds(0, parts_of[it])
        total = (
            stage[it, mine, some].astype(f32)
            if slab
            else jnp.zeros((parts_of[it], piece_rows, LANES), f32)
        )
        for h in reversed(tile_order):
            if h or not slab:
                landing(it, slab, peers[h]).wait_recv()
                total = total + landed[it, slab, peers[h], some].astype(f32)
        return total

    gather_order = sorted(
        [(h, slab) for slab in range(2) for h in range(n_tile) if h or not slab],
        key=lambda s: (s[1], tile_order.index(s[0])),
    )

    def gather_send(it, vectors):
        for l in range(lanes):
            passed[it, l] = vectors[0][l].astype(bf16)
            packed[it, mine, l] = vectors[1][l].astype(bf16)
        for h, slab in gather_order:
            gather_copy(it, slab, h).start()

    def joined(it, piece):
        return jnp.concatenate([packed[it, piece, l] for l in range(lanes)], axis=1)

    def column(it, c):
        return jnp.concatenate(
            [joined(it, r * col_groups + c) for r in range(row_groups)], axis=0
        )

    def forward(it):
        out = jnp.zeros((n_block, rows), f32)
        for j in reversed(range(summing)):

            @pl.when((odd == 0) | (ahead[j] != mine))
            def _():
                arriving(it, ahead[j]).wait_recv()

            if row_groups == 1:
                out = out + jnp.dot(
                    joined(it, ahead[j]), turned[ahead[j]], preferred_element_type=f32
                )
        if row_groups > 1:
            for c in range(col_groups):
                out = out + jnp.dot(column(it, c), turned[c], preferred_element_type=f32)
        out = jnp.where(names, out, jnp.zeros((), f32))
        cols = []
        per = k * pix // LANES
        for t in range(tile_rows):
            acc = out[:, t * per * LANES : t * per * LANES + LANES]
            for c in range(1, per):
                at = (t * per + c) * LANES
                acc = acc + out[:, at : at + LANES]
            acc = jnp.sum(acc, axis=0, keepdims=True)
            cols.append(acc + pltpu.roll(acc, pix, 1))
        return jnp.concatenate(
            [jnp.where(low, cols[t], cols[t + 1]) for t in range(0, tile_rows, 2)], axis=1
        )

    def keep_own(it):
        own = (lax.broadcasted_iota(jnp.int32, (8, n_block), 1) - me * tile_rows) == (
            lax.broadcasted_iota(jnp.int32, (8, n_block), 0)
        )
        own = jnp.where(own, 1.0, 0.0).astype(bf16)
        for c in range(col_groups):
            own_buf[it, :, c * piece_cols : (c + 1) * piece_cols] = jnp.dot(
                own, column(it, c), preferred_element_type=f32
            )

    def scatter_sent(it):
        for j in range(summing):

            @pl.when((odd == 0) | (ahead[j] != mine))
            def _():
                scatter_copy(it, j).wait_send()

    def gather_sent(it):
        @pl.when(sums_here)
        def _():
            for h in tile_order:
                gather_copy(it, 0, h).wait_send()
                if h:
                    gather_copy(it, 1, h).wait_send()

    start = measured[...]
    left = both_parts(start)
    columns = lax.broadcasted_iota(jnp.int32, (PACKED_ROWS, width), 1)
    bands = band * (width // BANDS_PER_GROUP_PIX) + columns // BANDS_PER_GROUP_PIX
    for e in range(entries):
        t, j = e // k, e % k
        inside = (bands >= window[t, 0, j]) & (bands < window[t, 1, j])
        inside = jnp.where(inside, 1.0, 0.0).astype(bf16)
        for c in range(col_groups):
            mask_buf[c, e] = inside[:, c * piece_cols : (c + 1) * piece_cols]

    def load(i, c):
        loads[i].wait()
        for e in range(entries):
            inside = mask_buf[c, e]
            for at in range(0, pix, PACKED_ROWS):
                at = pl.ds(at, PACKED_ROWS)
                held[c, e // k, e % k, at, :] = held[c, e // k, e % k, at, :] * inside
        if i == 0:
            pl.semaphore_wait(barrier, jnp.where(sums_here, 2 * n_tile - 1, summing) + n_band - 1)

    def put_rest(c, product):
        for r in range(row_groups):
            rest = slice(n_block + r * piece_rows, n_block + (r + 1) * piece_rows)
            put(2, r * col_groups + c, product[rest])

    scatter_send(0, left, load, lambda p, high, rest: put(0, p, high), put_rest)
    for c in range(col_groups):
        turned[c] = matrix(c).T
    norm_buf[...] = jnp.zeros((8, LANES), f32)

    @pl.when(sums_here)
    def _():
        own = landed_sum(0, 1)
        gradients = [landed_sum(0, 0), own]
        gather_send(0, gradients)
        norm_buf[3:4, :] = sum(lanes_sum(gradient * gradient) for gradient in gradients)
        for slab in range(2):
            grad_buf[slab] = gradients[slab]

    band_mine[1:2, :] = norm_buf[3:4, :]
    band_mine[0:1, :] = forward(0)
    for b in reversed(range(1, n_band)):
        band_copy(b).start()
    for j in range(summing):
        scatter_start(2, j)
    keep_own(0)
    scatter_sent(0)
    gather_sent(0)
    band_whole.wait_recv()
    total = band_mine[...]
    for b in range(1, n_band):
        total = total + band_in[b - 1]
    image = total[0:1, :]

    tail = three_parts((image * image, total[1:2, :]))
    for p in range(summing):
        stage[1, p, lanes] = tail
    scatter_send(
        1,
        both_parts(image),
        lambda i, c: None,
        lambda p, high, rest: put(1, p, high + rest),
        lambda c, product: None,
    )
    norm_buf[4:5, :] = image * image * (1.0 / n_band)
    band_whole.wait_send()
    scatter_sent(2)

    @pl.when(sums_here)
    def _():
        for slab in range(2):
            base_buf[slab] = grad_buf[slab] + landed_sum(2, slab)
        own = landed_sum(1, 1)
        sums = lane_total(own[lanes])
        image_square, gamma = [sum(sums[3 * i + l : 3 * i + l + 1] for l in range(3)) for i in range(2)]
        alpha = gamma / (image_square + RIDGE * gamma)
        kept = [
            base_buf[slab] - (RIDGE * alpha) * grad_buf[slab] for slab in range(2)
        ]
        turned_images = [landed_sum(1, 0)[:lanes], own[:lanes]]
        gradients = [kept[slab] - alpha * turned_images[slab] for slab in range(2)]
        gather_send(1, gradients)
        norm_buf[0:1, :] = sum(lanes_sum(x * x) for x in gradients)
        norm_buf[1:2, :] = sum(lanes_sum(x * grad_buf[slab]) for slab, x in enumerate(gradients))
        norm_buf[2:3, :] = sum(lanes_sum(x * y) for x, y in zip(gradients, turned_images))

    group = LANES // 8
    folded = norm_buf[...]
    for by in (4, 2, 1):
        folded = folded + pltpu.roll(folded, by * group, 1)
    one_of = lax.broadcasted_iota(jnp.int32, (8, LANES), 1) // group == lax.broadcasted_iota(
        jnp.int32, (8, LANES), 0
    )
    folded = jnp.sum(jnp.where(one_of, folded, jnp.zeros((), f32)), axis=0, keepdims=True)
    all_mine[1:2, :] = folded
    all_mine[0:1, :] = forward(1)
    for a, b in everyone:
        all_copy(a, b).start()
    keep_own(1)
    scatter_sent(1)
    gather_sent(1)
    all_whole.wait_recv()
    partial = square = None
    for a in range(n_tile):
        total = all_in[a * n_band - 1] if a else all_mine[...]
        for b in range(1, n_band):
            total = total + all_in[a * n_band + b - 1]
        if a:
            sums, square = sums + total, square + total * total
        else:
            partial, sums, square = total[0:1, :], total, total * total
    sums = jnp.broadcast_to(sums[1:2, :], (8, LANES))
    sums = lane_total(jnp.where(one_of, sums, jnp.zeros((), f32)))
    gamma_next, cross, image_cross, gamma, image_square = [sums[q : q + 1] for q in range(5)]
    alpha = gamma / (image_square + RIDGE * gamma)
    beta = gamma_next / gamma
    square = lane_total(square[0:1, :]) + 2.0 * beta * image_cross + beta * beta * image_square
    direction_square = gamma_next + 2.0 * beta * cross + beta * beta * gamma
    step = gamma_next / (square + RIDGE * direction_square)
    solved_out[...] = (alpha + step * beta) * own_buf[0, 0:tile_rows, :] + step * own_buf[1, 0:tile_rows, :]
    residual_out[...] = start - (alpha + step * beta) * image - step * partial
    all_whole.wait_send()


def finish_kernel(solved, residual, solution_out, residual_out):
    solution_out[...] = solved[...]
    residual_out[...] = residual[...]


def body(calib, support, band_window, measured):
    n_tile, n_band = lax.axis_size("tile"), lax.axis_size("band")
    tile_rows, k, pix, width = calib.shape
    entries = tile_rows * k
    sensor = tile_rows * pix
    n_block = n_tile * tile_rows
    _, _, piece_rows, piece_cols = pieces_of(n_tile, n_block, width)
    summing = centre_of(n_tile)[1]
    f32, bf16 = jnp.float32, jnp.bfloat16
    vmem = pl.BlockSpec(memory_space=pltpu.VMEM)
    dma = pltpu.SemaphoreType.DMA
    lanes = piece_cols // LANES
    piece = (lanes + 1, piece_rows, LANES)
    bare = (lanes, piece_rows, LANES)
    hbm = pl.BlockSpec(memory_space=pl.ANY)
    in_hbm = lambda x: pltpu.with_memory_space_constraint(x, pltpu.HBM)
    in_vmem = lambda x: pltpu.with_memory_space_constraint(x, pltpu.VMEM)
    turned_window = jnp.transpose(band_window, (0, 2, 1))
    held_back = pl.pallas_call(
        functools.partial(kernel, n_tile, n_band),
        out_shape=(pltpu.VMEM((tile_rows, width), f32), pltpu.VMEM((1, sensor), f32)),
        in_specs=[hbm] * 4,
        out_specs=(vmem,) * 2,
        scratch_shapes=[
            pltpu.SMEM((tile_rows, k), jnp.int32),
            pltpu.SMEM((tile_rows, 2, k), jnp.int32),
            pltpu.VMEM((1, sensor), f32),
            pltpu.VMEM((width // piece_cols, tile_rows, k, pix, piece_cols), bf16),
            pltpu.VMEM((width // piece_cols, piece_cols, entries * pix), bf16),
            pltpu.VMEM((3, summing) + piece, bf16),
            pltpu.VMEM((3, 2, n_tile) + piece, bf16),
            pltpu.VMEM((2, summing) + bare, bf16),
            pltpu.VMEM((2,) + bare, bf16),
            pltpu.VMEM((2,) + bare, f32),
            pltpu.VMEM((2,) + bare, f32),
            pltpu.VMEM((8, LANES), f32),
            pltpu.VMEM((2, 8, width), f32),
            pltpu.VMEM((width // piece_cols, entries, PACKED_ROWS, piece_cols), bf16),
            pltpu.VMEM((2, sensor), f32),
            pltpu.VMEM((n_band - 1, 2, sensor), f32),
            pltpu.VMEM((2, sensor), f32),
            pltpu.VMEM((n_band * n_tile - 1, 2, sensor), f32),
            dma((3,)),
            dma((width // piece_cols,)),
            dma((3, summing)),
            dma((3, 2, n_tile)),
            dma((2, n_tile)),
            dma((2, n_tile)),
            dma((2, summing)),
            dma,
            dma,
            dma,
            dma,
        ],
        compiler_params=pltpu.CompilerParams(
            collective_id=0, has_side_effects=True, vmem_limit_bytes=VMEM_BYTES
        ),
    )(in_hbm(calib), in_hbm(support), in_hbm(turned_window), in_hbm(measured.reshape(1, sensor)))
    solved, residual = pl.pallas_call(
        finish_kernel,
        out_shape=(
            jax.ShapeDtypeStruct((tile_rows, width), f32),
            jax.ShapeDtypeStruct((1, sensor), f32),
        ),
        in_specs=[vmem] * 2,
        out_specs=(vmem, vmem),
        compiler_params=pltpu.CompilerParams(vmem_limit_bytes=VMEM_BYTES),
    )(*[in_vmem(x) for x in held_back])
    return solved, residual.reshape(sensor)


def solution(mesh):
    placed = (P("tile", None, None, "band"), P("tile", None), P("tile", None, None), P("tile"))
    return jax.shard_map(
        body, mesh=mesh, in_specs=placed, out_specs=(P("tile", "band"), P("tile")), check_vma=False
    )
```

```python
import functools

import jax
import jax.numpy as jnp
from jax import lax
from jax.experimental import pallas as pl
from jax.experimental.pallas import tpu as pltpu
from jax.sharding import PartitionSpec as P

BANDS_PER_GROUP_PIX = 64
RIDGE = 0.25
LANES = 128
PACKED_ROWS = 16
VMEM_BYTES = 48 << 20
MESH = pl.DeviceIdType.MESH


def centre_of(n_tile):
    summing = n_tile // 2 if n_tile % 4 == 0 else n_tile
    return (n_tile - summing) // 2, summing


def far_first(n_tile):
    first, _ = centre_of(n_tile)

    def hops(h):
        there = first ^ h
        return abs(there // 2 - first // 2) + (there ^ first) % 2

    return sorted(range(n_tile), key=lambda h: (-hops(h), -abs((first ^ h) // 2 - first // 2), -h))


def pieces_of(n_tile, n_block, width):
    summing = centre_of(n_tile)[1]
    col_groups = min(summing, width // LANES)
    row_groups = summing // col_groups
    return col_groups, row_groups, n_block // row_groups, width // col_groups


def kernel(
    n_tile,
    n_band,
    calib,
    support_in,
    window_in,
    measured_in,
    solved_out,
    residual_out,
    support,
    window,
    measured,
    held,
    turned,
    stage,
    landed,
    packed,
    passed,
    grad_buf,
    base_buf,
    norm_buf,
    own_buf,
    mask_buf,
    band_mine,
    band_in,
    all_mine,
    all_in,
    small_sem,
    load_sem,
    rs_send,
    rs_recv,
    ag_send,
    ag_pass,
    ag_recv,
    band_send,
    band_recv,
    all_send,
    all_recv,
):
    tile_rows, k, pix, width = calib.shape
    entries = tile_rows * k
    rows = entries * pix
    n_block = n_tile * tile_rows
    col_groups, row_groups, piece_rows, piece_cols = pieces_of(n_tile, n_block, width)
    me = lax.axis_index("tile")
    band = lax.axis_index("band")
    odd = band % 2
    first, summing = centre_of(n_tile)
    mine = me - first
    sums_here = (odd == 1) & (mine >= 0) & (mine < summing)
    f32, bf16 = jnp.float32, jnp.bfloat16

    small = [
        pltpu.make_async_copy(source, target, small_sem.at[i])
        for i, (source, target) in enumerate(
            ((support_in, support), (window_in, window), (measured_in, measured))
        )
    ]
    for copy in small:
        copy.start()
    side = me // (n_tile // 2)
    across = me % 2
    ahead = []
    for j in range(summing):
        along = (1 - side) * (summing // 2 - 1 - j // 2) + side * (j // 2)
        ahead.append(2 * along + (across if j % 2 else 1 - across))
    pieces = ahead if row_groups == 1 else list(range(col_groups))
    loads = []
    for c in pieces:
        cols = pl.ds(pl.multiple_of(c * piece_cols, LANES), piece_cols)
        copy = pltpu.make_async_copy(calib.at[:, :, :, cols], held.at[c], load_sem.at[c])
        copy.start()
        loads.append(copy)

    def paired(index, n):
        turns = [(1 << b) * (1 - 2 * (index // (1 << b) % 2)) for b in range(n.bit_length() - 1)]
        return [
            sum([turn for b, turn in enumerate(turns) if h >> b & 1], index) for h in range(n)
        ]

    peers, others = paired(me, n_tile), paired(band, n_band)
    tile_order = far_first(n_tile)
    everyone = sorted(
        [(a, b) for a in range(n_tile) for b in range(n_band) if a or b],
        key=lambda s: (-(s[0] // 2 + s[0] % 2 + s[1] // 2), s[1] % 2),
    )
    barrier = pltpu.get_barrier_semaphore()

    def greet(tile, band):
        pl.semaphore_signal(
            barrier, inc=1, device_id={"tile": tile, "band": band}, device_id_type=MESH
        )

    @pl.when(sums_here)
    def _():
        for h in tile_order:
            greet(peers[h], band - 1)
            if h:
                greet(peers[h], band)

    @pl.when(jnp.logical_not(sums_here))
    def _():
        for p in range(summing):
            greet(first + p, band + 1 - odd)

    for b in range(1, n_band):
        greet(me, others[b])

    for copy in small:
        copy.wait()
    lane_entry = lax.broadcasted_iota(jnp.int32, (1, rows), 1) // pix
    sup_row = jnp.zeros((1, rows), jnp.int32)
    for e in range(entries):
        sup_row = jnp.where(lane_entry == e, support[e // k, e % k], sup_row)
    names = jnp.broadcast_to(sup_row, (n_block, rows)) == lax.broadcasted_iota(
        jnp.int32, (n_block, rows), 0
    )

    lane = lax.broadcasted_iota(jnp.int32, (1, LANES), 1)
    low = lane < pix

    def spread(w):
        pieces = []
        for t in range(tile_rows):
            col = t * pix // LANES * LANES
            tilev = w[:, col : col + LANES]
            rolled = pltpu.roll(tilev, pix, 1)
            both = jnp.where(low, tilev, rolled) if t * pix % LANES == 0 else jnp.where(low, rolled, tilev)
            pieces += [both] * (k * pix // LANES)
        return jnp.concatenate(pieces, axis=1)

    def rounded(x):
        return x.astype(bf16).astype(f32)

    def left_side(w):
        wide = jnp.broadcast_to(spread(w), (n_block, rows))
        return jnp.where(names, wide, jnp.zeros((), f32)).astype(bf16)

    def both_parts(w):
        high = rounded(w)
        return jnp.concatenate([left_side(high), left_side(w - high)], axis=0)

    def three_parts(values):
        row = lax.broadcasted_iota(jnp.int32, (piece_rows, LANES), 0)
        parts = jnp.zeros((piece_rows, LANES), f32)
        for i, x in enumerate(values):
            high = rounded(x)
            middle = rounded(x - high)
            for l, part in enumerate((high, middle, x - high - middle)):
                parts = jnp.where(row == 3 * i + l, part, parts)
        return parts.astype(bf16)

    def lane_total(x):
        return jnp.sum(x, axis=1, keepdims=True)

    lanes = piece_cols // LANES

    def part(it, slab):
        return pl.ds(0, lanes + 1 if it == 1 and slab else lanes)

    def scatter_copy(it, j, slab):
        some = part(it, slab)
        return pltpu.make_async_remote_copy(
            src_ref=stage.at[it, ahead[j], some],
            dst_ref=landed.at[it, slab, me, some],
            send_sem=rs_send.at[it, j],
            recv_sem=rs_recv.at[it, slab, me],
            device_id={"tile": first + ahead[j], "band": band + 1 - slab},
            device_id_type=MESH,
        )

    def landing(it, slab, tile):
        some = part(it, slab)
        return pltpu.make_async_remote_copy(
            src_ref=stage.at[it, 0, some],
            dst_ref=landed.at[it, slab, tile, some],
            send_sem=rs_send.at[it, 0],
            recv_sem=rs_recv.at[it, slab, tile],
            device_id={"tile": tile, "band": band - 1},
            device_id_type=MESH,
        )

    def gather_copy(it, slab, h):
        return pltpu.make_async_remote_copy(
            src_ref=packed.at[it, mine] if slab else passed.at[it],
            dst_ref=packed.at[it, mine],
            send_sem=(ag_send if slab else ag_pass).at[it, h],
            recv_sem=ag_recv.at[it, mine],
            device_id={"tile": peers[h], "band": band if slab else band - 1},
            device_id_type=MESH,
        )

    def arriving(it, piece):
        return pltpu.make_async_remote_copy(
            src_ref=packed.at[it, piece],
            dst_ref=packed.at[it, piece],
            send_sem=ag_send.at[it, 0],
            recv_sem=ag_recv.at[it, piece],
            device_id={"tile": first + piece, "band": band + 1 - odd},
            device_id_type=MESH,
        )

    def band_copy(b):
        return pltpu.make_async_remote_copy(
            src_ref=band_mine,
            dst_ref=band_in.at[b - 1],
            send_sem=band_send,
            recv_sem=band_recv,
            device_id={"tile": me, "band": others[b]},
            device_id_type=MESH,
        )

    def all_copy(a, b):
        return pltpu.make_async_remote_copy(
            src_ref=all_mine,
            dst_ref=all_in.at[a * n_band + b - 1],
            send_sem=all_send,
            recv_sem=all_recv,
            device_id={"tile": peers[a], "band": others[b]},
            device_id_type=MESH,
        )

    band_whole = pltpu.make_async_remote_copy(
        src_ref=band_in,
        dst_ref=band_in,
        send_sem=band_send,
        recv_sem=band_recv,
        device_id={"tile": me, "band": others[1]},
        device_id_type=MESH,
    )
    all_whole = pltpu.make_async_remote_copy(
        src_ref=all_in,
        dst_ref=all_in,
        send_sem=all_send,
        recv_sem=all_recv,
        device_id={"tile": me, "band": others[1]},
        device_id_type=MESH,
    )

    def each_scatter(it, j, act):
        @pl.when(odd == 0)
        def _():
            act(scatter_copy(it, j, 0))

        @pl.when((odd == 1) & (ahead[j] != mine))
        def _():
            act(scatter_copy(it, j, 1))

    def scatter_start(it, j):
        each_scatter(it, j, lambda copy: copy.start())

    def put(it, p, product):
        for l in range(lanes):
            stage[it, p, l] = product[:, l * LANES : (l + 1) * LANES].astype(bf16)

    def matrix(c):
        return held[c].reshape(rows, piece_cols)

    def windowed(c):
        return jnp.concatenate(
            [
                held[c, e // k, e % k, at : at + PACKED_ROWS, :] * mask_buf[c, e]
                for e in range(entries)
                for at in range(0, pix, PACKED_ROWS)
            ],
            axis=0,
        )

    def scatter_send(it, left, ready, source, finish, later):
        for i, c in enumerate(pieces):
            ready(i, c)
            product = jnp.dot(left, source(c), preferred_element_type=f32)
            for r in range(row_groups):
                at = slice(r * piece_rows, (r + 1) * piece_rows)
                rest = slice(n_block + r * piece_rows, n_block + (r + 1) * piece_rows)
                finish(r * col_groups + c, product[at], product[rest])
            if row_groups == 1:
                scatter_start(it, i)
            later(c, product)
        if row_groups > 1:
            for j in range(summing):
                scatter_start(it, j)

    def lanes_sum(x):
        total = x[0]
        for l in range(1, lanes):
            total = total + x[l]
        return jnp.sum(total, axis=0, keepdims=True)

    def landed_sum(it, slab):
        some = part(it, slab)
        total = (
            stage[it, mine, some].astype(f32)
            if slab
            else jnp.zeros((lanes, piece_rows, LANES), f32)
        )
        for h in reversed(tile_order):
            if h or not slab:
                landing(it, slab, peers[h]).wait_recv()
                total = total + landed[it, slab, peers[h], some].astype(f32)
        return total

    gather_order = sorted(
        [(h, slab) for slab in range(2) for h in range(n_tile) if h or not slab],
        key=lambda s: (s[1], tile_order.index(s[0])),
    )

    def gather_send(it, vectors):
        for l in range(lanes):
            passed[it, l] = vectors[0][l].astype(bf16)
            packed[it, mine, l] = vectors[1][l].astype(bf16)
        for h, slab in gather_order:
            gather_copy(it, slab, h).start()

    def joined(it, piece):
        return jnp.concatenate([packed[it, piece, l] for l in range(lanes)], axis=1)

    def column(it, c):
        return jnp.concatenate(
            [joined(it, r * col_groups + c) for r in range(row_groups)], axis=0
        )

    def forward(it):
        out = jnp.zeros((n_block, rows), f32)
        for j in reversed(range(summing)):

            @pl.when((odd == 0) | (ahead[j] != mine))
            def _():
                arriving(it, ahead[j]).wait_recv()

            if row_groups == 1:
                out = out + jnp.dot(
                    joined(it, ahead[j]), turned[ahead[j]], preferred_element_type=f32
                )
        if row_groups > 1:
            for c in range(col_groups):
                out = out + jnp.dot(column(it, c), turned[c], preferred_element_type=f32)
        out = jnp.where(names, out, jnp.zeros((), f32))
        cols = []
        per = k * pix // LANES
        for t in range(tile_rows):
            acc = out[:, t * per * LANES : t * per * LANES + LANES]
            for c in range(1, per):
                at = (t * per + c) * LANES
                acc = acc + out[:, at : at + LANES]
            acc = jnp.sum(acc, axis=0, keepdims=True)
            cols.append(acc + pltpu.roll(acc, pix, 1))
        return jnp.concatenate(
            [jnp.where(low, cols[t], cols[t + 1]) for t in range(0, tile_rows, 2)], axis=1
        )

    def keep_own(it):
        own = (lax.broadcasted_iota(jnp.int32, (8, n_block), 1) - me * tile_rows) == (
            lax.broadcasted_iota(jnp.int32, (8, n_block), 0)
        )
        own = jnp.where(own, 1.0, 0.0).astype(bf16)
        for c in range(col_groups):
            own_buf[it, :, c * piece_cols : (c + 1) * piece_cols] = jnp.dot(
                own, column(it, c), preferred_element_type=f32
            )

    def scatter_sent(it):
        for j in range(summing):
            each_scatter(it, j, lambda copy: copy.wait_send())

    def gather_sent(it):
        @pl.when(sums_here)
        def _():
            for h in tile_order:
                gather_copy(it, 0, h).wait_send()
                if h:
                    gather_copy(it, 1, h).wait_send()

    start = measured[...]
    left = both_parts(start)
    columns = lax.broadcasted_iota(jnp.int32, (PACKED_ROWS, width), 1)
    bands = band * (width // BANDS_PER_GROUP_PIX) + columns // BANDS_PER_GROUP_PIX
    for e in range(entries):
        t, j = e // k, e % k
        inside = (bands >= window[t, 0, j]) & (bands < window[t, 1, j])
        inside = jnp.where(inside, 1.0, 0.0).astype(bf16)
        for c in range(col_groups):
            mask_buf[c, e] = inside[:, c * piece_cols : (c + 1) * piece_cols]

    def load(i, c):
        loads[i].wait()
        if i == 0:
            pl.semaphore_wait(barrier, jnp.where(sums_here, 2 * n_tile - 1, summing) + n_band - 1)

    def put_rest(c, product):
        for r in range(row_groups):
            rest = slice(n_block + r * piece_rows, n_block + (r + 1) * piece_rows)
            put(2, r * col_groups + c, product[rest])

    scatter_send(0, left, load, windowed, lambda p, high, rest: put(0, p, high), put_rest)
    for c in range(col_groups):
        for e in range(entries):
            for at in range(0, pix, PACKED_ROWS):
                at = pl.ds(at, PACKED_ROWS)
                held[c, e // k, e % k, at, :] = held[c, e // k, e % k, at, :] * mask_buf[c, e]
        turned[c] = matrix(c).T
    norm_buf[...] = jnp.zeros((8, LANES), f32)

    @pl.when(sums_here)
    def _():
        own = landed_sum(0, 1)
        gradients = [landed_sum(0, 0), own]
        gather_send(0, gradients)
        norm_buf[3:4, :] = sum(lanes_sum(gradient * gradient) for gradient in gradients)
        for slab in range(2):
            grad_buf[slab] = gradients[slab]

    band_mine[1:2, :] = norm_buf[3:4, :]
    band_mine[0:1, :] = forward(0)
    for b in reversed(range(1, n_band)):
        band_copy(b).start()
    for j in range(summing):
        scatter_start(2, j)
    keep_own(0)
    scatter_sent(0)
    gather_sent(0)
    band_whole.wait_recv()
    total = band_mine[...]
    for b in range(1, n_band):
        total = total + band_in[b - 1]
    image = total[0:1, :]

    tail = three_parts((image * image, total[1:2, :]))
    for p in range(summing):
        stage[1, p, lanes] = tail
    scatter_send(
        1,
        both_parts(image),
        lambda i, c: None,
        matrix,
        lambda p, high, rest: put(1, p, high + rest),
        lambda c, product: None,
    )
    norm_buf[4:5, :] = image * image * (1.0 / n_band)
    band_whole.wait_send()
    scatter_sent(2)

    @pl.when(sums_here)
    def _():
        for slab in range(2):
            base_buf[slab] = grad_buf[slab] + landed_sum(2, slab)
        own = landed_sum(1, 1)
        sums = lane_total(own[lanes])
        image_square, gamma = [sum(sums[3 * i + l : 3 * i + l + 1] for l in range(3)) for i in range(2)]
        alpha = gamma / (image_square + RIDGE * gamma)
        kept = [
            base_buf[slab] - (RIDGE * alpha) * grad_buf[slab] for slab in range(2)
        ]
        turned_images = [landed_sum(1, 0), own[:lanes]]
        gradients = [kept[slab] - alpha * turned_images[slab] for slab in range(2)]
        gather_send(1, gradients)
        norm_buf[0:1, :] = sum(lanes_sum(x * x) for x in gradients)
        norm_buf[1:2, :] = sum(lanes_sum(x * grad_buf[slab]) for slab, x in enumerate(gradients))
        norm_buf[2:3, :] = sum(lanes_sum(x * y) for x, y in zip(gradients, turned_images))

    group = LANES // 8
    folded = norm_buf[...]
    for by in (4, 2, 1):
        folded = folded + pltpu.roll(folded, by * group, 1)
    one_of = lax.broadcasted_iota(jnp.int32, (8, LANES), 1) // group == lax.broadcasted_iota(
        jnp.int32, (8, LANES), 0
    )
    folded = jnp.sum(jnp.where(one_of, folded, jnp.zeros((), f32)), axis=0, keepdims=True)
    all_mine[1:2, :] = folded
    all_mine[0:1, :] = forward(1)
    for a, b in everyone:
        all_copy(a, b).start()
    keep_own(1)
    scatter_sent(1)
    gather_sent(1)
    all_whole.wait_recv()
    partial = square = None
    for a in range(n_tile):
        total = all_in[a * n_band - 1] if a else all_mine[...]
        for b in range(1, n_band):
            total = total + all_in[a * n_band + b - 1]
        if a:
            sums, square = sums + total, square + total * total
        else:
            partial, sums, square = total[0:1, :], total, total * total
    sums = jnp.broadcast_to(sums[1:2, :], (8, LANES))
    sums = lane_total(jnp.where(one_of, sums, jnp.zeros((), f32)))
    gamma_next, cross, image_cross, gamma, image_square = [sums[q : q + 1] for q in range(5)]
    alpha = gamma / (image_square + RIDGE * gamma)
    beta = gamma_next / gamma
    square = lane_total(square[0:1, :]) + 2.0 * beta * image_cross + beta * beta * image_square
    direction_square = gamma_next + 2.0 * beta * cross + beta * beta * gamma
    step = gamma_next / (square + RIDGE * direction_square)
    solved_out[...] = (alpha + step * beta) * own_buf[0, 0:tile_rows, :] + step * own_buf[1, 0:tile_rows, :]
    residual_out[...] = start - (alpha + step * beta) * image - step * partial
    all_whole.wait_send()


def finish_kernel(solved, residual, solution_out, residual_out):
    solution_out[...] = solved[...]
    residual_out[...] = residual[...]


def body(calib, support, band_window, measured):
    n_tile, n_band = lax.axis_size("tile"), lax.axis_size("band")
    tile_rows, k, pix, width = calib.shape
    entries = tile_rows * k
    sensor = tile_rows * pix
    n_block = n_tile * tile_rows
    _, _, piece_rows, piece_cols = pieces_of(n_tile, n_block, width)
    summing = centre_of(n_tile)[1]
    f32, bf16 = jnp.float32, jnp.bfloat16
    vmem = pl.BlockSpec(memory_space=pltpu.VMEM)
    dma = pltpu.SemaphoreType.DMA
    lanes = piece_cols // LANES
    piece = (lanes + 1, piece_rows, LANES)
    bare = (lanes, piece_rows, LANES)
    hbm = pl.BlockSpec(memory_space=pl.ANY)
    in_hbm = lambda x: pltpu.with_memory_space_constraint(x, pltpu.HBM)
    in_vmem = lambda x: pltpu.with_memory_space_constraint(x, pltpu.VMEM)
    turned_window = jnp.transpose(band_window, (0, 2, 1))
    held_back = pl.pallas_call(
        functools.partial(kernel, n_tile, n_band),
        out_shape=(pltpu.VMEM((tile_rows, width), f32), pltpu.VMEM((1, sensor), f32)),
        in_specs=[hbm] * 4,
        out_specs=(vmem,) * 2,
        scratch_shapes=[
            pltpu.SMEM((tile_rows, k), jnp.int32),
            pltpu.SMEM((tile_rows, 2, k), jnp.int32),
            pltpu.VMEM((1, sensor), f32),
            pltpu.VMEM((width // piece_cols, tile_rows, k, pix, piece_cols), bf16),
            pltpu.VMEM((width // piece_cols, piece_cols, entries * pix), bf16),
            pltpu.VMEM((3, summing) + piece, bf16),
            pltpu.VMEM((3, 2, n_tile) + piece, bf16),
            pltpu.VMEM((2, summing) + bare, bf16),
            pltpu.VMEM((2,) + bare, bf16),
            pltpu.VMEM((2,) + bare, f32),
            pltpu.VMEM((2,) + bare, f32),
            pltpu.VMEM((8, LANES), f32),
            pltpu.VMEM((2, 8, width), f32),
            pltpu.VMEM((width // piece_cols, entries, PACKED_ROWS, piece_cols), bf16),
            pltpu.VMEM((2, sensor), f32),
            pltpu.VMEM((n_band - 1, 2, sensor), f32),
            pltpu.VMEM((2, sensor), f32),
            pltpu.VMEM((n_band * n_tile - 1, 2, sensor), f32),
            dma((3,)),
            dma((width // piece_cols,)),
            dma((3, summing)),
            dma((3, 2, n_tile)),
            dma((2, n_tile)),
            dma((2, n_tile)),
            dma((2, summing)),
            dma,
            dma,
            dma,
            dma,
        ],
        compiler_params=pltpu.CompilerParams(
            collective_id=0, has_side_effects=True, vmem_limit_bytes=VMEM_BYTES
        ),
    )(in_hbm(calib), in_hbm(support), in_hbm(turned_window), in_hbm(measured.reshape(1, sensor)))
    solved, residual = pl.pallas_call(
        finish_kernel,
        out_shape=(
            jax.ShapeDtypeStruct((tile_rows, width), f32),
            jax.ShapeDtypeStruct((1, sensor), f32),
        ),
        in_specs=[vmem] * 2,
        out_specs=(vmem, vmem),
        compiler_params=pltpu.CompilerParams(vmem_limit_bytes=VMEM_BYTES),
    )(*[in_vmem(x) for x in held_back])
    return solved, residual.reshape(sensor)


def solution(mesh):
    placed = (P("tile", None, None, "band"), P("tile", None), P("tile", None, None), P("tile"))
    return jax.shard_map(
        body, mesh=mesh, in_specs=placed, out_specs=(P("tile", "band"), P("tile")), check_vma=False
    )
```

```python
import functools

import jax
import jax.numpy as jnp
from jax import lax
from jax.experimental import pallas as pl
from jax.experimental.pallas import tpu as pltpu
from jax.sharding import PartitionSpec as P

BANDS_PER_GROUP_PIX = 64
RIDGE = 0.25
LANES = 128
PACKED_ROWS = 16
VMEM_BYTES = 48 << 20
MESH = pl.DeviceIdType.MESH


def centre_of(n_tile):
    summing = n_tile // 2 if n_tile % 4 == 0 else n_tile
    return (n_tile - summing) // 2, summing


def far_first(n_tile):
    first, _ = centre_of(n_tile)

    def hops(h):
        there = first ^ h
        return abs(there // 2 - first // 2) + (there ^ first) % 2

    return sorted(range(n_tile), key=lambda h: (-hops(h), -abs((first ^ h) // 2 - first // 2), -h))


def pieces_of(n_tile, n_block, width):
    summing = centre_of(n_tile)[1]
    col_groups = min(summing, width // LANES)
    row_groups = summing // col_groups
    return col_groups, row_groups, n_block // row_groups, width // col_groups


def kernel(
    n_tile,
    n_band,
    calib,
    support_in,
    window_in,
    measured_in,
    solved_out,
    residual_out,
    support,
    window,
    measured,
    held,
    turned,
    stage,
    landed,
    packed,
    passed,
    grad_buf,
    base_buf,
    norm_buf,
    own_buf,
    mask_buf,
    band_mine,
    band_in,
    all_mine,
    all_in,
    small_sem,
    load_sem,
    rs_send,
    rs_recv,
    ag_send,
    ag_pass,
    ag_recv,
    band_send,
    band_recv,
    all_send,
    all_recv,
):
    tile_rows, k, pix, width = calib.shape
    entries = tile_rows * k
    rows = entries * pix
    n_block = n_tile * tile_rows
    col_groups, row_groups, piece_rows, piece_cols = pieces_of(n_tile, n_block, width)
    me = lax.axis_index("tile")
    band = lax.axis_index("band")
    odd = band % 2
    first, summing = centre_of(n_tile)
    mine = me - first
    sums_here = (odd == 1) & (mine >= 0) & (mine < summing)
    f32, bf16 = jnp.float32, jnp.bfloat16

    small = [
        pltpu.make_async_copy(source, target, small_sem.at[i])
        for i, (source, target) in enumerate(
            ((support_in, support), (window_in, window), (measured_in, measured))
        )
    ]
    for copy in small:
        copy.start()
    side = me // (n_tile // 2)
    across = me % 2
    ahead = []
    for j in range(summing):
        along = (1 - side) * (summing // 2 - 1 - j // 2) + side * (j // 2)
        ahead.append(2 * along + (across if j % 2 else 1 - across))
    pieces = ahead if row_groups == 1 else list(range(col_groups))
    loads = []
    for c in pieces:
        cols = pl.ds(pl.multiple_of(c * piece_cols, LANES), piece_cols)
        copy = pltpu.make_async_copy(calib.at[:, :, :, cols], held.at[c], load_sem.at[c])
        copy.start(priority=len(loads) % 2)
        loads.append(copy)

    def paired(index, n):
        turns = [(1 << b) * (1 - 2 * (index // (1 << b) % 2)) for b in range(n.bit_length() - 1)]
        return [
            sum([turn for b, turn in enumerate(turns) if h >> b & 1], index) for h in range(n)
        ]

    peers, others = paired(me, n_tile), paired(band, n_band)
    tile_order = far_first(n_tile)
    everyone = sorted(
        [(a, b) for a in range(n_tile) for b in range(n_band) if a or b],
        key=lambda s: (-(s[0] // 2 + s[0] % 2 + s[1] // 2), s[1] % 2),
    )
    barrier = pltpu.get_barrier_semaphore()

    def greet(tile, band):
        pl.semaphore_signal(
            barrier, inc=1, device_id={"tile": tile, "band": band}, device_id_type=MESH
        )

    @pl.when(sums_here)
    def _():
        for h in tile_order:
            greet(peers[h], band - 1)
            if h:
                greet(peers[h], band)

    @pl.when(jnp.logical_not(sums_here))
    def _():
        for p in range(summing):
            greet(first + p, band + 1 - odd)

    for b in range(1, n_band):
        greet(me, others[b])

    for copy in small:
        copy.wait()
    lane_entry = lax.broadcasted_iota(jnp.int32, (1, rows), 1) // pix
    sup_row = jnp.zeros((1, rows), jnp.int32)
    for e in range(entries):
        sup_row = jnp.where(lane_entry == e, support[e // k, e % k], sup_row)
    names = jnp.broadcast_to(sup_row, (n_block, rows)) == lax.broadcasted_iota(
        jnp.int32, (n_block, rows), 0
    )

    lane = lax.broadcasted_iota(jnp.int32, (1, LANES), 1)
    low = lane < pix

    def spread(w):
        pieces = []
        for t in range(tile_rows):
            col = t * pix // LANES * LANES
            tilev = w[:, col : col + LANES]
            rolled = pltpu.roll(tilev, pix, 1)
            both = jnp.where(low, tilev, rolled) if t * pix % LANES == 0 else jnp.where(low, rolled, tilev)
            pieces += [both] * (k * pix // LANES)
        return jnp.concatenate(pieces, axis=1)

    def rounded(x):
        return x.astype(bf16).astype(f32)

    def left_side(w):
        wide = jnp.broadcast_to(w, (n_block, rows))
        return jnp.where(names, wide, jnp.zeros((), f32)).astype(bf16)

    def both_parts(w):
        high = rounded(w)
        return jnp.concatenate([left_side(high), left_side(w - high)], axis=0)

    def three_parts(values):
        row = lax.broadcasted_iota(jnp.int32, (piece_rows, LANES), 0)
        parts = jnp.zeros((piece_rows, LANES), f32)
        for i, x in enumerate(values):
            high = rounded(x)
            middle = rounded(x - high)
            for l, part in enumerate((high, middle, x - high - middle)):
                parts = jnp.where(row == 3 * i + l, part, parts)
        return parts.astype(bf16)

    def lane_total(x):
        return jnp.sum(x, axis=1, keepdims=True)

    lanes = piece_cols // LANES

    def part(it, slab):
        return pl.ds(0, lanes + 1 if it == 1 and slab else lanes)

    def scatter_copy(it, j, slab):
        some = part(it, slab)
        return pltpu.make_async_remote_copy(
            src_ref=stage.at[it, ahead[j], some],
            dst_ref=landed.at[it, slab, me, some],
            send_sem=rs_send.at[it, j],
            recv_sem=rs_recv.at[it, slab, me],
            device_id={"tile": first + ahead[j], "band": band + 1 - slab},
            device_id_type=MESH,
        )

    def landing(it, slab, tile):
        some = part(it, slab)
        return pltpu.make_async_remote_copy(
            src_ref=stage.at[it, 0, some],
            dst_ref=landed.at[it, slab, tile, some],
            send_sem=rs_send.at[it, 0],
            recv_sem=rs_recv.at[it, slab, tile],
            device_id={"tile": tile, "band": band - 1},
            device_id_type=MESH,
        )

    def gather_copy(it, slab, h):
        return pltpu.make_async_remote_copy(
            src_ref=packed.at[it, mine] if slab else passed.at[it],
            dst_ref=packed.at[it, mine],
            send_sem=(ag_send if slab else ag_pass).at[it, h],
            recv_sem=ag_recv.at[it, mine],
            device_id={"tile": peers[h], "band": band if slab else band - 1},
            device_id_type=MESH,
        )

    def arriving(it, piece):
        return pltpu.make_async_remote_copy(
            src_ref=packed.at[it, piece],
            dst_ref=packed.at[it, piece],
            send_sem=ag_send.at[it, 0],
            recv_sem=ag_recv.at[it, piece],
            device_id={"tile": first + piece, "band": band + 1 - odd},
            device_id_type=MESH,
        )

    def band_copy(b):
        return pltpu.make_async_remote_copy(
            src_ref=band_mine,
            dst_ref=band_in.at[b - 1],
            send_sem=band_send,
            recv_sem=band_recv,
            device_id={"tile": me, "band": others[b]},
            device_id_type=MESH,
        )

    def all_copy(a, b):
        return pltpu.make_async_remote_copy(
            src_ref=all_mine,
            dst_ref=all_in.at[a * n_band + b - 1],
            send_sem=all_send,
            recv_sem=all_recv,
            device_id={"tile": peers[a], "band": others[b]},
            device_id_type=MESH,
        )

    band_whole = pltpu.make_async_remote_copy(
        src_ref=band_in,
        dst_ref=band_in,
        send_sem=band_send,
        recv_sem=band_recv,
        device_id={"tile": me, "band": others[1]},
        device_id_type=MESH,
    )
    all_whole = pltpu.make_async_remote_copy(
        src_ref=all_in,
        dst_ref=all_in,
        send_sem=all_send,
        recv_sem=all_recv,
        device_id={"tile": me, "band": others[1]},
        device_id_type=MESH,
    )

    def each_scatter(it, j, act):
        @pl.when(odd == 0)
        def _():
            act(scatter_copy(it, j, 0))

        @pl.when((odd == 1) & (ahead[j] != mine))
        def _():
            act(scatter_copy(it, j, 1))

    def scatter_start(it, j):
        each_scatter(it, j, lambda copy: copy.start())

    def put(it, p, product):
        for l in range(lanes):
            stage[it, p, l] = product[:, l * LANES : (l + 1) * LANES].astype(bf16)

    def matrix(c):
        return held[c].reshape(rows, piece_cols)

    def windowed(c):
        return jnp.concatenate(
            [
                held[c, e // k, e % k, at : at + PACKED_ROWS, :] * mask_buf[c, e]
                for e in range(entries)
                for at in range(0, pix, PACKED_ROWS)
            ],
            axis=0,
        )

    def scatter_send(it, left, ready, source, finish, later):
        for i, c in enumerate(pieces):
            ready(i, c)
            product = jnp.dot(left, source(c), preferred_element_type=f32)
            for r in range(row_groups):
                at = slice(r * piece_rows, (r + 1) * piece_rows)
                rest = slice(n_block + r * piece_rows, n_block + (r + 1) * piece_rows)
                finish(r * col_groups + c, product[at], product[rest])
            if row_groups == 1:
                scatter_start(it, i)
            later(c, product)
        if row_groups > 1:
            for j in range(summing):
                scatter_start(it, j)

    def lanes_sum(x):
        total = x[0]
        for l in range(1, lanes):
            total = total + x[l]
        return jnp.sum(total, axis=0, keepdims=True)

    def landed_sum(it, slab):
        some = part(it, slab)
        total = (
            stage[it, mine, some].astype(f32)
            if slab
            else jnp.zeros((lanes, piece_rows, LANES), f32)
        )
        for h in reversed(tile_order):
            if h or not slab:
                landing(it, slab, peers[h]).wait_recv()
                total = total + landed[it, slab, peers[h], some].astype(f32)
        return total

    gather_order = sorted(
        [(h, slab) for slab in range(2) for h in range(n_tile) if h or not slab],
        key=lambda s: (s[1], tile_order.index(s[0])),
    )

    def gather_send(it, vectors):
        for l in range(lanes):
            passed[it, l] = vectors[0][l].astype(bf16)
        for h, slab in gather_order:
            if not slab:
                gather_copy(it, slab, h).start()
        for l in range(lanes):
            packed[it, mine, l] = vectors[1][l].astype(bf16)
        for h, slab in gather_order:
            if slab:
                gather_copy(it, slab, h).start()

    def joined(it, piece):
        return jnp.concatenate([packed[it, piece, l] for l in range(lanes)], axis=1)

    def column(it, c):
        return jnp.concatenate(
            [joined(it, r * col_groups + c) for r in range(row_groups)], axis=0
        )

    def forward(it):
        out = jnp.zeros((n_block, rows), f32)
        for j in reversed(range(summing)):

            @pl.when((odd == 0) | (ahead[j] != mine))
            def _():
                arriving(it, ahead[j]).wait_recv()

            if row_groups == 1:
                out = out + jnp.dot(
                    joined(it, ahead[j]), turned[ahead[j]], preferred_element_type=f32
                )
        if row_groups > 1:
            for c in range(col_groups):
                out = out + jnp.dot(column(it, c), turned[c], preferred_element_type=f32)
        out = jnp.where(names, out, jnp.zeros((), f32))
        cols = []
        per = k * pix // LANES
        for t in range(tile_rows):
            acc = out[:, t * per * LANES : t * per * LANES + LANES]
            for c in range(1, per):
                at = (t * per + c) * LANES
                acc = acc + out[:, at : at + LANES]
            cols.append(jnp.sum(acc, axis=0, keepdims=True))
        return jnp.concatenate(cols, axis=0)

    def image_of(twice):
        return jnp.concatenate(
            [
                jnp.where(low, twice[t : t + 1], twice[t + 1 : t + 2])
                for t in range(0, tile_rows, 2)
            ],
            axis=1,
        )

    def both_lanes(x):
        return x + pltpu.roll(x, pix, 1)

    def keep_own(it):
        own = (lax.broadcasted_iota(jnp.int32, (8, n_block), 1) - me * tile_rows) == (
            lax.broadcasted_iota(jnp.int32, (8, n_block), 0)
        )
        own = jnp.where(own, 1.0, 0.0).astype(bf16)
        for c in range(col_groups):
            own_buf[it, :, c * piece_cols : (c + 1) * piece_cols] = jnp.dot(
                own, column(it, c), preferred_element_type=f32
            )

    def scatter_sent(it):
        for j in range(summing):
            each_scatter(it, j, lambda copy: copy.wait_send())

    def gather_sent(it):
        @pl.when(sums_here)
        def _():
            for h in tile_order:
                gather_copy(it, 0, h).wait_send()
                if h:
                    gather_copy(it, 1, h).wait_send()

    start = measured[...]
    left = both_parts(spread(start))
    columns = lax.broadcasted_iota(jnp.int32, (PACKED_ROWS, width), 1)
    bands = band * (width // BANDS_PER_GROUP_PIX) + columns // BANDS_PER_GROUP_PIX
    for e in range(entries):
        t, j = e // k, e % k
        inside = (bands >= window[t, 0, j]) & (bands < window[t, 1, j])
        inside = jnp.where(inside, 1.0, 0.0).astype(bf16)
        for c in range(col_groups):
            mask_buf[c, e] = inside[:, c * piece_cols : (c + 1) * piece_cols]

    def load(i, c):
        loads[i].wait()
        if i == 0:
            pl.semaphore_wait(barrier, jnp.where(sums_here, 2 * n_tile - 1, summing) + n_band - 1)

    def put_rest(c, product):
        for r in range(row_groups):
            rest = slice(n_block + r * piece_rows, n_block + (r + 1) * piece_rows)
            put(2, r * col_groups + c, product[rest])

    scatter_send(0, left, load, windowed, lambda p, high, rest: put(0, p, high), put_rest)
    for c in range(col_groups):
        for e in range(entries):
            for at in range(0, pix, PACKED_ROWS):
                at = pl.ds(at, PACKED_ROWS)
                held[c, e // k, e % k, at, :] = held[c, e // k, e % k, at, :] * mask_buf[c, e]
        turned[c] = matrix(c).T
    norm_buf[...] = jnp.zeros((8, LANES), f32)

    @pl.when(sums_here)
    def _():
        own = landed_sum(0, 1)
        gradients = [landed_sum(0, 0), own]
        gather_send(0, gradients)
        norm_buf[3:4, :] = sum(lanes_sum(gradient * gradient) for gradient in gradients)
        for slab in range(2):
            grad_buf[slab] = gradients[slab]

    band_mine[tile_rows : tile_rows + 1, :] = norm_buf[3:4, :]
    band_mine[0:tile_rows, :] = forward(0)
    for b in reversed(range(1, n_band)):
        band_copy(b).start()
    for j in range(summing):
        scatter_start(2, j)
    keep_own(0)
    scatter_sent(0)
    gather_sent(0)
    band_whole.wait_recv()
    total = band_mine[...]
    for b in range(1, n_band):
        total = total + band_in[b - 1]
    twice = both_lanes(total[0:tile_rows, :])
    image = image_of(twice)

    tail = three_parts((image * image, total[tile_rows : tile_rows + 1, :]))
    for p in range(summing):
        stage[1, p, lanes] = tail
    scatter_send(
        1,
        both_parts(
            jnp.concatenate(
                [twice[t : t + 1] for t in range(tile_rows) for _ in range(k * pix // LANES)], axis=1
            )
        ),
        lambda i, c: None,
        matrix,
        lambda p, high, rest: put(1, p, high + rest),
        lambda c, product: None,
    )
    norm_buf[4:5, :] = image * image * (1.0 / n_band)
    band_whole.wait_send()
    scatter_sent(2)

    @pl.when(sums_here)
    def _():
        for slab in range(2):
            base_buf[slab] = grad_buf[slab] + landed_sum(2, slab)
        own = landed_sum(1, 1)
        sums = lane_total(own[lanes])
        image_square, gamma = [sum(sums[3 * i + l : 3 * i + l + 1] for l in range(3)) for i in range(2)]
        alpha = gamma / (image_square + RIDGE * gamma)
        kept = [
            base_buf[slab] - (RIDGE * alpha) * grad_buf[slab] for slab in range(2)
        ]
        turned_images = [landed_sum(1, 0), own[:lanes]]
        gradients = [kept[slab] - alpha * turned_images[slab] for slab in range(2)]
        gather_send(1, gradients)
        norm_buf[0:1, :] = sum(lanes_sum(x * x) for x in gradients)
        norm_buf[1:2, :] = sum(lanes_sum(x * grad_buf[slab]) for slab, x in enumerate(gradients))
        norm_buf[2:3, :] = sum(lanes_sum(x * y) for x, y in zip(gradients, turned_images))

    group = LANES // 8
    folded = norm_buf[...]
    for by in (4, 2, 1):
        folded = folded + pltpu.roll(folded, by * group, 1)
    one_of = lax.broadcasted_iota(jnp.int32, (8, LANES), 1) // group == lax.broadcasted_iota(
        jnp.int32, (8, LANES), 0
    )
    folded = jnp.sum(jnp.where(one_of, folded, jnp.zeros((), f32)), axis=0, keepdims=True)
    all_mine[1:2, :] = folded
    all_mine[0:1, :] = image_of(both_lanes(forward(1)))
    for a, b in everyone:
        all_copy(a, b).start()
    keep_own(1)
    scatter_sent(1)
    gather_sent(1)
    all_whole.wait_recv()
    partial = square = None
    for a in range(n_tile):
        total = all_in[a * n_band - 1] if a else all_mine[...]
        for b in range(1, n_band):
            total = total + all_in[a * n_band + b - 1]
        if a:
            sums, square = sums + total, square + total * total
        else:
            partial, sums, square = total[0:1, :], total, total * total
    sums = jnp.broadcast_to(sums[1:2, :], (8, LANES))
    sums = lane_total(jnp.where(one_of, sums, jnp.zeros((), f32)))
    gamma_next, cross, image_cross, gamma, image_square = [sums[q : q + 1] for q in range(5)]
    alpha = gamma / (image_square + RIDGE * gamma)
    beta = gamma_next / gamma
    square = lane_total(square[0:1, :]) + 2.0 * beta * image_cross + beta * beta * image_square
    direction_square = gamma_next + 2.0 * beta * cross + beta * beta * gamma
    step = gamma_next / (square + RIDGE * direction_square)
    solved_out[...] = (alpha + step * beta) * own_buf[0, 0:tile_rows, :] + step * own_buf[1, 0:tile_rows, :]
    residual_out[...] = start - (alpha + step * beta) * image - step * partial
    all_whole.wait_send()


def finish_kernel(solved, residual, solution_out, residual_out):
    solution_out[...] = solved[...]
    residual_out[...] = residual[...]


def body(calib, support, band_window, measured):
    n_tile, n_band = lax.axis_size("tile"), lax.axis_size("band")
    tile_rows, k, pix, width = calib.shape
    entries = tile_rows * k
    sensor = tile_rows * pix
    n_block = n_tile * tile_rows
    _, _, piece_rows, piece_cols = pieces_of(n_tile, n_block, width)
    summing = centre_of(n_tile)[1]
    f32, bf16 = jnp.float32, jnp.bfloat16
    vmem = pl.BlockSpec(memory_space=pltpu.VMEM)
    dma = pltpu.SemaphoreType.DMA
    lanes = piece_cols // LANES
    piece = (lanes + 1, piece_rows, LANES)
    bare = (lanes, piece_rows, LANES)
    hbm = pl.BlockSpec(memory_space=pl.ANY)
    in_hbm = lambda x: pltpu.with_memory_space_constraint(x, pltpu.HBM)
    in_vmem = lambda x: pltpu.with_memory_space_constraint(x, pltpu.VMEM)
    turned_window = jnp.transpose(band_window, (0, 2, 1))
    held_back = pl.pallas_call(
        functools.partial(kernel, n_tile, n_band),
        out_shape=(pltpu.VMEM((tile_rows, width), f32), pltpu.VMEM((1, sensor), f32)),
        in_specs=[hbm] * 4,
        out_specs=(vmem,) * 2,
        scratch_shapes=[
            pltpu.SMEM((tile_rows, k), jnp.int32),
            pltpu.SMEM((tile_rows, 2, k), jnp.int32),
            pltpu.VMEM((1, sensor), f32),
            pltpu.VMEM((width // piece_cols, tile_rows, k, pix, piece_cols), bf16),
            pltpu.VMEM((width // piece_cols, piece_cols, entries * pix), bf16),
            pltpu.VMEM((3, summing) + piece, bf16),
            pltpu.VMEM((3, 2, n_tile) + piece, bf16),
            pltpu.VMEM((2, summing) + bare, bf16),
            pltpu.VMEM((2,) + bare, bf16),
            pltpu.VMEM((2,) + bare, f32),
            pltpu.VMEM((2,) + bare, f32),
            pltpu.VMEM((8, LANES), f32),
            pltpu.VMEM((2, 8, width), f32),
            pltpu.VMEM((width // piece_cols, entries, PACKED_ROWS, piece_cols), bf16),
            pltpu.VMEM((tile_rows + 1, LANES), f32),
            pltpu.VMEM((n_band - 1, tile_rows + 1, LANES), f32),
            pltpu.VMEM((2, sensor), f32),
            pltpu.VMEM((n_band * n_tile - 1, 2, sensor), f32),
            dma((3,)),
            dma((width // piece_cols,)),
            dma((3, summing)),
            dma((3, 2, n_tile)),
            dma((2, n_tile)),
            dma((2, n_tile)),
            dma((2, summing)),
            dma,
            dma,
            dma,
            dma,
        ],
        compiler_params=pltpu.CompilerParams(
            collective_id=0, has_side_effects=True, vmem_limit_bytes=VMEM_BYTES
        ),
    )(in_hbm(calib), in_hbm(support), in_hbm(turned_window), in_hbm(measured.reshape(1, sensor)))
    solved, residual = pl.pallas_call(
        finish_kernel,
        out_shape=(
            jax.ShapeDtypeStruct((tile_rows, width), f32),
            jax.ShapeDtypeStruct((1, sensor), f32),
        ),
        in_specs=[vmem] * 2,
        out_specs=(vmem, vmem),
        compiler_params=pltpu.CompilerParams(vmem_limit_bytes=VMEM_BYTES),
    )(*[in_vmem(x) for x in held_back])
    return solved, residual.reshape(sensor)


def solution(mesh):
    placed = (P("tile", None, None, "band"), P("tile", None), P("tile", None, None), P("tile"))
    return jax.shard_map(
        body, mesh=mesh, in_specs=placed, out_specs=(P("tile", "band"), P("tile")), check_vma=False
    )
```

```python
import functools

import jax
import jax.numpy as jnp
from jax import lax
from jax.experimental import pallas as pl
from jax.experimental.pallas import tpu as pltpu
from jax.sharding import PartitionSpec as P

BANDS_PER_GROUP_PIX = 64
RIDGE = 0.25
LANES = 128
PACKED_ROWS = 16
VMEM_BYTES = 48 << 20
MESH = pl.DeviceIdType.MESH


def centre_of(n_tile):
    summing = n_tile // 2 if n_tile % 4 == 0 else n_tile
    return (n_tile - summing) // 2, summing


def far_first(n_tile):
    first, _ = centre_of(n_tile)

    def hops(h):
        there = first ^ h
        return abs(there // 2 - first // 2) + (there ^ first) % 2

    return sorted(range(n_tile), key=lambda h: (-hops(h), -abs((first ^ h) // 2 - first // 2), -h))


def pieces_of(n_tile, n_block, width):
    summing = centre_of(n_tile)[1]
    col_groups = min(summing, width // LANES)
    row_groups = summing // col_groups
    return col_groups, row_groups, n_block // row_groups, width // col_groups


def kernel(
    n_tile,
    n_band,
    calib,
    support_in,
    window_in,
    measured_in,
    solved_out,
    residual_out,
    support,
    window,
    measured,
    held,
    turned,
    stage,
    landed,
    packed,
    passed,
    grad_buf,
    base_buf,
    norm_buf,
    own_buf,
    mask_buf,
    band_mine,
    band_in,
    all_mine,
    all_in,
    small_sem,
    load_sem,
    rs_send,
    rs_recv,
    ag_send,
    ag_pass,
    ag_recv,
    band_send,
    band_recv,
    all_send,
    all_recv,
):
    tile_rows, k, pix, width = calib.shape
    entries = tile_rows * k
    rows = entries * pix
    n_block = n_tile * tile_rows
    col_groups, row_groups, piece_rows, piece_cols = pieces_of(n_tile, n_block, width)
    me = lax.axis_index("tile")
    band = lax.axis_index("band")
    odd = band % 2
    first, summing = centre_of(n_tile)
    mine = me - first
    sums_here = (odd == 1) & (mine >= 0) & (mine < summing)
    f32, bf16 = jnp.float32, jnp.bfloat16

    small = [
        pltpu.make_async_copy(source, target, small_sem.at[i])
        for i, (source, target) in enumerate(
            ((support_in, support), (window_in, window), (measured_in, measured))
        )
    ]
    for copy in small:
        copy.start()
    side = me // (n_tile // 2)
    across = me % 2
    ahead = []
    for j in range(summing):
        along = (1 - side) * (summing // 2 - 1 - j // 2) + side * (j // 2)
        ahead.append(2 * along + (across if j % 2 else 1 - across))
    pieces = ahead if row_groups == 1 else list(range(col_groups))
    loads = []
    for c in pieces:
        cols = pl.ds(pl.multiple_of(c * piece_cols, LANES), piece_cols)
        copy = pltpu.make_async_copy(calib.at[:, :, :, cols], held.at[c], load_sem.at[c])
        copy.start(priority=min(len(loads), 1))
        loads.append(copy)

    def paired(index, n):
        turns = [(1 << b) * (1 - 2 * (index // (1 << b) % 2)) for b in range(n.bit_length() - 1)]
        return [
            sum([turn for b, turn in enumerate(turns) if h >> b & 1], index) for h in range(n)
        ]

    peers, others = paired(me, n_tile), paired(band, n_band)
    tile_order = far_first(n_tile)
    everyone = sorted(
        [(a, b) for a in range(n_tile) for b in range(n_band) if a or b],
        key=lambda s: (-(s[0] // 2 + s[0] % 2 + s[1] // 2), s[1] % 2),
    )
    barrier = pltpu.get_barrier_semaphore()

    def greet(tile, band):
        pl.semaphore_signal(
            barrier, inc=1, device_id={"tile": tile, "band": band}, device_id_type=MESH
        )

    @pl.when(sums_here)
    def _():
        for h in tile_order:
            greet(peers[h], band - 1)
            if h:
                greet(peers[h], band)

    @pl.when(jnp.logical_not(sums_here))
    def _():
        for p in range(summing):
            greet(first + p, band + 1 - odd)

    for b in range(1, n_band):
        greet(me, others[b])

    for copy in small:
        copy.wait()
    lane_entry = lax.broadcasted_iota(jnp.int32, (1, rows), 1) // pix
    sup_row = jnp.zeros((1, rows), jnp.int32)
    for e in range(entries):
        sup_row = jnp.where(lane_entry == e, support[e // k, e % k], sup_row)
    names = jnp.broadcast_to(sup_row, (n_block, rows)) == lax.broadcasted_iota(
        jnp.int32, (n_block, rows), 0
    )

    lane = lax.broadcasted_iota(jnp.int32, (1, LANES), 1)
    low = lane < pix

    def spread(w):
        pieces = []
        for t in range(tile_rows):
            col = t * pix // LANES * LANES
            tilev = w[:, col : col + LANES]
            rolled = pltpu.roll(tilev, pix, 1)
            both = jnp.where(low, tilev, rolled) if t * pix % LANES == 0 else jnp.where(low, rolled, tilev)
            pieces += [both] * (k * pix // LANES)
        return jnp.concatenate(pieces, axis=1)

    def rounded(x):
        return x.astype(bf16).astype(f32)

    def left_side(w):
        wide = jnp.broadcast_to(w, (n_block, rows))
        return jnp.where(names, wide, jnp.zeros((), f32)).astype(bf16)

    def both_parts(w):
        high = rounded(w)
        return jnp.concatenate([left_side(high), left_side(w - high)], axis=0)

    def three_parts(values):
        row = lax.broadcasted_iota(jnp.int32, (piece_rows, LANES), 0)
        parts = jnp.zeros((piece_rows, LANES), f32)
        for i, x in enumerate(values):
            high = rounded(x)
            middle = rounded(x - high)
            for l, part in enumerate((high, middle, x - high - middle)):
                parts = jnp.where(row == 3 * i + l, part, parts)
        return parts.astype(bf16)

    def lane_total(x):
        return jnp.sum(x, axis=1, keepdims=True)

    lanes = piece_cols // LANES

    def part(it, slab):
        return pl.ds(0, lanes + 1 if it == 1 and slab else lanes)

    def scatter_copy(it, j, slab):
        some = part(it, slab)
        return pltpu.make_async_remote_copy(
            src_ref=stage.at[it, ahead[j], some],
            dst_ref=landed.at[it, slab, me, some],
            send_sem=rs_send.at[it, j],
            recv_sem=rs_recv.at[it, slab, me],
            device_id={"tile": first + ahead[j], "band": band + 1 - slab},
            device_id_type=MESH,
        )

    def landing(it, slab, tile):
        some = part(it, slab)
        return pltpu.make_async_remote_copy(
            src_ref=stage.at[it, 0, some],
            dst_ref=landed.at[it, slab, tile, some],
            send_sem=rs_send.at[it, 0],
            recv_sem=rs_recv.at[it, slab, tile],
            device_id={"tile": tile, "band": band - 1},
            device_id_type=MESH,
        )

    def gather_copy(it, slab, h):
        return pltpu.make_async_remote_copy(
            src_ref=packed.at[it, mine] if slab else passed.at[it],
            dst_ref=packed.at[it, mine],
            send_sem=(ag_send if slab else ag_pass).at[it, h],
            recv_sem=ag_recv.at[it, mine],
            device_id={"tile": peers[h], "band": band if slab else band - 1},
            device_id_type=MESH,
        )

    def arriving(it, piece):
        return pltpu.make_async_remote_copy(
            src_ref=packed.at[it, piece],
            dst_ref=packed.at[it, piece],
            send_sem=ag_send.at[it, 0],
            recv_sem=ag_recv.at[it, piece],
            device_id={"tile": first + piece, "band": band + 1 - odd},
            device_id_type=MESH,
        )

    def band_copy(b):
        return pltpu.make_async_remote_copy(
            src_ref=band_mine,
            dst_ref=band_in.at[b - 1],
            send_sem=band_send,
            recv_sem=band_recv,
            device_id={"tile": me, "band": others[b]},
            device_id_type=MESH,
        )

    def all_copy(a, b):
        return pltpu.make_async_remote_copy(
            src_ref=all_mine,
            dst_ref=all_in.at[a * n_band + b - 1],
            send_sem=all_send,
            recv_sem=all_recv,
            device_id={"tile": peers[a], "band": others[b]},
            device_id_type=MESH,
        )

    band_whole = pltpu.make_async_remote_copy(
        src_ref=band_in,
        dst_ref=band_in,
        send_sem=band_send,
        recv_sem=band_recv,
        device_id={"tile": me, "band": others[1]},
        device_id_type=MESH,
    )
    all_whole = pltpu.make_async_remote_copy(
        src_ref=all_in,
        dst_ref=all_in,
        send_sem=all_send,
        recv_sem=all_recv,
        device_id={"tile": me, "band": others[1]},
        device_id_type=MESH,
    )

    def each_scatter(it, j, act):
        @pl.when(odd == 0)
        def _():
            act(scatter_copy(it, j, 0))

        @pl.when((odd == 1) & (ahead[j] != mine))
        def _():
            act(scatter_copy(it, j, 1))

    def scatter_start(it, j):
        each_scatter(it, j, lambda copy: copy.start())

    def put(it, p, product):
        for l in range(lanes):
            stage[it, p, l] = product[:, l * LANES : (l + 1) * LANES].astype(bf16)

    def matrix(c):
        return held[c].reshape(rows, piece_cols)

    def windowed(c):
        return jnp.concatenate(
            [
                held[c, e // k, e % k, at : at + PACKED_ROWS, :] * mask_buf[c, e]
                for e in range(entries)
                for at in range(0, pix, PACKED_ROWS)
            ],
            axis=0,
        )

    def scatter_send(it, left, ready, source, finish, later):
        for i, c in enumerate(pieces):
            ready(i, c)
            product = jnp.dot(left, source(c), preferred_element_type=f32)
            for r in range(row_groups):
                at = slice(r * piece_rows, (r + 1) * piece_rows)
                rest = slice(n_block + r * piece_rows, n_block + (r + 1) * piece_rows)
                finish(r * col_groups + c, product[at], product[rest])
            if row_groups == 1:
                scatter_start(it, i)
            later(c, product)
        if row_groups > 1:
            for j in range(summing):
                scatter_start(it, j)

    def lanes_sum(x):
        total = x[0]
        for l in range(1, lanes):
            total = total + x[l]
        return jnp.sum(total, axis=0, keepdims=True)

    def landed_sum(it, slab):
        some = part(it, slab)
        total = (
            stage[it, mine, some].astype(f32)
            if slab
            else jnp.zeros((lanes, piece_rows, LANES), f32)
        )
        for h in reversed(tile_order):
            if h or not slab:
                landing(it, slab, peers[h]).wait_recv()
                total = total + landed[it, slab, peers[h], some].astype(f32)
        return total

    gather_order = sorted(
        [(h, slab) for slab in range(2) for h in range(n_tile) if h or not slab],
        key=lambda s: (s[1], tile_order.index(s[0])),
    )

    def gather_send(it, vectors):
        for l in range(lanes):
            passed[it, l] = vectors[0][l].astype(bf16)
        for h, slab in gather_order:
            if not slab:
                gather_copy(it, slab, h).start()
        for l in range(lanes):
            packed[it, mine, l] = vectors[1][l].astype(bf16)
        for h, slab in gather_order:
            if slab:
                gather_copy(it, slab, h).start()

    def joined(it, piece):
        return jnp.concatenate([packed[it, piece, l] for l in range(lanes)], axis=1)

    def column(it, c):
        return jnp.concatenate(
            [joined(it, r * col_groups + c) for r in range(row_groups)], axis=0
        )

    def forward(it):
        out = jnp.zeros((n_block, rows), f32)
        for j in reversed(range(summing)):

            @pl.when((odd == 0) | (ahead[j] != mine))
            def _():
                arriving(it, ahead[j]).wait_recv()

            if row_groups == 1:
                out = out + jnp.dot(
                    joined(it, ahead[j]), turned[ahead[j]], preferred_element_type=f32
                )
        if row_groups > 1:
            for c in range(col_groups):
                out = out + jnp.dot(column(it, c), turned[c], preferred_element_type=f32)
        out = jnp.where(names, out, jnp.zeros((), f32))
        cols = []
        per = k * pix // LANES
        for t in range(tile_rows):
            acc = out[:, t * per * LANES : t * per * LANES + LANES]
            for c in range(1, per):
                at = (t * per + c) * LANES
                acc = acc + out[:, at : at + LANES]
            cols.append(jnp.sum(acc, axis=0, keepdims=True))
        return jnp.concatenate(cols, axis=0)

    def image_of(twice):
        return jnp.concatenate(
            [
                jnp.where(low, twice[t : t + 1], twice[t + 1 : t + 2])
                for t in range(0, tile_rows, 2)
            ],
            axis=1,
        )

    def both_lanes(x):
        return x + pltpu.roll(x, pix, 1)

    def keep_own(it):
        own = (lax.broadcasted_iota(jnp.int32, (8, n_block), 1) - me * tile_rows) == (
            lax.broadcasted_iota(jnp.int32, (8, n_block), 0)
        )
        own = jnp.where(own, 1.0, 0.0).astype(bf16)
        for c in range(col_groups):
            own_buf[it, :, c * piece_cols : (c + 1) * piece_cols] = jnp.dot(
                own, column(it, c), preferred_element_type=f32
            )

    def scatter_sent(it):
        for j in range(summing):
            each_scatter(it, j, lambda copy: copy.wait_send())

    def gather_sent(it):
        @pl.when(sums_here)
        def _():
            for h in tile_order:
                gather_copy(it, 0, h).wait_send()
                if h:
                    gather_copy(it, 1, h).wait_send()

    start = measured[...]
    left = both_parts(spread(start))
    columns = lax.broadcasted_iota(jnp.int32, (PACKED_ROWS, width), 1)
    bands = band * (width // BANDS_PER_GROUP_PIX) + columns // BANDS_PER_GROUP_PIX
    for e in range(entries):
        t, j = e // k, e % k
        inside = (bands >= window[t, 0, j]) & (bands < window[t, 1, j])
        inside = jnp.where(inside, 1.0, 0.0).astype(bf16)
        for c in range(col_groups):
            mask_buf[c, e] = inside[:, c * piece_cols : (c + 1) * piece_cols]

    def load(i, c):
        loads[i].wait()
        if i == 0:
            pl.semaphore_wait(barrier, jnp.where(sums_here, 2 * n_tile - 1, summing) + n_band - 1)

    def put_rest(c, product):
        for r in range(row_groups):
            rest = slice(n_block + r * piece_rows, n_block + (r + 1) * piece_rows)
            put(2, r * col_groups + c, product[rest])

    scatter_send(0, left, load, windowed, lambda p, high, rest: put(0, p, high), put_rest)
    for c in range(col_groups):
        for e in range(entries):
            for at in range(0, pix, PACKED_ROWS):
                at = pl.ds(at, PACKED_ROWS)
                held[c, e // k, e % k, at, :] = held[c, e // k, e % k, at, :] * mask_buf[c, e]
        turned[c] = matrix(c).T
    norm_buf[...] = jnp.zeros((8, LANES), f32)

    @pl.when(sums_here)
    def _():
        own = landed_sum(0, 1)
        gradients = [landed_sum(0, 0), own]
        gather_send(0, gradients)
        norm_buf[3:4, :] = sum(lanes_sum(gradient * gradient) for gradient in gradients)
        for slab in range(2):
            grad_buf[slab] = gradients[slab]

    band_mine[tile_rows : tile_rows + 1, :] = norm_buf[3:4, :]
    band_mine[0:tile_rows, :] = forward(0)
    for b in reversed(range(1, n_band)):
        band_copy(b).start()
    for j in range(summing):
        scatter_start(2, j)
    keep_own(0)
    scatter_sent(0)
    gather_sent(0)
    band_whole.wait_recv()
    total = band_mine[...]
    for b in range(1, n_band):
        total = total + band_in[b - 1]
    twice = both_lanes(total[0:tile_rows, :])
    image = image_of(twice)

    tail = three_parts((image * image, total[tile_rows : tile_rows + 1, :]))
    for p in range(summing):
        stage[1, p, lanes] = tail
    scatter_send(
        1,
        both_parts(
            jnp.concatenate(
                [twice[t : t + 1] for t in range(tile_rows) for _ in range(k * pix // LANES)], axis=1
            )
        ),
        lambda i, c: None,
        matrix,
        lambda p, high, rest: put(1, p, high + rest),
        lambda c, product: None,
    )
    norm_buf[4:5, :] = image * image * (1.0 / n_band)
    band_whole.wait_send()
    scatter_sent(2)

    @pl.when(sums_here)
    def _():
        for slab in range(2):
            base_buf[slab] = grad_buf[slab] + landed_sum(2, slab)
        own = landed_sum(1, 1)
        sums = lane_total(own[lanes])
        image_square, gamma = [sum(sums[3 * i + l : 3 * i + l + 1] for l in range(3)) for i in range(2)]
        alpha = gamma / (image_square + RIDGE * gamma)
        kept = [
            base_buf[slab] - (RIDGE * alpha) * grad_buf[slab] for slab in range(2)
        ]
        turned_images = [landed_sum(1, 0), own[:lanes]]
        gradients = [kept[slab] - alpha * turned_images[slab] for slab in range(2)]
        gather_send(1, gradients)
        norm_buf[0:1, :] = sum(lanes_sum(x * x) for x in gradients)
        norm_buf[1:2, :] = sum(lanes_sum(x * grad_buf[slab]) for slab, x in enumerate(gradients))
        norm_buf[2:3, :] = sum(lanes_sum(x * y) for x, y in zip(gradients, turned_images))

    group = LANES // 8
    folded = norm_buf[...]
    for by in (4, 2, 1):
        folded = folded + pltpu.roll(folded, by * group, 1)
    one_of = lax.broadcasted_iota(jnp.int32, (8, LANES), 1) // group == lax.broadcasted_iota(
        jnp.int32, (8, LANES), 0
    )
    folded = jnp.sum(jnp.where(one_of, folded, jnp.zeros((), f32)), axis=0, keepdims=True)
    all_mine[1:2, :] = folded
    all_mine[0:1, :] = image_of(both_lanes(forward(1)))
    for a, b in everyone:
        all_copy(a, b).start()
    keep_own(1)
    scatter_sent(1)
    gather_sent(1)
    all_whole.wait_recv()
    partial = square = None
    for a in range(n_tile):
        total = all_in[a * n_band - 1] if a else all_mine[...]
        for b in range(1, n_band):
            total = total + all_in[a * n_band + b - 1]
        if a:
            sums, square = sums + total, square + total * total
        else:
            partial, sums, square = total[0:1, :], total, total * total
    sums = jnp.broadcast_to(sums[1:2, :], (8, LANES))
    sums = lane_total(jnp.where(one_of, sums, jnp.zeros((), f32)))
    gamma_next, cross, image_cross, gamma, image_square = [sums[q : q + 1] for q in range(5)]
    alpha = gamma / (image_square + RIDGE * gamma)
    beta = gamma_next / gamma
    square = lane_total(square[0:1, :]) + 2.0 * beta * image_cross + beta * beta * image_square
    direction_square = gamma_next + 2.0 * beta * cross + beta * beta * gamma
    step = gamma_next / (square + RIDGE * direction_square)
    solved_out[...] = (alpha + step * beta) * own_buf[0, 0:tile_rows, :] + step * own_buf[1, 0:tile_rows, :]
    residual_out[...] = start - (alpha + step * beta) * image - step * partial
    all_whole.wait_send()


def finish_kernel(solved, residual, solution_out, residual_out):
    solution_out[...] = solved[...]
    residual_out[...] = residual[...]


def body(calib, support, band_window, measured):
    n_tile, n_band = lax.axis_size("tile"), lax.axis_size("band")
    tile_rows, k, pix, width = calib.shape
    entries = tile_rows * k
    sensor = tile_rows * pix
    n_block = n_tile * tile_rows
    _, _, piece_rows, piece_cols = pieces_of(n_tile, n_block, width)
    summing = centre_of(n_tile)[1]
    f32, bf16 = jnp.float32, jnp.bfloat16
    vmem = pl.BlockSpec(memory_space=pltpu.VMEM)
    dma = pltpu.SemaphoreType.DMA
    lanes = piece_cols // LANES
    piece = (lanes + 1, piece_rows, LANES)
    bare = (lanes, piece_rows, LANES)
    hbm = pl.BlockSpec(memory_space=pl.ANY)
    in_hbm = lambda x: pltpu.with_memory_space_constraint(x, pltpu.HBM)
    in_vmem = lambda x: pltpu.with_memory_space_constraint(x, pltpu.VMEM)
    turned_window = jnp.transpose(band_window, (0, 2, 1))
    held_back = pl.pallas_call(
        functools.partial(kernel, n_tile, n_band),
        out_shape=(pltpu.VMEM((tile_rows, width), f32), pltpu.VMEM((1, sensor), f32)),
        in_specs=[hbm] * 4,
        out_specs=(vmem,) * 2,
        scratch_shapes=[
            pltpu.SMEM((tile_rows, k), jnp.int32),
            pltpu.SMEM((tile_rows, 2, k), jnp.int32),
            pltpu.VMEM((1, sensor), f32),
            pltpu.VMEM((width // piece_cols, tile_rows, k, pix, piece_cols), bf16),
            pltpu.VMEM((width // piece_cols, piece_cols, entries * pix), bf16),
            pltpu.VMEM((3, summing) + piece, bf16),
            pltpu.VMEM((3, 2, n_tile) + piece, bf16),
            pltpu.VMEM((2, summing) + bare, bf16),
            pltpu.VMEM((2,) + bare, bf16),
            pltpu.VMEM((2,) + bare, f32),
            pltpu.VMEM((2,) + bare, f32),
            pltpu.VMEM((8, LANES), f32),
            pltpu.VMEM((2, 8, width), f32),
            pltpu.VMEM((width // piece_cols, entries, PACKED_ROWS, piece_cols), bf16),
            pltpu.VMEM((tile_rows + 1, LANES), f32),
            pltpu.VMEM((n_band - 1, tile_rows + 1, LANES), f32),
            pltpu.VMEM((2, sensor), f32),
            pltpu.VMEM((n_band * n_tile - 1, 2, sensor), f32),
            dma((3,)),
            dma((width // piece_cols,)),
            dma((3, summing)),
            dma((3, 2, n_tile)),
            dma((2, n_tile)),
            dma((2, n_tile)),
            dma((2, summing)),
            dma,
            dma,
            dma,
            dma,
        ],
        compiler_params=pltpu.CompilerParams(
            collective_id=0, has_side_effects=True, vmem_limit_bytes=VMEM_BYTES
        ),
    )(in_hbm(calib), in_hbm(support), in_hbm(turned_window), in_hbm(measured.reshape(1, sensor)))
    solved, residual = pl.pallas_call(
        finish_kernel,
        out_shape=(
            jax.ShapeDtypeStruct((tile_rows, width), f32),
            jax.ShapeDtypeStruct((1, sensor), f32),
        ),
        in_specs=[vmem] * 2,
        out_specs=(vmem, vmem),
        compiler_params=pltpu.CompilerParams(vmem_limit_bytes=VMEM_BYTES),
    )(*[in_vmem(x) for x in held_back])
    return solved, residual.reshape(sensor)


def solution(mesh):
    placed = (P("tile", None, None, "band"), P("tile", None), P("tile", None, None), P("tile"))
    return jax.shard_map(
        body, mesh=mesh, in_specs=placed, out_specs=(P("tile", "band"), P("tile")), check_vma=False
    )
```
